32 devices in a mesh: rep: 4 (over y, core), shard: 8 (over z, x).
Axes of the slice: x: 2, y: 2, z: 4, core: 2. Of those that a mesh axis runs over, the one named last changes fastest.
Arguments:
- tokens: bfloat16 [64, 1024, 512], P(('rep', 'shard')), may hold values from -6 to 6
- encoder: bfloat16 [64, 512, 512], P(('rep', 'shard')), may hold values from -6 to 6
- timesteps: int32 [64], P(('rep', 'shard')), may hold values from 0 to 49
- seg_starts: int32 [64, 13], P(('rep', 'shard')), may hold values from 0 to 992, as said below
- out_grad: bfloat16 [64, 1024, 512], P(('rep', 'shard')), may hold values from -6 to 6
- time_table: bfloat16 [50, 512], P(None, 'shard'), may hold values from -6 to 6
- norm_gain: bfloat16 [3, 512], P(None, 'shard'), may hold values from 0.5 to 1.5
- norm_bias: bfloat16 [3, 512], P(None, 'shard'), may hold values from -3 to 3
- self_qkv: bfloat16 [512, 1536], P('shard'), may hold values from -0.25 to 0.25
- self_out: bfloat16 [512, 512], P('shard'), may hold values from -3 to 3
- cross_query: bfloat16 [512, 512], P('shard'), may hold values from -0.25 to 0.25
- cross_kv: bfloat16 [512, 1024], P('shard'), may hold values from -0.25 to 0.25
- cross_out: bfloat16 [512, 512], P('shard'), may hold values from -3 to 3
- ffn_in: bfloat16 [512, 2048], P('shard'), may hold values from -0.25 to 0.25
- ffn_in_bias: bfloat16 [2048], P('shard'), may hold values from -3 to 3
- ffn_out: bfloat16 [2048, 512], P('shard'), may hold values from -0.125 to 0.125
- ffn_out_bias: bfloat16 [512], P('shard'), may hold values from -3 to 3
Outputs:
- layer_out: bfloat16 [64, 1024, 512], P(('rep', 'shard'))
- tokens_grad: bfloat16 [64, 1024, 512], P(('rep', 'shard'))
- encoder_grad: bfloat16 [64, 512, 512], P(('rep', 'shard'))
- time_table_grad: float32 [50, 512], P(None, 'shard')
- norm_gain_grad: float32 [3, 512], P(None, 'shard')
- norm_bias_grad: float32 [3, 512], P(None, 'shard')
- self_qkv_grad: float32 [512, 1536], P('shard')
- self_out_grad: float32 [512, 512], P('shard')
- cross_query_grad: float32 [512, 512], P('shard')
- cross_kv_grad: float32 [512, 1024], P('shard')
- cross_out_grad: float32 [512, 512], P('shard')
- ffn_in_grad: float32 [512, 2048], P('shard')
- ffn_in_bias_grad: float32 [2048], P('shard')
- ffn_out_grad: float32 [2048, 512], P('shard')
- ffn_out_bias_grad: float32 [512], P('shard')
The draws below stay inside these ranges and needn't reach their ends.
Inputs may be any that keep to these rules, and one draw needn't show every extreme that they name: `seg_starts`: per tree the 13 starts rise: the first is 0, each segment is 1 to 2 times 1024 // 32 tokens long except the trunk, which takes the rest (at least 8 times 1024 // 32); in tree 0 the last leaf is 32 long.
All inputs are finite; a program needn't handle non-finite values.
Results may differ from the reference program's by a relative error of at most 0.02.
Values may be sent and summed in bfloat16 or wider, within the bound.
No kernel may reach another device: no remote copies, remote signals or barrier semaphores. Data moves between devices by JAX's collectives and lax.ppermute only.
A program may use at most 256 MiB of HBM per device.

```python
import jax
import jax.numpy as jnp
from jax import lax

D = 512
HEADS = 8
HEAD = 64
FF = 2048
STEPS = 50
TOK = 1024
ENC = 512
TREES = 64


def draw_seg_starts(key, part):
    unit_len = TOK // 32
    lengths = jax.random.randint(key, (TREES, 12), 1, 3).astype(jnp.int32) * unit_len
    lengths = lengths.at[0, 11].set(unit_len)
    trunk = TOK - jnp.sum(lengths, axis=1, keepdims=True)
    whole = jnp.concatenate([trunk, lengths], axis=1)
    starts = jnp.cumsum(whole, axis=1) - whole
    return starts.astype(jnp.int32)


def with_ends(array, key, smallest, high):
    dims = array.shape
    place = [jax.random.randint(jax.random.fold_in(key, axis), (), 0, dims[axis]) for axis in range(len(dims))]
    array = array.at[tuple(place)].set(smallest)
    longest = dims.index(max(dims))
    place[longest] = (place[longest] + 1) % dims[longest]
    return array.at[tuple(place)].set(high)


def steps_of(rng, extent, cuts, least, top_value):
    factor_of, own = 1.0, jax.random.fold_in(rng, 6)
    for axis_at, blocks in cuts:
        draws = jnp.exp(jax.random.uniform(jax.random.fold_in(own, axis_at), (blocks,), jnp.float32, least / len(cuts), top_value / len(cuts)))
        factor_of = factor_of * jnp.repeat(draws, extent[axis_at] // blocks).reshape([-1 if axis == axis_at else 1 for axis in range(len(extent))])
    return factor_of


def gaussian(stream_key, dims, deviation, reach, shards=(), held_as=jnp.bfloat16):
    gain = steps_of(stream_key, dims, shards, -0.22, 0.18) if shards else 1.0
    array = jax.random.normal(stream_key, dims, jnp.float32) * deviation * gain
    return jnp.minimum(jnp.maximum(array, -reach), reach).astype(held_as)


def setup_inputs(seed: int = 0) -> dict:
    streams_of = jax.random.split(jax.random.key(seed), 18)
    tokens = gaussian(streams_of[0], (TREES, TOK, D), 1.0, 6.0, ((0, 32),))
    encoder = gaussian(streams_of[1], (TREES, ENC, D), 1.0, 6.0, ((0, 32),))
    timesteps = with_ends(jax.random.randint(streams_of[2], (TREES,), 0, STEPS), jax.random.fold_in(streams_of[2], 1), 0, STEPS - 1).astype(jnp.int32)
    seg_starts = draw_seg_starts(jax.random.fold_in(streams_of[17], 71), 0)
    out_grad = gaussian(streams_of[4], (TREES, TOK, D), 1.0, 6.0, ((0, 32),))
    time_table = gaussian(streams_of[5], (STEPS, D), 1.0, 6.0, ((1, 8),))
    norm_gain = jnp.clip(1.0 + 0.1 * jax.random.normal(streams_of[6], (3, D), jnp.float32), 0.5, 1.5).astype(jnp.bfloat16)
    norm_bias = gaussian(streams_of[7], (3, D), 0.3, 3.0, ((1, 8),))
    self_qkv = gaussian(streams_of[8], (D, 3 * D), D ** -0.5, 0.25, ((0, 8),))
    self_out = gaussian(streams_of[9], (D, D), 4 ** -0.5, 3.0, ((0, 8),))
    cross_query = gaussian(streams_of[10], (D, D), D ** -0.5, 0.25, ((0, 8),))
    cross_kv = gaussian(streams_of[11], (D, 2 * D), D ** -0.5, 0.25, ((0, 8),))
    cross_out = gaussian(streams_of[12], (D, D), 4 ** -0.5, 3.0, ((0, 8),))
    ffn_in = gaussian(streams_of[13], (D, FF), D ** -0.5, 0.25, ((0, 8),))
    ffn_in_bias = gaussian(streams_of[14], (FF,), 0.3, 3.0, ((0, 8),))
    ffn_out = gaussian(streams_of[15], (FF, D), FF ** -0.5, 0.125, ((0, 8),))
    ffn_out_bias = gaussian(streams_of[16], (D,), 0.3, 3.0, ((0, 8),))
    return {"tokens": tokens, "encoder": encoder, "timesteps": timesteps, "seg_starts": seg_starts, "out_grad": out_grad, "time_table": time_table, "norm_gain": norm_gain, "norm_bias": norm_bias, "self_qkv": self_qkv, "self_out": self_out, "cross_query": cross_query, "cross_kv": cross_kv, "cross_out": cross_out, "ffn_in": ffn_in, "ffn_in_bias": ffn_in_bias, "ffn_out": ffn_out, "ffn_out_bias": ffn_out_bias}


@jax.custom_vjp
def low(v):
    return lax.optimization_barrier(v.astype(jnp.bfloat16)).astype(jnp.float32)

@jax.custom_vjp
def low_back(v):
    return v

def low_keep(v):
    return (low(v), None)

def low_pass(kept, grad):
    return (grad,)

def back_keep(v):
    return (v, None)

def back_low(kept, grad):
    return (low(grad),)
low.defvjp(low_keep, low_pass)
low_back.defvjp(back_keep, back_low)

def ancestry():
    row_ids = lax.broadcasted_iota(jnp.int32, (13, 13), 0)
    col_ids = lax.broadcasted_iota(jnp.int32, (13, 13), 1)
    parent = jnp.where(row_ids >= 5, 1 + (row_ids - 5) // 2, 0)
    visible = (col_ids == row_ids) | (col_ids == 0) | (row_ids >= 5) & (col_ids == parent)
    return visible.astype(jnp.float32)

def segment_table(starts, row_count):
    position = lax.broadcasted_iota(jnp.int32, (row_count, 13), 0)
    seg_end = jnp.concatenate([starts[1:], jnp.full((1,), row_count, jnp.int32)])
    inside = (position >= starts[None, :]) & (position < seg_end[None, :])
    return inside.astype(jnp.float32)

def dot_high(left, right):
    return jnp.dot(left, right, precision=lax.Precision.HIGHEST)

def layer_norm(hidden_rows, gain_row, bias_row):
    row_mean = lax.optimization_barrier(jnp.mean(hidden_rows, -1, keepdims=True))
    centred = hidden_rows - row_mean
    inv_std = lax.rsqrt(lax.optimization_barrier(jnp.mean(centred * centred, -1, keepdims=True)) + 1e-05)
    return centred * inv_std * gain_row + bias_row

def attention(queries, key_rows, value_rows, row_table, key_table):
    row_count = queries.shape[0]
    block_rows = min(512, row_count)
    block_count = row_count // block_rows
    key_heads = key_rows.reshape(key_rows.shape[0], HEADS, HEAD)
    value_heads = value_rows.reshape(value_rows.shape[0], HEADS, HEAD)
    query_blocks = queries.reshape(block_count, block_rows, HEADS, HEAD)
    if row_table is None:
        table_blocks = jnp.zeros((block_count, block_rows, 13), jnp.float32)
    else:
        table_blocks = row_table.reshape(block_count, block_rows, 13)

    def one_block(item):
        query_block, rows_here = item
        scores = jnp.einsum('qhd,khd->hqk', query_block, key_heads, precision=lax.Precision.HIGHEST)
        scores = low_back(scores * 0.125)
        if row_table is not None:
            allowed = dot_high(dot_high(rows_here, ancestry()), key_table.T) > 0.5
            scores = jnp.where(allowed[None], scores, jnp.float32(-1e+30))
        row_peak = lax.optimization_barrier(jnp.max(scores, -1, keepdims=True))
        exponent = jnp.exp(scores - row_peak)
        probs = low(exponent / lax.optimization_barrier(jnp.sum(exponent, -1, keepdims=True)))
        attended = jnp.einsum('hqk,khd->qhd', probs, value_heads, precision=lax.Precision.HIGHEST)
        return attended.reshape(block_rows, HEADS * HEAD)
    result = lax.map(jax.checkpoint(one_block), (query_blocks, table_blocks))
    return result.reshape(row_count, HEADS * HEAD)

def forward(tokens_row, encoder_row, step_index, row_table, weights):
    step_table, gain_rows, bias_rows, self_qkv, self_out, cross_query, cross_kv, cross_out, ffn_in, ffn_in_bias, ffn_out, ffn_out_bias = weights
    model_width = self_out.shape[0]
    start_state = tokens_row + lax.dynamic_index_in_dim(step_table, step_index, 0, keepdims=False)
    first_low = low(layer_norm(start_state, gain_rows[0], bias_rows[0]))
    qkv_rows = low(low_back(dot_high(first_low, self_qkv)))
    self_mixed = low(low_back(attention(qkv_rows[:, :model_width], qkv_rows[:, model_width:2 * model_width], qkv_rows[:, 2 * model_width:], row_table, row_table)))
    after_self = start_state + low_back(dot_high(self_mixed, self_out))
    second_low = low(layer_norm(after_self, gain_rows[1], bias_rows[1]))
    cross_rows = low(low_back(dot_high(second_low, cross_query)))
    cross_pairs = low(low_back(dot_high(encoder_row, cross_kv)))
    cross_mixed = low(low_back(attention(cross_rows, cross_pairs[:, :model_width], cross_pairs[:, model_width:], None, None)))
    after_cross = after_self + low_back(dot_high(cross_mixed, cross_out))
    third_low = low(layer_norm(after_cross, gain_rows[2], bias_rows[2]))
    hidden_pre = low_back(dot_high(third_low, ffn_in) + ffn_in_bias)
    hidden_low = low(jax.nn.gelu(hidden_pre))
    return after_cross + low_back(dot_high(hidden_low, ffn_out) + ffn_out_bias)

def reference(tokens, encoder, timesteps, seg_starts, out_grad, time_table, norm_gain, norm_bias, self_qkv, self_out, cross_query, cross_kv, cross_out, ffn_in, ffn_in_bias, ffn_out, ffn_out_bias):
    weights = tuple((w.astype(jnp.float32) for w in (time_table, norm_gain, norm_bias, self_qkv, self_out, cross_query, cross_kv, cross_out, ffn_in, ffn_in_bias, ffn_out, ffn_out_bias)))
    zeros = tuple((jnp.zeros_like(w) for w in weights))

    def one_tree(totals, item):
        tokens_row, encoder_row, step_index, starts, cotangent = item
        row_table = segment_table(starts, tokens_row.shape[0])

        def run_layer(tokens_in, encoder_in, weight_set):
            return forward(tokens_in, encoder_in, step_index, row_table, weight_set)
        result, pull = jax.vjp(run_layer, tokens_row.astype(jnp.float32), encoder_row.astype(jnp.float32), weights)
        tokens_back, encoder_back, weight_back = pull(cotangent.astype(jnp.float32))
        totals = tuple((earlier + later for earlier, later in zip(totals, weight_back)))
        return (totals, (result.astype(jnp.bfloat16), tokens_back.astype(jnp.bfloat16), encoder_back.astype(jnp.bfloat16)))
    totals, (layer_out, tokens_grad, encoder_grad) = lax.scan(one_tree, zeros, (tokens, encoder, timesteps, seg_starts, out_grad))
    return (layer_out, tokens_grad, encoder_grad, totals[0], totals[1], totals[2], totals[3], totals[4], totals[5], totals[6], totals[7], totals[8], totals[9], totals[10], totals[11])
```

```python
import functools

import jax
import jax.numpy as jnp
from jax import lax
from jax.experimental import pallas as pl
from jax.experimental.pallas import tpu as pltpu
from jax.sharding import PartitionSpec as P

BF = jnp.bfloat16
F32 = jnp.float32


def nt(a, b):
    return lax.dot_general(a, b, (((1,), (1,)), ((), ())), preferred_element_type=F32)


def nn(a, b):
    return jnp.dot(a, b, preferred_element_type=F32)


def cost(flops, moved, exps=0):
    return pl.CostEstimate(flops=int(flops), bytes_accessed=int(moved), transcendentals=int(exps))


def kernel_params(axes):
    return pltpu.CompilerParams(vmem_limit_bytes=58 << 20, dimension_semantics=("arbitrary",) * axes)


def split3(x):
    hi = x.astype(BF)
    rest = x - hi.astype(F32)
    mid = rest.astype(BF)
    return hi, mid, (rest - mid.astype(F32)).astype(BF)


def place3(sub, parts, base):
    hi, mid, lo = parts
    return jnp.where(sub == 13, hi, jnp.where(sub == 14, mid, jnp.where(sub == 15, lo, base)))


def attend_forward_kernel(masked, tile, *refs):
    if masked:
        q_ref, k_ref, v_ref, qm_ref, ko_ref, o_ref, ext_ref = refs
    else:
        q_ref, k_ref, v_ref, o_ref, ext_ref = refs
    lane = lax.broadcasted_iota(jnp.int32, (1, 128), 1)
    first, sub = lane < 64, lane & 63
    zero, one = jnp.zeros((1, 128), BF), jnp.ones((1, 128), BF)
    k, v = k_ref[...], v_ref[...]
    other = ko_ref[...] if masked else zero
    keys = (jnp.where(first, k, other), jnp.where(first, other, k))
    vals = (jnp.where(first, v, one), jnp.where(first, one, v))
    for i in range(q_ref.shape[0] // tile):
        rows = pl.ds(i * tile, tile)
        q = q_ref[rows, :] * jnp.asarray(0.125, BF)
        qm = qm_ref[rows, :] if masked else zero
        outs, peaks = [], []
        for h in range(2):
            s = nt(jnp.where(first, q, qm) if h == 0 else jnp.where(first, qm, q), keys[h])
            peak = jnp.max(s, axis=1, keepdims=True)
            outs.append(nn(jnp.exp(s - peak).astype(BF), vals[h]))
            peaks.append(peak)
        sums = jnp.where(first, outs[1], outs[0])
        o_ref[rows, :] = (jnp.where(first, outs[0], outs[1]) / pltpu.roll(sums, 64, 1)).astype(BF)
        logsum = jnp.where(first, peaks[1], peaks[0]) + jnp.log(sums)
        ext_ref[rows, :] = place3(sub, split3(-logsum), qm)


def attend_forward(q, k, v, cols, pairs, trees, qm=None, ko=None, tile=512):
    qlen, klen = q.shape[0] // trees, k.shape[0] // trees
    tile = min(tile, qlen)
    at = lambda n, c: pl.BlockSpec((n, 128), lambda t, h: (t, c + h))
    specs = [at(qlen, cols[0]), at(klen, cols[1]), at(klen, cols[2])]
    args = [q, k, v]
    if qm is not None:
        specs += [pl.BlockSpec((qlen, 128), lambda t, h: (t, 0)), pl.BlockSpec((klen, 128), lambda t, h: (t, 0))]
        args += [qm, ko]
    shape = jax.ShapeDtypeStruct((trees * qlen, pairs * 128), BF)
    return pl.pallas_call(
        functools.partial(attend_forward_kernel, qm is not None, tile),
        grid=(trees, pairs), in_specs=specs, out_specs=[at(qlen, 0)] * 2, out_shape=[shape] * 2,
        compiler_params=kernel_params(2), name="attend_forward",
        cost_estimate=cost(trees * pairs * qlen * klen * 2000, trees * pairs * qlen * 1600, trees * pairs * 2 * qlen * klen),
    )(*args)


def attend_backward_kernel(masked, tq, tk, *refs):
    if masked:
        q_ref, k_ref, v_ref, do_ref, o_ref, ext_ref, ko_ref = refs[:7]
    else:
        q_ref, k_ref, v_ref, do_ref, o_ref, ext_ref = refs[:6]
    dq_ref, dk_ref, dv_ref, qa, qz, da, dz, kt, dqt = refs[-9:]
    lane = lax.broadcasted_iota(jnp.int32, (1, 128), 1)
    first, sub = lane < 64, lane & 63
    zero = jnp.zeros((1, 128), BF)
    ones = jnp.where((sub >= 13) & (sub < 16), jnp.ones((1, 128), BF), zero)
    q = q_ref[...] * jnp.asarray(0.125, BF)
    ext, do = ext_ref[...], do_ref[...]
    prod = do.astype(F32) * o_ref[...].astype(F32)
    for h in range(2):
        mine = first if h == 0 else ~first
        delta = jnp.sum(jnp.where(mine, prod, 0.0), axis=1, keepdims=True)
        parts = place3(sub, split3(jnp.broadcast_to(-delta, prod.shape)), zero)
        qa[h] = jnp.where(mine, q, ext)
        qz[h] = jnp.where(mine, q, zero)
        da[h] = jnp.where(mine, do, parts)
        dz[h] = jnp.where(mine, do, zero)
    kt[...] = k_ref[...].T
    dqt[...] = jnp.zeros_like(dqt)
    nq, nk = q_ref.shape[0] // tq, k_ref.shape[0] // tk

    @pl.loop(0, nk)
    def _(j):
        kr = pl.ds(pl.multiple_of(j * tk, tk), tk)
        k, v = k_ref[kr, :], v_ref[kr, :]
        other = ko_ref[kr, :] if masked else ones
        dk = jnp.zeros((tk, 128), F32)
        dv = jnp.zeros((tk, 128), F32)
        for i in range(nq):
            qr = pl.ds(i * tq, tq)
            for h in range(2):
                mine = first if h == 0 else ~first
                probs = jnp.exp(nt(jnp.where(mine, k, other), qa[h, qr, :]))
                centred = nt(jnp.where(mine, v, ones), da[h, qr, :])
                ds = (probs * centred).astype(BF)
                dv = dv + nn(probs.astype(BF), dz[h, qr, :])
                dk = dk + nn(ds, qz[h, qr, :])
                dqt[pl.ds(64 * h, 64), qr] += nn(kt[pl.ds(64 * h, 64), kr], ds)
        dk_ref[kr, :] = dk.astype(BF)
        dv_ref[kr, :] = dv.astype(BF)

    dq_ref[...] = (dqt[...].T * 0.125).astype(BF)


def attend_backward(q, k, v, do, o, ext, cols, pairs, trees, ko=None, tq=512, tk=512):
    qlen, klen = q.shape[0] // trees, k.shape[0] // trees
    tq, tk = min(tq, qlen), min(tk, klen)
    at = lambda n, c: pl.BlockSpec((n, 128), lambda t, h: (t, c + h))
    specs = [at(qlen, cols[0]), at(klen, cols[1]), at(klen, cols[2])] + [at(qlen, cols[3])] * 3
    args = [q, k, v, do, o, ext]
    if ko is not None:
        specs += [pl.BlockSpec((klen, 128), lambda t, h: (t, 0))]
        args += [ko]
    return pl.pallas_call(
        functools.partial(attend_backward_kernel, ko is not None, tq, tk),
        grid=(trees, pairs), in_specs=specs, out_specs=[at(qlen, 0), at(klen, 0), at(klen, 0)],
        out_shape=[jax.ShapeDtypeStruct((trees * n, pairs * 128), BF) for n in (qlen, klen, klen)],
        scratch_shapes=[pltpu.VMEM((2, qlen, 128), BF)] * 4 + [pltpu.VMEM((128, klen), BF), pltpu.VMEM((128, qlen), F32)],
        compiler_params=kernel_params(2), name="attend_backward",
        cost_estimate=cost(trees * pairs * qlen * klen * 4000, trees * pairs * qlen * 2500, trees * pairs * 2 * qlen * klen),
    )(*args)


def mask_rows(starts, count):
    trees = starts.shape[0]
    position = lax.broadcasted_iota(jnp.int32, (trees, count, 1), 1)
    seg = jnp.sum((position >= starts[:, None, :]).astype(jnp.int32), -1, keepdims=True) - 1
    sub = lax.broadcasted_iota(jnp.int32, (1, 1, 128), 2) & 63
    parent = jnp.where(seg >= 5, 1 + (seg - 5) // 2, 0)
    seen = (sub == seg) | (sub == 0) | (sub == parent) | (sub >= 13)
    barred = jnp.where(seen, 0.0, -1e30).astype(BF)
    own = ((sub == seg) | ((sub >= 13) & (sub < 16))).astype(BF)
    return barred.reshape(trees * count, 128), own.reshape(trees * count, 128)


TR = 512


def norm_rows(h, gain, bias):
    centred = h - jnp.mean(h, -1, keepdims=True)
    inv = lax.rsqrt(jnp.mean(centred * centred, -1, keepdims=True) + 1e-05)
    normed = centred * inv
    return normed * gain + bias, normed, inv


def norm_pull(dy, normed, inv, gain):
    scaled = dy * gain
    along = jnp.mean(scaled * normed, -1, keepdims=True)
    dx = inv * (scaled - jnp.mean(scaled, -1, keepdims=True) - normed * along)
    return dx, jnp.sum(dy * normed, 0, keepdims=True), jnp.sum(dy, 0, keepdims=True)


def row_spec(width, rows=TR):
    return pl.BlockSpec((rows, width), lambda i, at: (i, 0))


def full_spec(shape):
    return pl.BlockSpec(shape, lambda i, at: (0,) * len(shape))


def part_spec(packed, part, rows):
    return pl.BlockSpec((4, packed.shape[1], rows, 128), lambda i, at: (0, 0, part, 0))


def flip_bits(value, count):
    return sum(((value >> b) & 1) << (count - 1 - b) for b in range(count))


def place_weight(at, relative, ref, dst):
    shards, rows = ref.shape[1], ref.shape[2]
    bits = shards.bit_length() - 1
    for q in range(4):
        for j in range(shards):
            if relative:
                piece = ref[((q & 1) ^ at[0]) * 2 + ((q >> 1) ^ at[1]), flip_bits(j, bits) ^ at[2]]
            else:
                piece = ref[q, j]
            dst[j * rows:(j + 1) * rows, q * 128:(q + 1) * 128] = piece


def pack_grad(at, acc, keep, send, offset):
    shards = keep.shape[1]
    rows = acc.shape[0] // shards
    for q in range(4):
        piece = acc[:, q * 128:(q + 1) * 128].astype(BF).reshape(shards, rows, 128)
        for core in range(2):
            @pl.when(at[0] == core)
            def _(q=q, core=core, piece=piece):
                (keep if (q & 1) == core else send)[(q >> 1) ^ at[1], :, offset:offset + rows, :] = piece


def start_rows(tok_ref, small_ref, per_tree):
    tree = pl.program_id(0) // per_tree
    return tok_ref[...].astype(F32) + small_ref[pl.ds(11 + tree, 1), :]


def clear(*refs):
    for ref in refs:
        ref[...] = jnp.zeros_like(ref)


def gelu_both(x):
    k = 0.7978845608028654
    x2 = x * x
    t = jnp.tanh(k * x * (1.0 + 0.044715 * x2))
    half = 0.5 * (1.0 + t)
    return x * half, half + 0.5 * x * (1.0 - t * t) * (k + (3 * 0.044715 * k) * x2)


def row_call(kernel, name, at, args, specs, outs, out_specs, scratch, steps, flops):
    moved = sum(a.size * a.dtype.itemsize for a in (*args, *outs))
    return pl.pallas_call(
        kernel,
        grid_spec=pltpu.PrefetchScalarGridSpec(
            num_scalar_prefetch=1, grid=(steps,), in_specs=specs, out_specs=out_specs, scratch_shapes=scratch),
        out_shape=outs, compiler_params=kernel_params(1), name=name, cost_estimate=cost(flops, moved),
    )(at, *args)


def sds(shape, dtype):
    return jax.ShapeDtypeStruct(shape, dtype)


def first_kernel(per_tree, at, tok_ref, small_ref, wq, wk, wv, qkv_ref, w):
    @pl.when(pl.program_id(0) == 0)
    def _():
        for c, ref in enumerate((wq, wk, wv)):
            place_weight(at, True, ref, w.at[c])

    x, _, _ = norm_rows(start_rows(tok_ref, small_ref, per_tree), small_ref[0:1, :], small_ref[3:4, :])
    x = x.astype(BF)
    for c in range(3):
        qkv_ref[:, c * 512:(c + 1) * 512] = nn(x, w[c]).astype(BF)


def first_call(at, tokens, small, packed, per_tree):
    rows, r = tokens.shape[0], 512 // packed.shape[1]
    return row_call(
        functools.partial(first_kernel, per_tree), "project_qkv", at,
        (tokens, small, packed, packed, packed),
        [row_spec(512), full_spec(small.shape)] + [part_spec(packed, c, r) for c in range(3)],
        (sds((rows, 1536), BF),), [row_spec(1536)], [pltpu.VMEM((3, 512, 512), BF)], rows // TR, rows * 512 * 1536 * 2)[0]


def second_kernel(per_tree, at, tok_ref, small_ref, mixed_ref, enc_ref, wo, wq, wk, wv, after_ref, cq_ref, ckv_ref, w):
    @pl.when(pl.program_id(0) == 0)
    def _():
        for c, ref in enumerate((wo, wq, wk, wv)):
            place_weight(at, True, ref, w.at[c])

    h = start_rows(tok_ref, small_ref, per_tree) + nn(mixed_ref[...], w[0])
    after_ref[...] = h
    x, _, _ = norm_rows(h, small_ref[1:2, :], small_ref[4:5, :])
    cq_ref[...] = nn(x.astype(BF), w[1]).astype(BF)
    e = enc_ref[...]
    ckv_ref[:, :512] = nn(e, w[2]).astype(BF)
    ckv_ref[:, 512:] = nn(e, w[3]).astype(BF)


def second_call(at, tokens, small, mixed, enc, packed, per_tree):
    rows, r = tokens.shape[0], 512 // packed.shape[1]
    steps = rows // TR
    er = enc.shape[0] // steps
    return row_call(
        functools.partial(second_kernel, per_tree), "cross_inputs", at,
        (tokens, small, mixed, enc, packed, packed, packed, packed),
        [row_spec(512), full_spec(small.shape), row_spec(512), row_spec(512, er)] + [part_spec(packed, c, r) for c in range(4)],
        (sds((rows, 512), F32), sds((rows, 512), BF), sds((enc.shape[0], 1024), BF)),
        [row_spec(512), row_spec(512), row_spec(1024, er)], [pltpu.VMEM((4, 512, 512), BF)], steps, rows * 512 * 1536 * 2)


def ffn_kernel(at, after_ref, mixed_ref, g_ref, small_ref, wi0, wi1, wi2, wi3, wf, wc,
               out_ref, resid_ref, cmg_ref, keep, send, gs_ref, w, wo, aco, afi, afo):
    step = pl.program_id(0)
    r = wc.shape[2]

    @pl.when(step == 0)
    def _():
        clear(aco, afi, afo, gs_ref)
        for c, ref in enumerate((wi0, wi1, wi2, wi3, wc)):
            place_weight(at, False, ref, w.at[c])
        place_weight(at, False, wf, wo)

    mixed, g = mixed_ref[...], g_ref[...]
    h = after_ref[...] + nn(mixed, w[4])
    y, normed, inv = norm_rows(h, small_ref[2:3, :], small_ref[5:6, :])
    third = y.astype(BF)
    third_t, g_t = third.T, g.T
    out = h + small_ref[10:11, :]
    back = jnp.zeros(h.shape, F32)
    for c in range(4):
        wi, wf_c = w[c], wo[c * 512:(c + 1) * 512, :]
        value, slope = gelu_both(nn(third, wi) + small_ref[6 + c:7 + c, :])
        hidden = value.astype(BF)
        out = out + nn(hidden, wf_c)
        pre_grad = (nt(g, wf_c) * slope).astype(BF)
        gs_ref[2 + c:3 + c, :] += jnp.sum(pre_grad.astype(F32), 0, keepdims=True)
        back = back + nt(pre_grad, wi)
        afi[c] += nn(third_t, pre_grad)
        afo[c] += nn(g_t, hidden)
    out_ref[...] = out.astype(BF)
    g_high = g.astype(F32)
    gs_ref[6:7, :] += jnp.sum(g_high, 0, keepdims=True)
    dx, dg, db = norm_pull(back, normed, inv, small_ref[2:3, :])
    gs_ref[0:1, :] += dg
    gs_ref[1:2, :] += db
    resid = g_high + dx
    resid_ref[...] = resid
    low = resid.astype(BF)
    cmg_ref[...] = nt(low, w[4]).astype(BF)
    aco[...] += nn(mixed.T, low)

    @pl.when(step == pl.num_programs(0) - 1)
    def _():
        for c in range(4):
            pack_grad(at, afi[c], keep, send, c * r)
        for c in range(4):
            whole = afo[c].T
            shards = keep.shape[1]
            quarter = shards // 4
            for q in range(4):
                piece = whole[:, q * 128:(q + 1) * 128].astype(BF).reshape(quarter, 4 * r, 128)
                for core in range(2):
                    @pl.when(at[0] == core)
                    def _(q=q, core=core, piece=piece, c=c):
                        (keep if (q & 1) == core else send)[(q >> 1) ^ at[1], c * quarter:(c + 1) * quarter, 4 * r:8 * r, :] = piece
        pack_grad(at, aco[...], keep, send, 8 * r)


def ffn_call(at, after, mixed, g, small, packed):
    rows, shards = after.shape[0], packed.shape[1]
    r = 512 // shards
    half = sds((2, shards, 9 * r, 128), BF)
    return row_call(
        ffn_kernel, "ffn_both_ways", at,
        (after, mixed, g, small) + (packed,) * 6,
        [row_spec(512)] * 3 + [full_spec(small.shape)] + [part_spec(packed, c, r) for c in range(4)]
        + [part_spec(packed, 1, 4 * r), part_spec(packed, 8, r)],
        (sds((rows, 512), BF), sds((rows, 512), F32), sds((rows, 512), BF), half, half, sds((8, 512), F32)),
        [row_spec(512)] * 3 + [full_spec(half.shape)] * 2 + [full_spec((8, 512))],
        [pltpu.VMEM((5, 512, 512), BF), pltpu.VMEM((2048, 512), BF), pltpu.VMEM((512, 512), F32),
         pltpu.VMEM((4, 512, 512), F32), pltpu.VMEM((4, 512, 512), F32)],
        rows // TR, rows * 512 * 2048 * 12)


def middle_kernel(at, cqg_ref, after_ref, resid_ref, mixed_ref, enc_ref, ckg_ref, cvg_ref, small_ref, wo, wq, wk, wv,
                  resid2_ref, smg_ref, encg_ref, keep, send, gs_ref, w, acc):
    step = pl.program_id(0)
    r = wo.shape[2]

    @pl.when(step == 0)
    def _():
        clear(acc, gs_ref)
        for c, ref in enumerate((wo, wq, wk, wv)):
            place_weight(at, True, ref, w.at[c])

    y, normed, inv = norm_rows(after_ref[...], small_ref[1:2, :], small_ref[4:5, :])
    cqg = cqg_ref[...]
    acc[1] += nn(y.astype(BF).T, cqg)
    dx, dg, db = norm_pull(nt(cqg, w[1]), normed, inv, small_ref[1:2, :])
    gs_ref[0:1, :] += dg
    gs_ref[1:2, :] += db
    resid = resid_ref[...] + dx
    resid2_ref[...] = resid
    low = resid.astype(BF)
    acc[0] += nn(mixed_ref[...].T, low)
    smg_ref[...] = nt(low, w[0]).astype(BF)
    enc_t, ckg, cvg = enc_ref[...].T, ckg_ref[...], cvg_ref[...]
    acc[2] += nn(enc_t, ckg)
    acc[3] += nn(enc_t, cvg)
    encg_ref[...] = (nt(ckg, w[2]) + nt(cvg, w[3])).astype(BF)

    @pl.when(step == pl.num_programs(0) - 1)
    def _():
        for c in range(4):
            pack_grad(at, acc[c], keep, send, c * r)


def middle_call(at, cqg, after, resid, mixed, enc, ckg, cvg, small, packed):
    rows, shards = after.shape[0], packed.shape[1]
    r, steps = 512 // shards, rows // TR
    er = enc.shape[0] // steps
    half = sds((2, shards, 4 * r, 128), BF)
    return row_call(
        middle_kernel, "between_attentions", at,
        (cqg, after, resid, mixed, enc, ckg, cvg, small) + (packed,) * 4,
        [row_spec(512)] * 4 + [row_spec(512, er)] * 3 + [full_spec(small.shape)] + [part_spec(packed, c, r) for c in range(4)],
        (sds((rows, 512), F32), sds((rows, 512), BF), sds(enc.shape, BF), half, half, sds((8, 512), F32)),
        [row_spec(512), row_spec(512), row_spec(512, er)] + [full_spec(half.shape)] * 2 + [full_spec((8, 512))],
        [pltpu.VMEM((4, 512, 512), BF), pltpu.VMEM((4, 512, 512), F32)], steps, rows * 512 * 512 * 12)


def last_kernel(per_tree, at, tok_ref, qg_ref, kg_ref, vg_ref, resid_ref, small_ref, wq, wk, wv,
                tokg_ref, keep, send, gs_ref, w, acc):
    step = pl.program_id(0)
    r = wq.shape[2]

    @pl.when(step == 0)
    def _():
        clear(acc, gs_ref)
        for c, ref in enumerate((wq, wk, wv)):
            place_weight(at, True, ref, w.at[c])

    y, normed, inv = norm_rows(start_rows(tok_ref, small_ref, per_tree), small_ref[0:1, :], small_ref[3:4, :])
    x_t = y.astype(BF).T
    back = jnp.zeros(y.shape, F32)
    for c, ref in enumerate((qg_ref, kg_ref, vg_ref)):
        grad = ref[...]
        acc[c] += nn(x_t, grad)
        back = back + nt(grad, w[c])
    dx, dg, db = norm_pull(back, normed, inv, small_ref[0:1, :])
    gs_ref[0:1, :] += dg
    gs_ref[1:2, :] += db
    resid = resid_ref[...] + dx
    tokg_ref[...] = resid.astype(BF)
    gs_ref[pl.ds(2 + step // per_tree, 1), :] += jnp.sum(resid, 0, keepdims=True)

    @pl.when(step == pl.num_programs(0) - 1)
    def _():
        for c in range(3):
            pack_grad(at, acc[c], keep, send, c * r)


def last_call(at, tokens, qg, kg, vg, resid, small, packed, per_tree):
    rows, shards = tokens.shape[0], packed.shape[1]
    r = 512 // shards
    half = sds((2, shards, 3 * r, 128), BF)
    return row_call(
        functools.partial(last_kernel, per_tree), "first_norm_back", at,
        (tokens, qg, kg, vg, resid, small) + (packed,) * 3,
        [row_spec(512)] * 5 + [full_spec(small.shape)] + [part_spec(packed, c, r) for c in range(3)],
        (sds((rows, 512), BF), half, half, sds((8, 512), F32)),
        [row_spec(512)] + [full_spec(half.shape)] * 2 + [full_spec((8, 512))],
        [pltpu.VMEM((3, 512, 512), BF), pltpu.VMEM((3, 512, 512), F32)], rows // TR, rows * 512 * 1536 * 4)


def xor_pairs(count, bit):
    return [(i, i ^ bit) for i in range(count)]


def quarter_of(weight, quarter):
    rows, width = weight.shape
    parts = weight.reshape(rows, width // 512, 4, 128)
    mine = lax.dynamic_index_in_dim(parts, quarter, 2, keepdims=False)
    return jnp.transpose(mine, (1, 0, 2)).reshape(-1, 128)


def gather_steps(piece, shards):
    held = piece[None]
    bit = shards // 2
    while bit:
        held = jnp.concatenate([held, lax.ppermute(held, "shard", xor_pairs(shards, bit))])
        bit //= 2
    for bit in (2, 1):
        held = jnp.concatenate([held, lax.ppermute(held, "rep", xor_pairs(4, bit))])
    return held.reshape(4, shards, *piece.shape)


def reduce_steps(keep, send):
    got = lax.ppermute(send, "rep", xor_pairs(4, 1))
    mine = (keep[0].astype(F32) + got[0].astype(F32)).astype(BF)
    other = (keep[1].astype(F32) + got[1].astype(F32)).astype(BF)
    got = lax.ppermute(other, "rep", xor_pairs(4, 2))
    mine = (mine.astype(F32) + got.astype(F32)).astype(BF)
    got = lax.all_to_all(mine, "shard", split_axis=0, concat_axis=0, tiled=True)
    return jnp.sum(got.astype(F32), 0).astype(BF)


def finish_kernel(parts, at, p0, p1, p2, p3, *outs):
    for k, ref in enumerate((p0, p1, p2, p3)):
        lanes = pl.multiple_of((k ^ (at[1] * 2 + at[0])) * 128, 128)
        row = 0
        for out, (rows, blocks) in zip(outs, parts):
            for c in range(blocks):
                out[:, pl.ds(c * 512 + lanes, 128)] = ref[row:row + rows, :].astype(F32)
                row += rows


def finish(at, piece, parts):
    pieces = [piece] + [lax.ppermute(piece, "rep", xor_pairs(4, k)) for k in (1, 2, 3)]
    spec = lambda shape: pl.BlockSpec(shape, lambda i, at: (0,) * len(shape))
    shapes = [(rows, blocks * 512) for rows, blocks in parts]
    return pl.pallas_call(
        functools.partial(finish_kernel, parts),
        grid_spec=pltpu.PrefetchScalarGridSpec(
            num_scalar_prefetch=1, grid=(1,), in_specs=[spec(piece.shape)] * 4, out_specs=[spec(s) for s in shapes]),
        out_shape=[sds(s, F32) for s in shapes], compiler_params=kernel_params(1), name="finish_grads",
        cost_estimate=cost(piece.size * 4, piece.size * 24),
    )(at, *pieces)


def gather_small(shards, table, gain, bias, in_bias, out_bias):
    width = gain.shape[1]
    steps = table.shape[0]
    rows = jnp.concatenate([gain, bias, in_bias.reshape(4, width), out_bias[None], table])
    pad = -rows.shape[0] % 16
    rows = jnp.pad(rows, ((0, pad), (0, 0)))
    got = lax.all_to_all(jnp.broadcast_to(rows[None], (shards, *rows.shape)), "shard", split_axis=0, concat_axis=0, tiled=True)
    wide = jnp.transpose(got, (1, 0, 2)).reshape(-1, shards * width).astype(F32)
    inner = got[:, 6:10].astype(F32).reshape(4, 512)
    return wide[11:11 + steps], jnp.concatenate([wide[:6], inner, wide[10:11]])


def per_device(shards, tokens, encoder, timesteps, seg_starts, out_grad, time_table, norm_gain, norm_bias, self_qkv,
               self_out, cross_query, cross_kv, cross_out, ffn_in, ffn_in_bias, ffn_out, ffn_out_bias):
    trees, count, width = tokens.shape
    per_tree = count // TR
    rep, mine = lax.axis_index("rep"), lax.axis_index("shard")
    at = jnp.stack([rep & 1, rep >> 1, flip_bits(mine, shards.bit_length() - 1)]).astype(jnp.int32)
    quarter = lambda *weights: jnp.concatenate([quarter_of(w, rep) for w in weights])
    table, small = gather_small(shards, time_table, norm_gain, norm_bias, ffn_in_bias, ffn_out_bias)
    packed1 = gather_steps(quarter(self_qkv), shards)
    packed2 = gather_steps(quarter(self_out, cross_query, cross_kv), shards)
    packed3 = lax.all_gather(quarter(ffn_in, ffn_out, cross_out), ("rep", "shard"), axis=0)
    packed3 = packed3.reshape(4, shards, *packed3.shape[1:])
    steps_hot = (lax.broadcasted_iota(jnp.int32, (trees, table.shape[0]), 1) == timesteps[:, None]).astype(F32)
    rows_of = jnp.concatenate([lax.dynamic_slice_in_dim(table, timesteps[t], 1, 0) for t in range(trees)])
    small = jnp.concatenate([small, rows_of])
    small = jnp.pad(small, ((0, -small.shape[0] % 8), (0, 0)))
    tok, enc, g = tokens.reshape(-1, width), encoder.reshape(-1, width), out_grad.reshape(-1, width)
    barred, own = mask_rows(seg_starts, count)

    qkv = first_call(at, tok, small, packed1, per_tree)
    self_mixed, self_ext = attend_forward(qkv, qkv, qkv, (0, 4, 8), 4, trees, barred, own)
    after_self, cq, ckv = second_call(at, tok, small, self_mixed, enc, packed2, per_tree)
    cross_mixed, cross_ext = attend_forward(cq, ckv, ckv, (0, 0, 4), 4, trees)
    out, resid, cross_back, keep3, send3, small3 = ffn_call(at, after_self, cross_mixed, g, small, packed3)
    piece3 = reduce_steps(keep3, send3)
    cqg, ckg, cvg = attend_backward(cq, ckv, ckv, cross_back, cross_mixed, cross_ext, (0, 0, 4, 0), 4, trees)
    resid, self_back, enc_grad, keep2, send2, small2 = middle_call(
        at, cqg, after_self, resid, self_mixed, enc, ckg, cvg, small, packed2)
    piece2 = reduce_steps(keep2, send2)
    qg, kg, vg = attend_backward(qkv, qkv, qkv, self_back, self_mixed, self_ext, (0, 4, 8, 0), 4, trees, own)
    tok_grad, keep1, send1, small1 = last_call(at, tok, qg, kg, vg, resid, small, packed1, per_tree)
    piece1 = reduce_steps(keep1, send1)

    r = width // shards
    ffn_in_grad, ffn_out_grad, cross_out_grad = finish(at, piece3, ((r, 4), (4 * r, 1), (r, 1)))
    self_out_grad, cross_query_grad, cross_kv_grad = finish(at, piece2, ((r, 1), (r, 1), (r, 2)))
    (self_qkv_grad,) = finish(at, piece1, ((r, 3),))

    table_grad = jnp.einsum("ts,tw->sw", steps_hot, small1[2:2 + trees], precision=lax.Precision.HIGHEST)
    sums = jnp.concatenate([
        small1[0:1], small2[0:1], small3[0:1], small1[1:2], small2[1:2], small3[1:2], small3[6:7], table_grad])
    by_shard = jnp.transpose(sums.reshape(-1, shards, r), (1, 0, 2))
    by_shard = jnp.concatenate([by_shard, small3[2:6].reshape(shards, 4, r)], 1)
    got = lax.all_to_all(by_shard.astype(BF), "shard", split_axis=0, concat_axis=0, tiled=True)
    total = lax.psum(jnp.sum(got.astype(F32), 0), "rep")
    steps = table.shape[0]
    return (
        out.reshape(tokens.shape), tok_grad.reshape(tokens.shape), enc_grad.reshape(encoder.shape),
        total[7:7 + steps], total[0:3], total[3:6], self_qkv_grad, self_out_grad, cross_query_grad, cross_kv_grad,
        cross_out_grad, ffn_in_grad, total[7 + steps:].reshape(-1), ffn_out_grad, total[6],
    )


def solution(mesh):
    trees = P(("rep", "shard"), None, None)
    rows, columns, flat = P("shard", None), P(None, "shard"), P("shard")
    in_specs = (trees, trees, P(("rep", "shard")), P(("rep", "shard"), None), trees, columns, columns, columns,
                rows, rows, rows, rows, rows, rows, flat, rows, flat)
    out_specs = (trees, trees, trees, columns, columns, columns, rows, rows, rows, rows, rows, rows, flat, rows, flat)
    return jax.shard_map(
        functools.partial(per_device, mesh.shape["shard"]), mesh=mesh, in_specs=in_specs, out_specs=out_specs,
        check_vma=False)
```

```python
import functools

import jax
import jax.numpy as jnp
from jax import lax
from jax.experimental import pallas as pl
from jax.experimental.pallas import tpu as pltpu
from jax.sharding import PartitionSpec as P

BF = jnp.bfloat16
F32 = jnp.float32


def nt(a, b):
    return lax.dot_general(a, b, (((1,), (1,)), ((), ())), preferred_element_type=F32)


def nn(a, b):
    return jnp.dot(a, b, preferred_element_type=F32)


def cost(flops, moved, exps=0):
    return pl.CostEstimate(flops=int(flops), bytes_accessed=int(moved), transcendentals=int(exps))


def kernel_params(axes):
    return pltpu.CompilerParams(vmem_limit_bytes=58 << 20, dimension_semantics=("arbitrary",) * axes)


def split3(x):
    hi = x.astype(BF)
    rest = x - hi.astype(F32)
    mid = rest.astype(BF)
    return hi, mid, (rest - mid.astype(F32)).astype(BF)


def place3(sub, parts, base):
    hi, mid, lo = parts
    return jnp.where(sub == 13, hi, jnp.where(sub == 14, mid, jnp.where(sub == 15, lo, base)))


def forward_tiles(masked, qlen, klen, tile):
    if not masked:
        return [(i, i + tile, klen) for i in range(0, qlen, tile)]
    trunk, segment = qlen - 12 * (qlen // 32), 2 * (qlen // 32)
    cuts = [0, qlen // 2, qlen]
    ends = [min(qlen, -(-max(trunk, b + segment - 1) // 128) * 128) for b in cuts[1:]]
    return list(zip(cuts[:-1], cuts[1:], ends))


def attend_forward_kernel(masked, tile, *refs):
    if masked:
        q_ref, k_ref, v_ref, qm_ref, ko_ref = refs[:5]
    else:
        q_ref, k_ref, v_ref = refs[:3]
    o_ref, ext_ref = refs[-2:]
    lane = lax.broadcasted_iota(jnp.int32, (1, 128), 1)
    first, sub = lane < 64, lane & 63
    zero, one = jnp.zeros((1, 128), BF), jnp.ones((1, 128), BF)
    k, v = k_ref[...], v_ref[...]
    other = ko_ref[...] if masked else zero
    keys = (jnp.where(first, k, other), jnp.where(first, other, k))
    vals = (jnp.where(first, v, one), jnp.where(first, one, v))
    def scores(low, high, count, h):
        q = q_ref[low:high, :] * jnp.asarray(0.125, BF)
        qm = qm_ref[low:high, :] if masked else zero
        return nt(jnp.where(first, q, qm) if h == 0 else jnp.where(first, qm, q), keys[h][:count])

    work = [(*tile, h) for tile in forward_tiles(masked, q_ref.shape[0], k_ref.shape[0], tile) for h in range(2)]
    ahead = scores(*work[0])
    for n, (low, high, count, h) in enumerate(work):
        s = ahead
        if n + 1 < len(work):
            ahead = scores(*work[n + 1])
        peak = jnp.max(s, axis=1, keepdims=True)
        out = nn(jnp.exp(s - peak).astype(BF), vals[h][:count])
        if h == 0:
            kept = out, peak
            continue
        rows = pl.ds(low, high - low)
        sums = jnp.where(first, out, kept[0])
        o_ref[rows, :] = (jnp.where(first, kept[0], out) / pltpu.roll(sums, 64, 1)).astype(BF)
        logsum = jnp.where(first, peak, kept[1]) + jnp.log(sums)
        ext_ref[rows, :] = place3(sub, split3(-logsum), qm_ref[rows, :] if masked else zero)


def extend_blocks(into, args, specs):
    if into is None:
        return {}
    args += list(into)
    specs += [pl.BlockSpec(memory_space=pl.ANY)] * len(into)
    return {len(args) - len(into) + n: n for n in range(len(into))}


def attend_forward(q, k, v, cols, pairs, trees, qm=None, ko=None, into=None, tile=1024):
    qlen, klen = q.shape[0] // trees, k.shape[0] // trees
    tile = min(tile, qlen)
    low, count = pairs[0], pairs[1] - pairs[0]
    at = lambda n, c: pl.BlockSpec((n, 128), lambda t, h: (t, c + low + h))
    specs = [at(qlen, cols[0]), at(klen, cols[1]), at(klen, cols[2])]
    args = [q, k, v]
    if qm is not None:
        specs += [pl.BlockSpec((qlen, 128), lambda t, h: (t, 0)), pl.BlockSpec((klen, 128), lambda t, h: (t, 0))]
        args += [qm, ko]
    aliases = extend_blocks(into, args, specs)
    shape = jax.ShapeDtypeStruct((trees * qlen, 512), BF)
    return pl.pallas_call(
        functools.partial(attend_forward_kernel, qm is not None, tile),
        grid=(trees, count), in_specs=specs, out_specs=[at(qlen, 0)] * 2, out_shape=[shape] * 2,
        input_output_aliases=aliases, compiler_params=kernel_params(2), name="attend_forward",
        cost_estimate=cost(trees * count * qlen * klen * 2000, trees * count * qlen * 1600, trees * count * 2 * qlen * klen),
    )(*args)


def backward_tiles(masked, qlen, klen, tq, tk):
    if not masked:
        return [(j, j + tk, [(i, i + tq) for i in range(0, qlen, tq)]) for j in range(0, klen, tk)]
    trunk, segment = qlen - 12 * (qlen // 32), 2 * (qlen // 32)
    steps = []
    for low, high in [(0, trunk), (trunk, qlen)]:
        start = 0 if low < trunk else (low - segment + 1) // 64 * 64
        spans = [start] + [c for c in range(tq, qlen, tq) if c > start + 128] + [qlen]
        steps.append((low, high, list(zip(spans[:-1], spans[1:]))))
    return steps


def attend_backward_kernel(masked, tq, tk, *refs):
    if masked:
        q_ref, k_ref, v_ref, do_ref, o_ref, ext_ref, ko_ref = refs[:7]
    else:
        q_ref, k_ref, v_ref, do_ref, o_ref, ext_ref = refs[:6]
    dq_ref, dk_ref, dv_ref, qa, qz, da, dz, kt, dqt = refs[-9:]
    lane = lax.broadcasted_iota(jnp.int32, (1, 128), 1)
    first, sub = lane < 64, lane & 63
    zero = jnp.zeros((1, 128), BF)
    ones = jnp.where((sub >= 13) & (sub < 16), jnp.ones((1, 128), BF), zero)
    q = q_ref[...] * jnp.asarray(0.125, BF)
    ext, do = ext_ref[...], do_ref[...]
    prod = do.astype(F32) * o_ref[...].astype(F32)
    for h in range(2):
        mine = first if h == 0 else ~first
        delta = jnp.sum(jnp.where(mine, prod, 0.0), axis=1, keepdims=True)
        parts = place3(sub, split3(jnp.broadcast_to(-delta, prod.shape)), zero)
        qa[h] = jnp.where(mine, q, ext)
        qz[h] = jnp.where(mine, q, zero)
        da[h] = jnp.where(mine, do, parts)
        dz[h] = jnp.where(mine, do, zero)
    kt[...] = k_ref[...].T
    dqt[...] = jnp.zeros_like(dqt)
    def products(k_low, k_high, q_low, q_high, h):
        mine = first if h == 0 else ~first
        k, v = k_ref[k_low:k_high, :], v_ref[k_low:k_high, :]
        other = ko_ref[k_low:k_high, :] if masked else ones
        return (nt(jnp.where(mine, k, other), qa[h, q_low:q_high, :]),
                nt(jnp.where(mine, v, ones), da[h, q_low:q_high, :]))

    work = [(k_low, k_high, q_low, q_high, h)
            for k_low, k_high, spans in backward_tiles(masked, q_ref.shape[0], k_ref.shape[0], tq, tk)
            for q_low, q_high in spans for h in range(2)]
    ahead = products(*work[0])
    for n, (k_low, k_high, q_low, q_high, h) in enumerate(work):
        scores, centred = ahead
        if n + 1 < len(work):
            ahead = products(*work[n + 1])
        if n == 0 or k_low != work[n - 1][0]:
            dk = jnp.zeros((k_high - k_low, 128), F32)
            dv = jnp.zeros((k_high - k_low, 128), F32)
        probs = jnp.exp(scores)
        ds = (probs * centred).astype(BF)
        dv = dv + nn(probs.astype(BF), dz[h, q_low:q_high, :])
        dk = dk + nn(ds, qz[h, q_low:q_high, :])
        dqt[64 * h:64 * h + 64, q_low:q_high] += nn(kt[64 * h:64 * h + 64, k_low:k_high], ds)
        if n + 1 == len(work) or k_low != work[n + 1][0]:
            dk_ref[k_low:k_high, :] = dk.astype(BF)
            dv_ref[k_low:k_high, :] = dv.astype(BF)

    dq_ref[...] = (dqt[...].T * 0.125).astype(BF)


def attend_backward(q, k, v, do, o, ext, cols, pairs, trees, ko=None, into=None, tq=256, tk=512):
    qlen, klen = q.shape[0] // trees, k.shape[0] // trees
    tq, tk = min(tq, qlen), min(tk, klen)
    low, count = pairs[0], pairs[1] - pairs[0]
    at = lambda n, c: pl.BlockSpec((n, 128), lambda t, h: (t, c + low + h))
    specs = [at(qlen, cols[0]), at(klen, cols[1]), at(klen, cols[2])] + [at(qlen, 0)] * 3
    args = [q, k, v, do, o, ext]
    if ko is not None:
        specs += [pl.BlockSpec((klen, 128), lambda t, h: (t, 0))]
        args += [ko]
    aliases = extend_blocks(into, args, specs)
    return pl.pallas_call(
        functools.partial(attend_backward_kernel, ko is not None, tq, tk),
        grid=(trees, count), in_specs=specs, out_specs=[at(qlen, 0), at(klen, 0), at(klen, 0)],
        out_shape=[jax.ShapeDtypeStruct((trees * n, 512), BF) for n in (qlen, klen, klen)],
        scratch_shapes=[pltpu.VMEM((2, qlen, 128), BF)] * 4 + [pltpu.VMEM((128, klen), BF), pltpu.VMEM((128, qlen), F32)],
        input_output_aliases=aliases, compiler_params=kernel_params(2), name="attend_backward",
        cost_estimate=cost(trees * count * qlen * klen * 4000, trees * count * qlen * 2500, trees * count * 2 * qlen * klen),
    )(*args)


TR = 512


def norm_rows(h, gain, bias):
    centred = h - jnp.mean(h, -1, keepdims=True)
    inv = lax.rsqrt(jnp.mean(centred * centred, -1, keepdims=True) + 1e-05)
    normed = centred * inv
    return normed * gain + bias, normed, inv


def norm_pull(dy, normed, inv, gain):
    scaled = dy * gain
    along = jnp.mean(scaled * normed, -1, keepdims=True)
    dx = inv * (scaled - jnp.mean(scaled, -1, keepdims=True) - normed * along)
    return dx, jnp.sum(dy * normed, 0, keepdims=True), jnp.sum(dy, 0, keepdims=True)


def row_spec(width, rows=TR):
    return pl.BlockSpec((rows, width), lambda i, at: (i, 0))


def full_spec(shape):
    return pl.BlockSpec(shape, lambda i, at: (0,) * len(shape))


def part_spec(packed, part, rows):
    return pl.BlockSpec((4, packed.shape[1], rows, 128), lambda i, at: (0, 0, part, 0))


def flip_bits(value, count):
    return sum(((value >> b) & 1) << (count - 1 - b) for b in range(count))


def place_weight(at, relative, ref, dst):
    shards, rows = ref.shape[1], ref.shape[2]
    bits = shards.bit_length() - 1
    for q in range(4):
        for j in range(shards):
            if relative:
                piece = ref[((q & 1) ^ at[0]) * 2 + ((q >> 1) ^ at[1]), flip_bits(j, bits) ^ at[2]]
            else:
                piece = ref[q, j]
            dst[j * rows:(j + 1) * rows, q * 128:(q + 1) * 128] = piece


def pack_grad(at, acc, keep, send, offset):
    shards = keep.shape[1]
    rows = acc.shape[0] // shards
    for q in range(4):
        piece = acc[:, q * 128:(q + 1) * 128].astype(BF).reshape(shards, rows, 128)
        for core in range(2):
            @pl.when(at[0] == core)
            def _(q=q, core=core, piece=piece):
                (keep if (q & 1) == core else send)[(q >> 1) ^ at[1], :, offset:offset + rows, :] = piece


def start_rows(tok_ref, small_ref, per_tree):
    tree = pl.program_id(0) // per_tree
    return tok_ref[...].astype(F32) + small_ref[pl.ds(11 + tree, 1), :]


def clear(*refs):
    for ref in refs:
        ref[...] = jnp.zeros_like(ref)


def gelu_both(x):
    k = 0.7978845608028654
    x2 = x * x
    t = jnp.tanh(k * x * (1.0 + 0.044715 * x2))
    half = 0.5 * (1.0 + t)
    return x * half, half + 0.5 * x * (1.0 - t * t) * (k + (3 * 0.044715 * k) * x2)


def row_call(kernel, name, at, args, specs, outs, out_specs, scratch, steps, flops):
    moved = sum(a.size * a.dtype.itemsize for a in (*args, *outs))
    return pl.pallas_call(
        kernel,
        grid_spec=pltpu.PrefetchScalarGridSpec(
            num_scalar_prefetch=1, grid=(steps,), in_specs=specs, out_specs=out_specs, scratch_shapes=scratch),
        out_shape=outs, compiler_params=kernel_params(1), name=name, cost_estimate=cost(flops, moved),
    )(at, *args)


def sds(shape, dtype):
    return jax.ShapeDtypeStruct(shape, dtype)


def token_rows(starts, first_position, rows):
    position = lax.broadcasted_iota(jnp.int32, (rows, 128), 0) + first_position
    sub = lax.broadcasted_iota(jnp.int32, (rows, 128), 1) & 63
    seg = jnp.zeros((rows, 128), jnp.int32)
    for j in range(1, 13):
        seg = seg + (position >= starts(j)).astype(jnp.int32)
    parent = jnp.where(seg >= 5, 1 + ((seg - 5) >> 1), 0)
    seen = (sub == seg) | (sub == 0) | (sub == parent) | (sub >= 13)
    own = (sub == seg) | ((sub >= 13) & (sub < 16))
    return jnp.where(seen, 0.0, -1e30).astype(BF), jnp.where(own, 1.0, 0.0).astype(BF)


def first_kernel(per_tree, at, seg_ref, tok_ref, small_ref, wq, wk, wv, qkv_ref, barred_ref, own_ref, w):
    step = pl.program_id(0)

    @pl.when(step == 0)
    def _():
        for c, ref in enumerate((wq, wk, wv)):
            place_weight(at, True, ref, w.at[c])

    tree = step // per_tree
    barred_ref[...], own_ref[...] = token_rows(lambda j: seg_ref[tree, j], (step % per_tree) * TR, TR)
    x, _, _ = norm_rows(start_rows(tok_ref, small_ref, per_tree), small_ref[0:1, :], small_ref[3:4, :])
    x = x.astype(BF)
    for c in range(3):
        qkv_ref[:, c * 512:(c + 1) * 512] = nn(x, w[c]).astype(BF)


def first_call(at, seg_starts, tokens, small, packed, per_tree):
    rows, r = tokens.shape[0], 512 // packed.shape[1]
    return row_call(
        functools.partial(first_kernel, per_tree), "project_qkv", at,
        (seg_starts, tokens, small, packed, packed, packed),
        [pl.BlockSpec(memory_space=pltpu.SMEM), row_spec(512), full_spec(small.shape)] + [part_spec(packed, c, r) for c in range(3)],
        (sds((rows, 1536), BF), sds((rows, 128), BF), sds((rows, 128), BF)), [row_spec(1536), row_spec(128), row_spec(128)],
        [pltpu.VMEM((3, 512, 512), BF)], rows // TR, rows * 512 * 1536 * 2)


def second_kernel(per_tree, at, tok_ref, small_ref, mixed_ref, enc_ref, wo, wq, wk, wv, after_ref, cq_ref, ckv_ref, w):
    @pl.when(pl.program_id(0) == 0)
    def _():
        for c, ref in enumerate((wo, wq, wk, wv)):
            place_weight(at, True, ref, w.at[c])

    h = start_rows(tok_ref, small_ref, per_tree) + nn(mixed_ref[...], w[0])
    after_ref[...] = h
    x, _, _ = norm_rows(h, small_ref[1:2, :], small_ref[4:5, :])
    cq_ref[...] = nn(x.astype(BF), w[1]).astype(BF)
    e = enc_ref[...]
    ckv_ref[:, :512] = nn(e, w[2]).astype(BF)
    ckv_ref[:, 512:] = nn(e, w[3]).astype(BF)


def second_call(at, tokens, small, mixed, enc, packed, per_tree):
    rows, r = tokens.shape[0], 512 // packed.shape[1]
    steps = rows // TR
    er = enc.shape[0] // steps
    return row_call(
        functools.partial(second_kernel, per_tree), "cross_inputs", at,
        (tokens, small, mixed, enc, packed, packed, packed, packed),
        [row_spec(512), full_spec(small.shape), row_spec(512), row_spec(512, er)] + [part_spec(packed, c, r) for c in range(4)],
        (sds((rows, 512), F32), sds((rows, 512), BF), sds((enc.shape[0], 1024), BF)),
        [row_spec(512), row_spec(512), row_spec(1024, er)], [pltpu.VMEM((4, 512, 512), BF)], steps, rows * 512 * 1536 * 2)


def ffn_kernel(at, after_ref, mixed_ref, g_ref, small_ref, wi0, wi1, wi2, wi3, wf, wc,
               out_ref, resid_ref, cmg_ref, keep, send, gs_ref, w, wo, aco, afi, afo):
    step = pl.program_id(0)
    r = wc.shape[2]

    @pl.when(step == 0)
    def _():
        clear(aco, afi, afo, gs_ref)
        for c, ref in enumerate((wi0, wi1, wi2, wi3, wc)):
            place_weight(at, False, ref, w.at[c])
        place_weight(at, False, wf, wo)

    mixed, g = mixed_ref[...], g_ref[...]
    h = after_ref[...] + nn(mixed, w[4])
    y, normed, inv = norm_rows(h, small_ref[2:3, :], small_ref[5:6, :])
    third = y.astype(BF)
    third_t, g_t = third.T, g.T
    out = h + small_ref[10:11, :]
    back = jnp.zeros(h.shape, F32)
    for c in range(4):
        wi, wf_c = w[c], wo[c * 512:(c + 1) * 512, :]
        value, slope = gelu_both(nn(third, wi) + small_ref[6 + c:7 + c, :])
        hidden = value.astype(BF)
        out = out + nn(hidden, wf_c)
        pre_grad = (nt(g, wf_c) * slope).astype(BF)
        gs_ref[2 + c:3 + c, :] += jnp.sum(pre_grad.astype(F32), 0, keepdims=True)
        back = back + nt(pre_grad, wi)
        afi[c] += nn(third_t, pre_grad)
        afo[c] += nn(g_t, hidden)
    out_ref[...] = out.astype(BF)
    g_high = g.astype(F32)
    gs_ref[6:7, :] += jnp.sum(g_high, 0, keepdims=True)
    dx, dg, db = norm_pull(back, normed, inv, small_ref[2:3, :])
    gs_ref[0:1, :] += dg
    gs_ref[1:2, :] += db
    resid = g_high + dx
    resid_ref[...] = resid
    low = resid.astype(BF)
    cmg_ref[...] = nt(low, w[4]).astype(BF)
    aco[...] += nn(mixed.T, low)

    @pl.when(step == pl.num_programs(0) - 1)
    def _():
        for c in range(4):
            pack_grad(at, afi[c], keep, send, c * r)
        for c in range(4):
            whole = afo[c].T
            shards = keep.shape[1]
            quarter = shards // 4
            for q in range(4):
                piece = whole[:, q * 128:(q + 1) * 128].astype(BF).reshape(quarter, 4 * r, 128)
                for core in range(2):
                    @pl.when(at[0] == core)
                    def _(q=q, core=core, piece=piece, c=c):
                        (keep if (q & 1) == core else send)[(q >> 1) ^ at[1], c * quarter:(c + 1) * quarter, 4 * r:8 * r, :] = piece
        pack_grad(at, aco[...], keep, send, 8 * r)


def ffn_call(at, after, mixed, g, small, packed):
    rows, shards = after.shape[0], packed.shape[1]
    r = 512 // shards
    half = sds((2, shards, 9 * r, 128), BF)
    return row_call(
        ffn_kernel, "ffn_both_ways", at,
        (after, mixed, g, small) + (packed,) * 6,
        [row_spec(512)] * 3 + [full_spec(small.shape)] + [part_spec(packed, c, r) for c in range(4)]
        + [part_spec(packed, 1, 4 * r), part_spec(packed, 8, r)],
        (sds((rows, 512), BF), sds((rows, 512), F32), sds((rows, 512), BF), half, half, sds((8, 512), F32)),
        [row_spec(512)] * 3 + [full_spec(half.shape)] * 2 + [full_spec((8, 512))],
        [pltpu.VMEM((5, 512, 512), BF), pltpu.VMEM((2048, 512), BF), pltpu.VMEM((512, 512), F32),
         pltpu.VMEM((4, 512, 512), F32), pltpu.VMEM((4, 512, 512), F32)],
        rows // TR, rows * 512 * 2048 * 12)


def middle_kernel(at, cqg_ref, after_ref, resid_ref, mixed_ref, enc_ref, ckg_ref, cvg_ref, small_ref, wo, wq, wk, wv,
                  resid2_ref, smg_ref, encg_ref, keep, send, gs_ref, w, acc):
    step = pl.program_id(0)
    r = wo.shape[2]

    @pl.when(step == 0)
    def _():
        clear(acc, gs_ref)
        for c, ref in enumerate((wo, wq, wk, wv)):
            place_weight(at, True, ref, w.at[c])

    y, normed, inv = norm_rows(after_ref[...], small_ref[1:2, :], small_ref[4:5, :])
    cqg = cqg_ref[...]
    acc[1] += nn(y.astype(BF).T, cqg)
    dx, dg, db = norm_pull(nt(cqg, w[1]), normed, inv, small_ref[1:2, :])
    gs_ref[0:1, :] += dg
    gs_ref[1:2, :] += db
    resid = resid_ref[...] + dx
    resid2_ref[...] = resid
    low = resid.astype(BF)
    acc[0] += nn(mixed_ref[...].T, low)
    smg_ref[...] = nt(low, w[0]).astype(BF)
    enc_t, ckg, cvg = enc_ref[...].T, ckg_ref[...], cvg_ref[...]
    acc[2] += nn(enc_t, ckg)
    acc[3] += nn(enc_t, cvg)
    encg_ref[...] = (nt(ckg, w[2]) + nt(cvg, w[3])).astype(BF)

    @pl.when(step == pl.num_programs(0) - 1)
    def _():
        for c in range(4):
            pack_grad(at, acc[c], keep, send, c * r)


def middle_call(at, cqg, after, resid, mixed, enc, ckg, cvg, small, packed):
    rows, shards = after.shape[0], packed.shape[1]
    r, steps = 512 // shards, rows // TR
    er = enc.shape[0] // steps
    half = sds((2, shards, 4 * r, 128), BF)
    return row_call(
        middle_kernel, "between_attentions", at,
        (cqg, after, resid, mixed, enc, ckg, cvg, small) + (packed,) * 4,
        [row_spec(512)] * 4 + [row_spec(512, er)] * 3 + [full_spec(small.shape)] + [part_spec(packed, c, r) for c in range(4)],
        (sds((rows, 512), F32), sds((rows, 512), BF), sds(enc.shape, BF), half, half, sds((8, 512), F32)),
        [row_spec(512), row_spec(512), row_spec(512, er)] + [full_spec(half.shape)] * 2 + [full_spec((8, 512))],
        [pltpu.VMEM((4, 512, 512), BF), pltpu.VMEM((4, 512, 512), F32)], steps, rows * 512 * 512 * 12)


def last_grads_kernel(per_tree, at, tok_ref, qg_ref, kg_ref, vg_ref, small_ref, keep, send, acc):
    step = pl.program_id(0)

    @pl.when(step == 0)
    def _():
        clear(acc)

    y, _, _ = norm_rows(start_rows(tok_ref, small_ref, per_tree), small_ref[0:1, :], small_ref[3:4, :])
    x_t = y.astype(BF).T
    for c, ref in enumerate((qg_ref, kg_ref, vg_ref)):
        acc[c] += nn(x_t, ref[...])

    @pl.when(step == pl.num_programs(0) - 1)
    def _():
        for c in range(3):
            pack_grad(at, acc[c], keep, send, c * (512 // keep.shape[1]))


def last_grads_call(at, tokens, qg, kg, vg, small, shards, per_tree):
    rows, r = tokens.shape[0], 512 // shards
    half = sds((2, shards, 3 * r, 128), BF)
    return row_call(
        functools.partial(last_grads_kernel, per_tree), "qkv_grads", at, (tokens, qg, kg, vg, small),
        [row_spec(512)] * 4 + [full_spec(small.shape)], (half, half), [full_spec(half.shape)] * 2,
        [pltpu.VMEM((3, 512, 512), F32)], rows // TR, rows * 512 * 1536 * 2)


def last_kernel(per_tree, at, tok_ref, qg_ref, kg_ref, vg_ref, resid_ref, small_ref, wq, wk, wv, tokg_ref, gs_ref, w):
    step = pl.program_id(0)

    @pl.when(step == 0)
    def _():
        clear(gs_ref)
        for c, ref in enumerate((wq, wk, wv)):
            place_weight(at, True, ref, w.at[c])

    _, normed, inv = norm_rows(start_rows(tok_ref, small_ref, per_tree), small_ref[0:1, :], small_ref[3:4, :])
    back = nt(qg_ref[...], w[0]) + nt(kg_ref[...], w[1]) + nt(vg_ref[...], w[2])
    dx, dg, db = norm_pull(back, normed, inv, small_ref[0:1, :])
    gs_ref[0:1, :] += dg
    gs_ref[1:2, :] += db
    resid = resid_ref[...] + dx
    tokg_ref[...] = resid.astype(BF)
    gs_ref[pl.ds(2 + step // per_tree, 1), :] += jnp.sum(resid, 0, keepdims=True)


def last_call(at, tokens, qg, kg, vg, resid, small, packed, per_tree):
    rows, r = tokens.shape[0], 512 // packed.shape[1]
    return row_call(
        functools.partial(last_kernel, per_tree), "first_norm_back", at,
        (tokens, qg, kg, vg, resid, small) + (packed,) * 3,
        [row_spec(512)] * 5 + [full_spec(small.shape)] + [part_spec(packed, c, r) for c in range(3)],
        (sds((rows, 512), BF), sds((8, 512), F32)), [row_spec(512), full_spec((8, 512))],
        [pltpu.VMEM((3, 512, 512), BF)], rows // TR, rows * 512 * 1536 * 2)


def xor_pairs(count, bit):
    return [(i, i ^ bit) for i in range(count)]


def tie(value, *first):
    return lax.optimization_barrier((value, *first))[0]


def swap(value, axis, count, bit):
    return lax.ppermute(value, axis, xor_pairs(count, bit))


def quarter_of(weight, quarter):
    rows, width = weight.shape
    parts = weight.reshape(rows, width // 512, 4, 128)
    mine = lax.dynamic_index_in_dim(parts, quarter, 2, keepdims=False)
    return jnp.transpose(mine, (1, 0, 2)).reshape(-1, 128)


def double(held, axis, count, bit):
    return jnp.concatenate([held, swap(held, axis, count, bit)])


def high_bits(shards):
    return [1 << b for b in range(shards.bit_length() - 2, 0, -1)]


def spread(held, shards, bits):
    flips = [0]
    for bit in bits:
        flips = flips + [f ^ bit for f in flips]
    return jnp.concatenate([held if f == 0 else swap(held, "shard", shards, f) for f in flips])


def add_low(a, b):
    return (a.astype(F32) + b.astype(F32)).astype(BF)


def finish_kernel(parts, extra, at, p0, p1, p2, p3, *outs):
    row = sum(rows * blocks for rows, blocks in parts)
    if extra:
        outs[-1][...] = sum(ref[row:, :].astype(F32) for ref in (p0, p1, p2, p3))
    for k, ref in enumerate((p0, p1, p2, p3)):
        lanes = pl.multiple_of((k ^ (at[1] * 2 + at[0])) * 128, 128)
        row = 0
        for out, (rows, blocks) in zip(outs, parts):
            for c in range(blocks):
                out[:, pl.ds(c * 512 + lanes, 128)] = ref[row:row + rows, :].astype(F32)
                row += rows


def finish(at, piece, others, parts, extra=0):
    spec = lambda shape: pl.BlockSpec(shape, lambda i, at: (0,) * len(shape))
    shapes = [(rows, blocks * 512) for rows, blocks in parts] + ([(extra, 128)] if extra else [])
    return pl.pallas_call(
        functools.partial(finish_kernel, parts, extra),
        grid_spec=pltpu.PrefetchScalarGridSpec(
            num_scalar_prefetch=1, grid=(1,), in_specs=[spec(piece.shape)] * 4, out_specs=[spec(s) for s in shapes]),
        out_shape=[sds(s, F32) for s in shapes], compiler_params=kernel_params(1), name="finish_grads",
        cost_estimate=cost(piece.size * 4, piece.size * 24),
    )(at, piece, *others)


def small_rows(gain, bias, in_bias, out_bias, table):
    width = gain.shape[1]
    rows = jnp.concatenate([gain, bias, in_bias.reshape(4, width), out_bias[None], table])
    return jnp.pad(rows, ((0, -rows.shape[0] % 16), (0, 0)))


def order_shards(held, shards, mine):
    bits = shards.bit_length() - 1
    cube = held.reshape((2,) * bits + held.shape[1:])
    for axis in range(bits):
        cube = jnp.where((mine >> axis) & 1, jnp.flip(cube, axis), cube)
    cube = jnp.transpose(cube, tuple(range(bits - 1, -1, -1)) + tuple(range(bits, cube.ndim)))
    return cube.reshape(held.shape)


def small_table(got, steps):
    shards, _, width = got.shape
    wide = jnp.transpose(got, (1, 0, 2)).reshape(-1, shards * width).astype(F32)
    inner = got[:, 6:10].astype(F32).reshape(4, 512)
    return wide[11:11 + steps], jnp.concatenate([wide[:6], inner, wide[10:11]])


def per_device(shards, tokens, encoder, timesteps, seg_starts, out_grad, time_table, norm_gain, norm_bias, self_qkv,
               self_out, cross_query, cross_kv, cross_out, ffn_in, ffn_in_bias, ffn_out, ffn_out_bias):
    trees, count, width = tokens.shape
    per_tree, r = count // TR, width // shards
    rep, mine = lax.axis_index("rep"), lax.axis_index("shard")
    at = jnp.stack([rep & 1, rep >> 1, flip_bits(mine, shards.bit_length() - 1)]).astype(jnp.int32)
    quarter = lambda *weights: jnp.concatenate([quarter_of(w, rep) for w in weights])
    tok, enc, g = tokens.reshape(-1, width), encoder.reshape(-1, width), out_grad.reshape(-1, width)

    held = quarter(self_qkv)[None]
    held_small = small_rows(norm_gain, norm_bias, ffn_in_bias, ffn_out_bias, time_table)[None]
    bit, hop = shards // 2, 0
    while bit:
        held, held_small = lax.optimization_barrier((double(held, "shard", shards, bit), double(held_small, "shard", shards, bit)))
        if hop == 0:
            later = (self_out, cross_query, cross_kv, ffn_in, ffn_out, cross_out)
            self_out, cross_query, cross_kv, ffn_in, ffn_out, cross_out = tie(later, held)
            piece3 = quarter(ffn_in, ffn_out, cross_out)
            piece2 = quarter(self_out, cross_query, cross_kv)
        if hop == 1:
            packed3 = lax.all_gather(tie(piece3, held), ("rep", "shard"), axis=0).reshape(4, shards, *piece3.shape)
        bit //= 2
        hop += 1
    steps = time_table.shape[0]
    table, small = small_table(order_shards(held_small, shards, mine), steps)
    rows_of = jnp.concatenate([lax.dynamic_slice_in_dim(table, timesteps[t], 1, 0) for t in range(trees)])
    small = jnp.concatenate([small, rows_of])
    small = jnp.pad(small, ((0, -small.shape[0] % 8), (0, 0)))
    held, small, piece2 = lax.optimization_barrier((double(held, "rep", 4, 2), small, piece2))
    packed1 = double(held, "rep", 4, 1).reshape(4, shards, -1, 128)

    held2 = spread(tie(piece2, packed1)[None], shards, high_bits(shards))
    qkv, barred, own = first_call(at, seg_starts, tok, small, packed1, per_tree)
    under = lambda done, moved: lax.optimization_barrier((done, moved))
    attend = functools.partial(attend_forward, qm=barred, ko=own)
    qkv, held2 = under(qkv, held2)
    held2 = double(held2, "shard", shards, 1)
    fwd = attend(qkv, qkv, qkv, (0, 4, 8), (0, 1), trees)
    fwd, held2 = under(fwd, held2)
    held2 = double(held2, "rep", 4, 2)
    fwd = attend(qkv, qkv, qkv, (0, 4, 8), (1, 3), trees, into=fwd)
    fwd, held2 = under(fwd, held2)
    held2 = double(held2, "rep", 4, 1)
    self_mixed, self_ext = attend(qkv, qkv, qkv, (0, 4, 8), (3, 4), trees, into=fwd)
    packed2 = held2.reshape(4, shards, -1, 128)
    after_self, cq, ckv = second_call(at, tok, small, self_mixed, enc, packed2, per_tree)
    cross_mixed, cross_ext = attend_forward(cq, ckv, ckv, (0, 0, 4), (0, 4), trees)
    out, resid, cross_back, keep3, send3, small3 = ffn_call(at, after_self, cross_mixed, g, small, packed3)

    def landed(done, got, adds):
        done, got = lax.optimization_barrier((done, got))
        return lax.optimization_barrier((done, adds(got)))

    exchange = lambda v: lax.all_to_all(v, "shard", split_axis=0, concat_axis=0, tiled=True)
    sum_over = lambda v: jnp.sum(v.astype(F32), 0).astype(BF)
    halves = lambda keep: lambda got: (add_low(keep[0], got[0]), add_low(keep[1], got[1]))
    replicas = lambda v: [swap(v, "rep", 4, k) for k in (1, 2, 3)]
    got3 = swap(send3, "rep", 4, 1)
    cross = functools.partial(attend_backward, cq, ckv, ckv, cross_back, cross_mixed, cross_ext, (0, 0, 4))
    bwd, (mine3, other3) = landed(cross((0, 2), trees), got3, halves(keep3))
    got3 = swap(other3, "rep", 4, 2)
    cqg, ckg, cvg = cross((2, 4), trees, into=bwd)
    resid, self_back, enc_grad, keep2, send2, small2 = middle_call(
        at, cqg, after_self, resid, self_mixed, enc, ckg, cvg, small, packed2)
    (self_back, send2), mine3 = landed((self_back, send2), got3, lambda got: add_low(mine3, got))
    got3, got2 = exchange(mine3), swap(send2, "rep", 4, 1)
    self_ = functools.partial(attend_backward, qkv, qkv, qkv, self_back, self_mixed, self_ext, (0, 4, 8), ko=own)
    bwd, (mine2, other2) = landed(self_((0, 1), trees), got2, halves(keep2))
    got2 = swap(other2, "rep", 4, 2)
    bwd, (done3, mine2) = landed(self_((1, 3), trees, into=bwd), (got3, got2), lambda got: (sum_over(got[0]), add_low(mine2, got[1])))
    others3, got2 = replicas(done3), exchange(mine2)
    qg, kg, vg = self_((3, 4), trees, into=bwd)
    keep1, send1 = last_grads_call(at, tok, qg, kg, vg, small, shards, per_tree)
    (send1, others3), done2 = landed((send1, others3), got2, sum_over)
    others2, got1 = replicas(done2), swap(send1, "rep", 4, 1)
    tok_grad, small1 = last_call(at, tok, tie(qg, done2), kg, vg, resid, small, packed1, per_tree)
    (tok_grad, small1, others2), (mine1, other1) = landed((tok_grad, small1, others2), got1, halves(keep1))
    got1 = swap(other1, "rep", 4, 2)

    steps_hot = (lax.broadcasted_iota(jnp.int32, (trees, steps), 1) == timesteps[:, None]).astype(F32)
    table_grad = jnp.einsum("ts,tw->sw", steps_hot, small1[2:2 + trees], precision=lax.Precision.HIGHEST)
    sums = jnp.concatenate([
        small1[0:1], small2[0:1], small3[0:1], small1[1:2], small2[1:2], small3[1:2], small3[6:7], table_grad])
    by_shard = jnp.transpose(sums.reshape(-1, shards, r), (1, 0, 2))
    by_shard = jnp.concatenate([by_shard, small3[2:6].reshape(shards, 4, r)], 1).reshape(shards, -1).astype(BF)
    by_shard = jnp.pad(by_shard, ((0, 0), (0, -by_shard.shape[1] % 2048)))
    extra = by_shard.shape[1] // 128
    mine1 = jnp.concatenate([add_low(mine1, got1), by_shard.reshape(shards, extra, 128)], 1)
    got1 = exchange(mine1)
    ffn_in_grad, ffn_out_grad, cross_out_grad = finish(at, done3, others3, ((r, 4), (4 * r, 1), (r, 1)))
    self_out_grad, cross_query_grad, cross_kv_grad = finish(at, done2, others2, ((r, 1), (r, 1), (r, 2)))
    early = (ffn_in_grad, ffn_out_grad, cross_out_grad, self_out_grad, cross_query_grad, cross_kv_grad)
    early, done1 = landed(early, got1, sum_over)
    ffn_in_grad, ffn_out_grad, cross_out_grad, self_out_grad, cross_query_grad, cross_kv_grad = early
    others1 = replicas(done1)
    self_qkv_grad, total = finish(at, done1, others1, ((r, 3),), extra)
    total = total.reshape(-1)[:(11 + steps) * r].reshape(11 + steps, r)
    return (
        out.reshape(tokens.shape), tok_grad.reshape(tokens.shape), enc_grad.reshape(encoder.shape),
        total[7:7 + steps], total[0:3], total[3:6], self_qkv_grad, self_out_grad, cross_query_grad, cross_kv_grad,
        cross_out_grad, ffn_in_grad, total[7 + steps:].reshape(-1), ffn_out_grad, total[6],
    )


def solution(mesh):
    trees = P(("rep", "shard"), None, None)
    rows, columns, flat = P("shard", None), P(None, "shard"), P("shard")
    in_specs = (trees, trees, P(("rep", "shard")), P(("rep", "shard"), None), trees, columns, columns, columns,
                rows, rows, rows, rows, rows, rows, flat, rows, flat)
    out_specs = (trees, trees, trees, columns, columns, columns, rows, rows, rows, rows, rows, rows, flat, rows, flat)
    return jax.shard_map(
        functools.partial(per_device, mesh.shape["shard"]), mesh=mesh, in_specs=in_specs, out_specs=out_specs,
        check_vma=False)
```

```python
import functools

import jax
import jax.numpy as jnp
from jax import lax
from jax.experimental import pallas as pl
from jax.experimental.pallas import tpu as pltpu
from jax.sharding import PartitionSpec as P

BF = jnp.bfloat16
F32 = jnp.float32


def nt(a, b):
    return lax.dot_general(a, b, (((1,), (1,)), ((), ())), preferred_element_type=F32)


def nn(a, b):
    return jnp.dot(a, b, preferred_element_type=F32)


def cost(flops, moved, exps=0):
    return pl.CostEstimate(flops=int(flops), bytes_accessed=int(moved), transcendentals=int(exps))


def kernel_params(axes):
    return pltpu.CompilerParams(vmem_limit_bytes=58 << 20, dimension_semantics=("arbitrary",) * axes)


def split3(x):
    hi = x.astype(BF)
    rest = x - hi.astype(F32)
    mid = rest.astype(BF)
    return hi, mid, (rest - mid.astype(F32)).astype(BF)


def place3(sub, parts, base):
    hi, mid, lo = parts
    return jnp.where(sub == 13, hi, jnp.where(sub == 14, mid, jnp.where(sub == 15, lo, base)))


def forward_tiles(masked, qlen, klen, tile):
    if not masked:
        return [(i, i + tile, klen) for i in range(0, qlen, tile)]
    trunk, segment = qlen - 12 * (qlen // 32), 2 * (qlen // 32)
    cuts = [0, qlen // 2, qlen]
    ends = [min(qlen, -(-max(trunk, b + segment - 1) // 128) * 128) for b in cuts[1:]]
    return list(zip(cuts[:-1], cuts[1:], ends))


def attend_forward_kernel(masked, tile, *refs):
    if masked:
        q_ref, k_ref, v_ref, qm_ref, ko_ref = refs[:5]
    else:
        q_ref, k_ref, v_ref = refs[:3]
    o_ref, ext_ref = refs[-2:]
    lane = lax.broadcasted_iota(jnp.int32, (1, 128), 1)
    first, sub = lane < 64, lane & 63
    zero, one = jnp.zeros((1, 128), BF), jnp.ones((1, 128), BF)
    k, v = k_ref[...], v_ref[...]
    other = ko_ref[...] if masked else zero
    keys = (jnp.where(first, k, other), jnp.where(first, other, k))
    vals = (jnp.where(first, v, one), jnp.where(first, one, v))
    def scores(low, high, count, h):
        q = q_ref[low:high, :] * jnp.asarray(0.125, BF)
        qm = qm_ref[low:high, :] if masked else zero
        return nt(jnp.where(first, q, qm) if h == 0 else jnp.where(first, qm, q), keys[h][:count])

    work = [(*tile, h) for tile in forward_tiles(masked, q_ref.shape[0], k_ref.shape[0], tile) for h in range(2)]
    ahead = scores(*work[0])
    for n, (low, high, count, h) in enumerate(work):
        s = ahead
        if n + 1 < len(work):
            ahead = scores(*work[n + 1])
        peak = jnp.max(s, axis=1, keepdims=True)
        out = nn(jnp.exp(s - peak).astype(BF), vals[h][:count])
        if h == 0:
            kept = out, peak
            continue
        rows = pl.ds(low, high - low)
        sums = jnp.where(first, out, kept[0])
        o_ref[rows, :] = (jnp.where(first, kept[0], out) / pltpu.roll(sums, 64, 1)).astype(BF)
        logsum = jnp.where(first, peak, kept[1]) + jnp.log(sums)
        ext_ref[rows, :] = place3(sub, split3(-logsum), qm_ref[rows, :] if masked else zero)


def attend_forward(q, k, v, cols, pairs, trees, qm=None, ko=None, tile=1024):
    qlen, klen = q.shape[0] // trees, k.shape[0] // trees
    tile = min(tile, qlen)
    low, count = pairs[0], pairs[1] - pairs[0]
    at = lambda n, c: pl.BlockSpec((n, 128), lambda t, h: (t, c + h))
    specs = [at(qlen, cols[0] + low), at(klen, cols[1] + low), at(klen, cols[2] + low)]
    args = [q, k, v]
    if qm is not None:
        specs += [pl.BlockSpec((qlen, 128), lambda t, h: (t, 0)), pl.BlockSpec((klen, 128), lambda t, h: (t, 0))]
        args += [qm, ko]
    shape = jax.ShapeDtypeStruct((trees * qlen, count * 128), BF)
    return pl.pallas_call(
        functools.partial(attend_forward_kernel, qm is not None, tile),
        grid=(trees, count), in_specs=specs, out_specs=[at(qlen, 0)] * 2, out_shape=[shape] * 2,
        compiler_params=kernel_params(2), name="attend_forward",
        cost_estimate=cost(trees * count * qlen * klen * 2000, trees * count * qlen * 1600, trees * count * 2 * qlen * klen),
    )(*args)


def backward_tiles(masked, qlen, klen, tq, tk):
    if not masked:
        return [(j, j + tk, [(i, i + tq) for i in range(0, qlen, tq)]) for j in range(0, klen, tk)]
    trunk, segment = qlen - 12 * (qlen // 32), 2 * (qlen // 32)
    steps = []
    for low, high in [(0, trunk), (trunk, qlen)]:
        start = 0 if low < trunk else (low - segment + 1) // 64 * 64
        spans = [start] + [c for c in range(tq, qlen, tq) if c > start + 128] + [qlen]
        steps.append((low, high, list(zip(spans[:-1], spans[1:]))))
    return steps


def attend_backward_kernel(masked, tq, tk, *refs):
    if masked:
        q_ref, k_ref, v_ref, do_ref, o_ref, ext_ref, ko_ref = refs[:7]
    else:
        q_ref, k_ref, v_ref, do_ref, o_ref, ext_ref = refs[:6]
    dq_ref, dk_ref, dv_ref, qa, qz, da, dz, kt, dqt = refs[-9:]
    lane = lax.broadcasted_iota(jnp.int32, (1, 128), 1)
    first, sub = lane < 64, lane & 63
    zero = jnp.zeros((1, 128), BF)
    ones = jnp.where((sub >= 13) & (sub < 16), jnp.ones((1, 128), BF), zero)
    q = q_ref[...] * jnp.asarray(0.125, BF)
    ext, do = ext_ref[...], do_ref[...]
    prod = do.astype(F32) * o_ref[...].astype(F32)
    for h in range(2):
        mine = first if h == 0 else ~first
        delta = jnp.sum(jnp.where(mine, prod, 0.0), axis=1, keepdims=True)
        parts = place3(sub, split3(jnp.broadcast_to(-delta, prod.shape)), zero)
        qa[h] = jnp.where(mine, q, ext)
        qz[h] = jnp.where(mine, q, zero)
        da[h] = jnp.where(mine, do, parts)
        dz[h] = jnp.where(mine, do, zero)
    kt[...] = k_ref[...].T
    dqt[...] = jnp.zeros_like(dqt)
    def products(k_low, k_high, q_low, q_high, h):
        mine = first if h == 0 else ~first
        k, v = k_ref[k_low:k_high, :], v_ref[k_low:k_high, :]
        other = ko_ref[k_low:k_high, :] if masked else ones
        return (nt(jnp.where(mine, k, other), qa[h, q_low:q_high, :]),
                nt(jnp.where(mine, v, ones), da[h, q_low:q_high, :]))

    work = [(k_low, k_high, q_low, q_high, h)
            for k_low, k_high, spans in backward_tiles(masked, q_ref.shape[0], k_ref.shape[0], tq, tk)
            for q_low, q_high in spans for h in range(2)]
    ahead = products(*work[0])
    for n, (k_low, k_high, q_low, q_high, h) in enumerate(work):
        scores, centred = ahead
        if n + 1 < len(work):
            ahead = products(*work[n + 1])
        if n == 0 or k_low != work[n - 1][0]:
            dk = jnp.zeros((k_high - k_low, 128), F32)
            dv = jnp.zeros((k_high - k_low, 128), F32)
        probs = jnp.exp(scores)
        ds = (probs * centred).astype(BF)
        dv = dv + nn(probs.astype(BF), dz[h, q_low:q_high, :])
        dk = dk + nn(ds, qz[h, q_low:q_high, :])
        dqt[64 * h:64 * h + 64, q_low:q_high] += nn(kt[64 * h:64 * h + 64, k_low:k_high], ds)
        if n + 1 == len(work) or k_low != work[n + 1][0]:
            dk_ref[k_low:k_high, :] = dk.astype(BF)
            dv_ref[k_low:k_high, :] = dv.astype(BF)

    dq_ref[...] = (dqt[...].T * 0.125).astype(BF)


def attend_backward(q, k, v, do, o, ext, cols, pairs, trees, ko=None, mixed_from=0, tq=256, tk=512):
    qlen, klen = q.shape[0] // trees, k.shape[0] // trees
    tq, tk = min(tq, qlen), min(tk, klen)
    low, count = pairs[0], pairs[1] - pairs[0]
    at = lambda n, c: pl.BlockSpec((n, 128), lambda t, h: (t, c + h))
    specs = [at(qlen, cols[0] + low), at(klen, cols[1] + low), at(klen, cols[2] + low), at(qlen, low)]
    specs += [at(qlen, low - mixed_from)] * 2
    args = [q, k, v, do, o, ext]
    if ko is not None:
        specs += [pl.BlockSpec((klen, 128), lambda t, h: (t, 0))]
        args += [ko]
    return pl.pallas_call(
        functools.partial(attend_backward_kernel, ko is not None, tq, tk),
        grid=(trees, count), in_specs=specs, out_specs=[at(qlen, 0), at(klen, 0), at(klen, 0)],
        out_shape=[jax.ShapeDtypeStruct((trees * n, count * 128), BF) for n in (qlen, klen, klen)],
        scratch_shapes=[pltpu.VMEM((2, qlen, 128), BF)] * 4 + [pltpu.VMEM((128, klen), BF), pltpu.VMEM((128, qlen), F32)],
        compiler_params=kernel_params(2), name="attend_backward",
        cost_estimate=cost(trees * count * qlen * klen * 4000, trees * count * qlen * 2500, trees * count * 2 * qlen * klen),
    )(*args)


TR = 512
RESID = F32


def norm_rows(h, gain, bias):
    centred = h - jnp.mean(h, -1, keepdims=True)
    inv = lax.rsqrt(jnp.mean(centred * centred, -1, keepdims=True) + 1e-05)
    normed = centred * inv
    return normed * gain + bias, normed, inv


def norm_pull(dy, normed, inv, gain):
    scaled = dy * gain
    along = jnp.mean(scaled * normed, -1, keepdims=True)
    dx = inv * (scaled - jnp.mean(scaled, -1, keepdims=True) - normed * along)
    return dx, jnp.sum(dy * normed, 0, keepdims=True), jnp.sum(dy, 0, keepdims=True)


def row_spec(width, rows=TR):
    return pl.BlockSpec((rows, width), lambda i, at: (i, 0))


def full_spec(shape):
    return pl.BlockSpec(shape, lambda i, at: (0,) * len(shape))


def part_spec(packed, part, rows):
    lead = packed.shape[:-2]
    return pl.BlockSpec((*lead, rows, 128), lambda i, at: (0,) * len(lead) + (part, 0))


def flip_bits(value, count):
    return sum(((value >> b) & 1) << (count - 1 - b) for b in range(count))


def place_weight(at, relative, ref, dst):
    shards, rows = ref.shape[1], ref.shape[-2]
    bits = shards.bit_length() - 1
    for q in range(4):
        for j in range(shards):
            if relative and len(ref.shape) == 5:
                piece = ref[(q & 1) ^ at[0], flip_bits(j, bits) ^ at[2], (q >> 1) ^ at[1]]
            elif relative:
                piece = ref[((q & 1) ^ at[0]) * 2 + ((q >> 1) ^ at[1]), flip_bits(j, bits) ^ at[2]]
            else:
                piece = ref[q, j]
            dst[j * rows:(j + 1) * rows, q * 128:(q + 1) * 128] = piece


def pack_grad(at, acc, keep, send, offset):
    shards = keep.shape[1]
    rows = acc.shape[0] // shards
    for q in range(4):
        piece = acc[:, q * 128:(q + 1) * 128].astype(BF).reshape(shards, rows, 128)
        for core in range(2):
            @pl.when(at[0] == core)
            def _(q=q, core=core, piece=piece):
                (keep if (q & 1) == core else send)[(q >> 1) ^ at[1], :, offset:offset + rows, :] = piece


def start_rows(tok_ref, small_ref, per_tree):
    tree = pl.program_id(0) // per_tree
    return tok_ref[...].astype(F32) + small_ref[pl.ds(11 + tree, 1), :]


def side_by_side(refs):
    return jnp.concatenate([ref[...] for ref in refs], 1) if len(refs) > 1 else refs[0][...]


def clear(*refs):
    for ref in refs:
        ref[...] = jnp.zeros_like(ref)


def gelu_both(x):
    k = 0.7978845608028654
    x2 = x * x
    t = jnp.tanh(k * x * (1.0 + 0.044715 * x2))
    half = 0.5 * (1.0 + t)
    return x * half, half + 0.5 * x * (1.0 - t * t) * (k + (3 * 0.044715 * k) * x2)


def row_call(kernel, name, at, args, specs, outs, out_specs, scratch, steps, flops):
    moved = sum(a.size * a.dtype.itemsize for a in (*args, *outs))
    return pl.pallas_call(
        kernel,
        grid_spec=pltpu.PrefetchScalarGridSpec(
            num_scalar_prefetch=1, grid=(steps,), in_specs=specs, out_specs=out_specs, scratch_shapes=scratch),
        out_shape=outs, compiler_params=kernel_params(1), name=name, cost_estimate=cost(flops, moved),
    )(at, *args)


def sds(shape, dtype):
    return jax.ShapeDtypeStruct(shape, dtype)


def token_rows(starts, first_position, rows):
    position = lax.broadcasted_iota(jnp.int32, (rows, 128), 0) + first_position
    sub = lax.broadcasted_iota(jnp.int32, (rows, 128), 1) & 63
    seg = jnp.zeros((rows, 128), jnp.int32)
    for j in range(1, 13):
        seg = seg + (position >= starts(j)).astype(jnp.int32)
    parent = jnp.where(seg >= 5, 1 + ((seg - 5) >> 1), 0)
    seen = (sub == seg) | (sub == 0) | (sub == parent) | (sub >= 13)
    own = (sub == seg) | ((sub >= 13) & (sub < 16))
    return jnp.where(seen, 0.0, -1e30).astype(BF), jnp.where(own, 1.0, 0.0).astype(BF)


SMALL = 32
TABLE = 11


def pack_kernel(at, qkv, so, cq, ckv, co, fi, fo, gain, bias, in_bias, out_bias, table, p1, p2, p3, scratch):
    for out, flip, weights in ((p1.at[0], 0, (qkv,)), (p1.at[1], 2, (qkv,)), (p2, 0, (so, cq, ckv)), (p3, 0, (fi, fo, co))):
        lanes = pl.multiple_of(((at[1] * 2 + at[0]) ^ flip) * 128, 128)
        row = 0
        for ref in weights:
            for c in range(ref.shape[1] // 512):
                out[row:row + ref.shape[0], :] = ref[:, pl.ds(c * 512 + lanes, 128)]
                row += ref.shape[0]
    wide, steps, split = gain.shape[1], table.shape[0], SMALL - TABLE
    clear(scratch)
    for row, ref in ((0, gain), (3, bias), (10, out_bias)):
        scratch[row:row + ref.shape[0], :wide] = ref[...].astype(F32)
    for a in range(4):
        scratch[6 + a:7 + a, :wide] = in_bias[:, a * wide:(a + 1) * wide].astype(F32)
    scratch[TABLE:, :wide] = table[:split, :].astype(F32)
    scratch[:steps - split, 64:64 + wide] = table[split:, :].astype(F32)
    for half in range(2):
        p1[half, p1.shape[1] - SMALL:, :] = scratch[...].astype(BF)


def small_row(r):
    return -(-3 * r // SMALL) * SMALL


def pack_call(at, *args):
    r = args[0].shape[0]
    outs = (sds((2, small_row(r) + SMALL, 128), BF), sds((4 * r, 128), BF), sds((9 * r, 128), BF))
    return row_call(pack_kernel, "pack_quarters", at, args, [full_spec(a.shape) for a in args], outs,
                    [full_spec(o.shape) for o in outs], [pltpu.VMEM((SMALL, 128), F32)], 1, 0)


def join_lanes(pieces, wide):
    lane = lax.broadcasted_iota(jnp.int32, (1, 128), 1)
    out = pieces[0]
    for k, piece in enumerate(pieces[1:], 1):
        out = jnp.where(lane >= wide * k, pltpu.roll(piece, wide * k, 1), out)
    return out


def unpack_small(at, step_ref, ref, shards, trees, small, rows):
    wide, bits = 512 // shards, shards.bit_length() - 1
    each = 128 // wide
    pieces = [ref[0, flip_bits(j, bits) ^ at[2], 0].astype(F32) for j in range(shards)]
    turned = [pltpu.roll(p, 64, 1) for p in pieces]
    clear(small)
    for g in range(4):
        lanes = slice(g * 128, g * 128 + 128)
        rows[:SMALL, lanes] = join_lanes(pieces[g * each:(g + 1) * each], wide)
        rows[SMALL:, lanes] = join_lanes(turned[g * each:(g + 1) * each], wide)
    for n in range(16):
        parts = [divmod(n * each + k, 4) for k in range(each)]
        small[6 + n // 4:7 + n // 4, n % 4 * 128:n % 4 * 128 + 128] = join_lanes(
            [pieces[j][6 + a:7 + a, :] for j, a in parts], wide)
    small[0:6, :] = rows[0:6, :]
    small[10:11, :] = rows[10:11, :]
    for t in range(trees):
        small[TABLE + t:TABLE + t + 1, :] = rows[pl.ds(TABLE + step_ref[t], 1), :]


def first_kernel(shards, trees, per_tree, at, seg_ref, step_ref, tok_ref, held_ref, wq, wk, wv,
                 qkv_ref, barred_ref, own_ref, small_ref, w, small, rows):
    step = pl.program_id(0)

    @pl.when(step == 0)
    def _():
        for c, ref in enumerate((wq, wk, wv)):
            place_weight(at, True, ref, w.at[c])
        unpack_small(at, step_ref, held_ref, shards, trees, small, rows)
        small_ref[...] = small[...]

    tree = step // per_tree
    barred_ref[...], own_ref[...] = token_rows(lambda j: seg_ref[tree, j], (step % per_tree) * TR, TR)
    x, _, _ = norm_rows(start_rows(tok_ref, small, per_tree), small[0:1, :], small[3:4, :])
    x = x.astype(BF)
    for c in range(3):
        qkv_ref[:, c * 512:(c + 1) * 512] = nn(x, w[c]).astype(BF)


def first_call(at, seg_starts, timesteps, tokens, packed, per_tree):
    rows, shards, trees = tokens.shape[0], packed.shape[1], seg_starts.shape[0]
    r = 512 // shards
    held = pl.BlockSpec((1, shards, 1, SMALL, 128), lambda i, at: (0, 0, 0, small_row(r) // SMALL, 0))
    scalars = pl.BlockSpec(memory_space=pltpu.SMEM)
    lines = 16 * -(-(TABLE + trees) // 16)
    return row_call(
        functools.partial(first_kernel, shards, trees, per_tree), "project_qkv", at,
        (seg_starts, timesteps, tokens, packed, packed, packed, packed),
        [scalars, scalars, row_spec(512), held] + [part_spec(packed, c, r) for c in range(3)],
        (sds((rows, 1536), BF), sds((rows, 128), BF), sds((rows, 128), BF), sds((lines, 512), F32)),
        [row_spec(1536), row_spec(128), row_spec(128), full_spec((lines, 512))],
        [pltpu.VMEM((3, 512, 512), BF), pltpu.VMEM((lines, 512), F32), pltpu.VMEM((2 * SMALL, 512), F32)],
        rows // TR, rows * 512 * 1536 * 2)


def second_kernel(per_tree, count, at, tok_ref, small_ref, enc_ref, wo, wq, wk, wv, *refs):
    mixed_refs, (after_ref, cq_ref, ckv_ref, w) = refs[:count], refs[count:]

    @pl.when(pl.program_id(0) == 0)
    def _():
        for c, ref in enumerate((wo, wq, wk, wv)):
            place_weight(at, True, ref, w.at[c])

    h = start_rows(tok_ref, small_ref, per_tree) + nn(side_by_side(mixed_refs), w[0])
    after_ref[...] = h.astype(RESID)
    x, _, _ = norm_rows(h, small_ref[1:2, :], small_ref[4:5, :])
    cq_ref[...] = nn(x.astype(BF), w[1]).astype(BF)
    e = enc_ref[...]
    ckv_ref[:, :512] = nn(e, w[2]).astype(BF)
    ckv_ref[:, 512:] = nn(e, w[3]).astype(BF)


def second_call(at, tokens, small, mixed, enc, packed, per_tree):
    rows, r = tokens.shape[0], 512 // packed.shape[1]
    steps = rows // TR
    er = enc.shape[0] // steps
    return row_call(
        functools.partial(second_kernel, per_tree, len(mixed)), "cross_inputs", at,
        (tokens, small, enc, packed, packed, packed, packed, *mixed),
        [row_spec(512), full_spec(small.shape), row_spec(512, er)] + [part_spec(packed, c, r) for c in range(4)]
        + [row_spec(m.shape[1]) for m in mixed],
        (sds((rows, 512), RESID), sds((rows, 512), BF), sds((enc.shape[0], 1024), BF)),
        [row_spec(512), row_spec(512), row_spec(1024, er)], [pltpu.VMEM((4, 512, 512), BF)], steps, rows * 512 * 1536 * 2)


def ffn_kernel(at, after_ref, mixed_ref, g_ref, small_ref, wi0, wi1, wi2, wi3, wf, wc,
               out_ref, resid_ref, cmg_ref, keep, send, gs_ref, w, wo, aco, afi, afo):
    step = pl.program_id(0)
    r = wc.shape[-2]

    @pl.when(step == 0)
    def _():
        clear(aco, afi, afo, gs_ref)
        for c, ref in enumerate((wi0, wi1, wi2, wi3, wc)):
            place_weight(at, False, ref, w.at[c])
        place_weight(at, False, wf, wo)

    mixed, g = mixed_ref[...], g_ref[...]
    h = after_ref[...].astype(F32) + nn(mixed, w[4])
    y, normed, inv = norm_rows(h, small_ref[2:3, :], small_ref[5:6, :])
    third = y.astype(BF)
    third_t, g_t = third.T, g.T
    out = h + small_ref[10:11, :]
    back = jnp.zeros(h.shape, F32)
    for c in range(4):
        wi, wf_c = w[c], wo[c * 512:(c + 1) * 512, :]
        value, slope = gelu_both(nn(third, wi) + small_ref[6 + c:7 + c, :])
        hidden = value.astype(BF)
        out = out + nn(hidden, wf_c)
        pre_grad = (nt(g, wf_c) * slope).astype(BF)
        gs_ref[2 + c:3 + c, :] += jnp.sum(pre_grad.astype(F32), 0, keepdims=True)
        back = back + nt(pre_grad, wi)
        afi[c] += nn(third_t, pre_grad)
        afo[c] += nn(g_t, hidden)
    out_ref[...] = out.astype(BF)
    g_high = g.astype(F32)
    gs_ref[6:7, :] += jnp.sum(g_high, 0, keepdims=True)
    dx, dg, db = norm_pull(back, normed, inv, small_ref[2:3, :])
    gs_ref[0:1, :] += dg
    gs_ref[1:2, :] += db
    resid = g_high + dx
    resid_ref[...] = resid.astype(RESID)
    low = resid.astype(BF)
    cmg_ref[...] = nt(low, w[4]).astype(BF)
    aco[...] += nn(mixed.T, low)

    @pl.when(step == pl.num_programs(0) - 1)
    def _():
        for c in range(4):
            pack_grad(at, afi[c], keep, send, c * r)
        for c in range(4):
            whole = afo[c].T
            shards = keep.shape[1]
            quarter = shards // 4
            for q in range(4):
                piece = whole[:, q * 128:(q + 1) * 128].astype(BF).reshape(quarter, 4 * r, 128)
                for core in range(2):
                    @pl.when(at[0] == core)
                    def _(q=q, core=core, piece=piece, c=c):
                        (keep if (q & 1) == core else send)[(q >> 1) ^ at[1], c * quarter:(c + 1) * quarter, 4 * r:8 * r, :] = piece
        pack_grad(at, aco[...], keep, send, 8 * r)


def ffn_call(at, after, mixed, g, small, packed):
    rows, shards = after.shape[0], packed.shape[1]
    r = 512 // shards
    half = sds((2, shards, 9 * r, 128), BF)
    return row_call(
        ffn_kernel, "ffn_both_ways", at,
        (after, mixed, g, small) + (packed,) * 6,
        [row_spec(512)] * 3 + [full_spec(small.shape)] + [part_spec(packed, c, r) for c in range(4)]
        + [part_spec(packed, 1, 4 * r), part_spec(packed, 8, r)],
        (sds((rows, 512), BF), sds((rows, 512), RESID), sds((rows, 512), BF), half, half, sds((8, 512), F32)),
        [row_spec(512)] * 3 + [full_spec(half.shape)] * 2 + [full_spec((8, 512))],
        [pltpu.VMEM((5, 512, 512), BF), pltpu.VMEM((2048, 512), BF), pltpu.VMEM((512, 512), F32),
         pltpu.VMEM((4, 512, 512), F32), pltpu.VMEM((4, 512, 512), F32)],
        rows // TR, rows * 512 * 2048 * 12)


def middle_kernel(mixes, chunks, at, after_ref, resid_ref, enc_ref, small_ref, wo, wq, wk, wv, *refs):
    mixed_refs, refs = refs[:mixes], refs[mixes:]
    cqg_refs, ckg_refs, cvg_refs = refs[:chunks], refs[chunks:2 * chunks], refs[2 * chunks:3 * chunks]
    resid2_ref, smg_ref, encg_ref, keep, send, gs_ref, w, acc = refs[3 * chunks:]
    step = pl.program_id(0)
    r = wo.shape[-2]

    @pl.when(step == 0)
    def _():
        clear(acc, gs_ref)
        for c, ref in enumerate((wo, wq, wk, wv)):
            place_weight(at, True, ref, w.at[c])

    y, normed, inv = norm_rows(after_ref[...].astype(F32), small_ref[1:2, :], small_ref[4:5, :])
    cqg = side_by_side(cqg_refs)
    acc[1] += nn(y.astype(BF).T, cqg)
    dx, dg, db = norm_pull(nt(cqg, w[1]), normed, inv, small_ref[1:2, :])
    gs_ref[0:1, :] += dg
    gs_ref[1:2, :] += db
    resid = resid_ref[...].astype(F32) + dx
    resid2_ref[...] = resid.astype(RESID)
    low = resid.astype(BF)
    acc[0] += nn(side_by_side(mixed_refs).T, low)
    smg_ref[...] = nt(low, w[0]).astype(BF)
    enc_t, ckg, cvg = enc_ref[...].T, side_by_side(ckg_refs), side_by_side(cvg_refs)
    acc[2] += nn(enc_t, ckg)
    acc[3] += nn(enc_t, cvg)
    encg_ref[...] = (nt(ckg, w[2]) + nt(cvg, w[3])).astype(BF)

    @pl.when(step == pl.num_programs(0) - 1)
    def _():
        for c in range(4):
            pack_grad(at, acc[c], keep, send, c * r)


def middle_call(at, cross_grads, after, resid, mixed, enc, small, packed):
    rows, shards = after.shape[0], packed.shape[1]
    r, steps = 512 // shards, rows // TR
    er = enc.shape[0] // steps
    half = sds((2, shards, 4 * r, 128), BF)
    cqg, ckg, cvg = zip(*cross_grads)
    return row_call(
        functools.partial(middle_kernel, len(mixed), len(cqg)), "between_attentions", at,
        (after, resid, enc, small) + (packed,) * 4 + tuple(mixed) + cqg + ckg + cvg,
        [row_spec(512)] * 2 + [row_spec(512, er), full_spec(small.shape)] + [part_spec(packed, c, r) for c in range(4)]
        + [row_spec(m.shape[1]) for m in (*mixed, *cqg)] + [row_spec(m.shape[1], er) for m in (*ckg, *cvg)],
        (sds((rows, 512), RESID), sds((rows, 512), BF), sds(enc.shape, BF), half, half, sds((8, 512), F32)),
        [row_spec(512), row_spec(512), row_spec(512, er)] + [full_spec(half.shape)] * 2 + [full_spec((8, 512))],
        [pltpu.VMEM((4, 512, 512), BF), pltpu.VMEM((4, 512, 512), F32)], steps, rows * 512 * 512 * 12)


def last_grads_kernel(per_tree, chunks, at, tok_ref, small_ref, *refs):
    grads, outs, acc = [refs[n * chunks:(n + 1) * chunks] for n in range(3)], refs[3 * chunks:-1], refs[-1]
    step = pl.program_id(0)

    @pl.when(step == 0)
    def _():
        clear(acc)

    y, _, _ = norm_rows(start_rows(tok_ref, small_ref, per_tree), small_ref[0:1, :], small_ref[3:4, :])
    x_t = y.astype(BF).T
    for c in range(3):
        acc[c] += nn(x_t, side_by_side(grads[c]))

    @pl.when(step == pl.num_programs(0) - 1)
    def _():
        shards = outs[0].shape[0]
        r = 512 // shards
        for rep in range(4):
            @pl.when(at[1] * 2 + at[0] == rep)
            def _(rep=rep):
                for q in range(4):
                    for c in range(3):
                        outs[q ^ rep][:, c * r:(c + 1) * r, :] = acc[c, :, q * 128:(q + 1) * 128].astype(BF).reshape(shards, r, 128)


def last_grads_call(at, tokens, self_grads, small, shards, per_tree):
    rows, r = tokens.shape[0], 512 // shards
    qg, kg, vg = zip(*self_grads)
    outs = (sds((shards, 3 * r, 128), BF),) * 4
    return row_call(
        functools.partial(last_grads_kernel, per_tree, len(qg)), "qkv_grads", at, (tokens, small) + qg + kg + vg,
        [row_spec(512), full_spec(small.shape)] + [row_spec(m.shape[1]) for m in (*qg, *kg, *vg)],
        outs, [full_spec(o.shape) for o in outs], [pltpu.VMEM((3, 512, 512), F32)], rows // TR, rows * 512 * 1536 * 2)


def pack_small_grads(at, step_ref, sums, gs2, gs3, trees, rows, piece, extra):
    shards = extra.shape[0]
    wide = 512 // shards
    lane = lax.broadcasted_iota(jnp.int32, (1, 128), 1)
    clear(rows)
    for row, ref, src in ((0, sums, 0), (1, gs2, 0), (2, gs3, 0), (3, sums, 1), (4, gs2, 1), (5, gs3, 1), (10, gs3, 6)):
        rows[row:row + 1, :] = ref[src:src + 1, :]
    for t in range(trees):
        rows[pl.ds(TABLE + step_ref[t], 1), :] += sums[2 + t:3 + t, :]
    turn = lambda value, by: pltpu.roll(value, by % 128, 1) if by % 128 else value
    for j in range(shards):
        at_lane = j * wide
        lanes, off = slice(at_lane // 128 * 128, at_lane // 128 * 128 + 128), at_lane % 128
        low, high = turn(rows[:SMALL, lanes], -off), turn(rows[SMALL:, lanes], 64 - off)
        piece[...] = jnp.where(lane < wide, low, jnp.where((lane >= 64) & (lane < 64 + wide), high, 0.0))
        for a in range(4):
            row, col = divmod((j * 4 + a) * wide, 512)
            value = turn(gs3[2 + row:3 + row, col // 128 * 128:col // 128 * 128 + 128], -(col % 128))
            piece[6 + a:7 + a, :] = jnp.where(lane < wide, value, piece[6 + a:7 + a, :])
        extra[j] = piece[...].astype(BF)


def last_kernel(per_tree, trees, chunks, at, step_ref, tok_ref, resid_ref, small_ref, gs2, gs3, wq, wk, wv, *refs):
    grads = [refs[n * chunks:(n + 1) * chunks] for n in range(3)]
    tokg_ref, extra, w, sums, rows, piece = refs[3 * chunks:]
    step = pl.program_id(0)

    @pl.when(step == 0)
    def _():
        clear(sums)
        for c, ref in enumerate((wq, wk, wv)):
            place_weight(at, True, ref, w.at[c])

    _, normed, inv = norm_rows(start_rows(tok_ref, small_ref, per_tree), small_ref[0:1, :], small_ref[3:4, :])
    back = sum(nt(side_by_side(grads[c]), w[c]) for c in range(3))
    dx, dg, db = norm_pull(back, normed, inv, small_ref[0:1, :])
    sums[0:1, :] += dg
    sums[1:2, :] += db
    resid = resid_ref[...].astype(F32) + dx
    tokg_ref[...] = resid.astype(BF)
    sums[pl.ds(2 + step // per_tree, 1), :] += jnp.sum(resid, 0, keepdims=True)

    @pl.when(step == pl.num_programs(0) - 1)
    def _():
        pack_small_grads(at, step_ref, sums, gs2, gs3, trees, rows, piece, extra)


def last_call(at, timesteps, tokens, self_grads, resid, small, small2, small3, packed, per_tree):
    rows, shards, trees = tokens.shape[0], packed.shape[1], timesteps.shape[0]
    r = 512 // shards
    qg, kg, vg = zip(*self_grads)
    extra = sds((shards, SMALL, 128), BF)
    lines = 8 * -(-(2 + trees) // 8)
    return row_call(
        functools.partial(last_kernel, per_tree, trees, len(qg)), "first_norm_back", at,
        (timesteps, tokens, resid, small, small2, small3) + (packed,) * 3 + qg + kg + vg,
        [pl.BlockSpec(memory_space=pltpu.SMEM)] + [row_spec(512)] * 2 + [full_spec(a.shape) for a in (small, small2, small3)]
        + [part_spec(packed, c, r) for c in range(3)] + [row_spec(m.shape[1]) for m in (*qg, *kg, *vg)],
        (sds((rows, 512), BF), extra), [row_spec(512), full_spec(extra.shape)],
        [pltpu.VMEM((3, 512, 512), BF), pltpu.VMEM((lines, 512), F32), pltpu.VMEM((2 * SMALL, 512), F32), pltpu.VMEM((SMALL, 128), F32)],
        rows // TR, rows * 512 * 1536 * 2)


def finish_kernel(parts, steps, at, p0, p1, p2, p3, *outs):
    pieces = (p0, p1, p2, p3)
    if steps:
        row = p0.shape[0] - SMALL
        *outs, gain, bias, in_bias, out_bias, table, total = outs
        wide, split = gain.shape[1], SMALL - TABLE
        total[...] = sum(ref[row:, :].astype(F32) for ref in pieces)
        for at_row, out in ((0, gain), (3, bias), (10, out_bias)):
            out[...] = total[at_row:at_row + out.shape[0], :wide]
        each = min(128 // wide, 4)
        for n in range(4 // each):
            joined = join_lanes([total[6 + n * each + k:7 + n * each + k, :] for k in range(each)], wide)
            in_bias[:, n * each * wide:(n + 1) * each * wide] = joined[:, :each * wide]
        table[:split, :] = total[TABLE:, :wide]
        table[split:, :] = pltpu.roll(total[...], 64, 1)[:steps - split, :wide]
    for k, ref in enumerate(pieces):
        lanes = pl.multiple_of((k ^ (at[1] * 2 + at[0])) * 128, 128)
        row = 0
        for out, (rows, blocks) in zip(outs, parts):
            for c in range(blocks):
                out[:, pl.ds(c * 512 + lanes, 128)] = ref[row:row + rows, :].astype(F32)
                row += rows


def finish(at, piece, others, parts, wide=0, steps=0):
    shapes = [(rows, blocks * 512) for rows, blocks in parts]
    if steps:
        shapes += [(3, wide), (3, wide), (1, 4 * wide), (1, wide), (steps, wide)]
    outs = tuple(sds(s, F32) for s in shapes)
    return row_call(
        functools.partial(finish_kernel, parts, steps), "finish_grads", at, (piece, *others),
        [full_spec(piece.shape)] * 4, outs, [full_spec(s) for s in shapes],
        [pltpu.VMEM((SMALL, 128), F32)] if steps else [], 1, 0)


def swap(value, axis, count, bit):
    return lax.ppermute(value, axis, [(i, i ^ bit) for i in range(count)])


def tie(value, *first):
    return lax.optimization_barrier((value, *first))[0]


def double(held, axis, count, bit):
    return jnp.concatenate([held, swap(held, axis, count, bit)])


def spread(held, shards, bits):
    flips = [0]
    for bit in bits:
        flips = flips + [f ^ bit for f in flips]
    return jnp.concatenate([held if f == 0 else swap(held, "shard", shards, f) for f in flips])


def add_low(a, *others):
    return sum((v.astype(F32) for v in others), a.astype(F32)).astype(BF)


def landed(done, got, adds):
    done, got = lax.optimization_barrier((done, got))
    return lax.optimization_barrier((done, adds(got)))


def per_device(shards, tokens, encoder, timesteps, seg_starts, out_grad, time_table, norm_gain, norm_bias, self_qkv,
               self_out, cross_query, cross_kv, cross_out, ffn_in, ffn_in_bias, ffn_out, ffn_out_bias):
    trees, count, width = tokens.shape
    per_tree, r, steps = count // TR, width // shards, time_table.shape[0]
    rep, mine = lax.axis_index("rep"), lax.axis_index("shard")
    at = jnp.stack([rep & 1, rep >> 1, flip_bits(mine, shards.bit_length() - 1)]).astype(jnp.int32)
    tok, enc, g = tokens.reshape(-1, width), encoder.reshape(-1, width), out_grad.reshape(-1, width)
    piece1, piece2, piece3 = pack_call(
        at, self_qkv, self_out, cross_query, cross_kv, cross_out, ffn_in, ffn_out, norm_gain, norm_bias,
        ffn_in_bias.reshape(1, 4 * r), ffn_out_bias.reshape(1, r), time_table)

    high = [1 << b for b in range(shards.bit_length() - 2, 0, -1)]
    held = spread(piece1[None], shards, high)
    held, piece2 = lax.optimization_barrier((held, piece2))
    held, held2 = lax.optimization_barrier((double(held, "shard", shards, 1), spread(piece2[None], shards, high)))
    packed3 = lax.all_gather(tie(piece3, held), ("rep", "shard"), axis=0).reshape(4, shards, *piece3.shape)
    packed1 = double(held, "rep", 4, 1).reshape(2, shards, *piece1.shape)
    held2 = double(tie(held2, packed1), "shard", shards, 1)

    (qkv, barred, own, small), held2 = lax.optimization_barrier(
        (first_call(at, seg_starts, timesteps, tok, packed1, per_tree), held2))
    held2 = double(held2, "rep", 4, 2)
    attend = lambda x, pairs: attend_forward(x, x, x, (0, 4, 8), pairs, trees, qm=barred, ko=own)
    (first, qkv), held2 = lax.optimization_barrier(((attend(qkv, (0, 2)), qkv), held2))
    packed2 = double(held2, "rep", 4, 1).reshape(4, shards, *piece2.shape)
    second = attend(qkv, (2, 4))
    self_mixed, self_ext = zip(first, second)
    after_self, cq, ckv = second_call(at, tok, small, self_mixed, enc, packed2, per_tree)
    cross_mixed, cross_ext = attend_forward(cq, ckv, ckv, (0, 0, 4), (0, 4), trees)
    out, resid, cross_back, keep3, send3, small3 = ffn_call(at, after_self, cross_mixed, g, small, packed3)

    exchange = lambda v: lax.all_to_all(v, "shard", split_axis=0, concat_axis=0, tiled=True)
    sum_over = lambda v: jnp.sum(v.astype(F32), 0).astype(BF)
    halves = lambda keep: lambda got: (add_low(keep[0], got[0]), add_low(keep[1], got[1]))
    replicas = lambda v: [swap(v, "rep", 4, k) for k in (1, 2, 3)]
    got3 = swap(send3, "rep", 4, 1)
    cross = functools.partial(attend_backward, cq, ckv, ckv, cross_back, cross_mixed, cross_ext, (0, 0, 4))
    (cross_low, cross_back), (mine3, other3) = landed((cross((0, 2), trees), cross_back), got3, halves(keep3))
    got3 = swap(other3, "rep", 4, 2)
    cross_high = attend_backward(cq, ckv, ckv, cross_back, cross_mixed, cross_ext, (0, 0, 4), (2, 4), trees)
    resid, self_back, enc_grad, keep2, send2, small2 = middle_call(
        at, (cross_low, cross_high), after_self, resid, self_mixed, enc, small, packed2)
    (self_back, send2), mine3 = landed((self_back, send2), got3, lambda got: add_low(mine3, got))
    got3, got2 = exchange(mine3), swap(send2, "rep", 4, 1)
    back = lambda grad, pair, part: attend_backward(
        qkv, qkv, qkv, grad, self_mixed[part], self_ext[part], (0, 4, 8), pair, trees, ko=own, mixed_from=2 * part)
    (first, self_back), (mine2, other2) = landed((back(self_back, (0, 1), 0), self_back), got2, halves(keep2))
    got2 = swap(other2, "rep", 4, 2)
    (second, self_back), mine2 = landed((back(self_back, (1, 2), 0), self_back), got2, lambda got: add_low(mine2, got))
    (third, self_back), done3 = landed((back(self_back, (2, 3), 1), self_back), got3, sum_over)
    others3, got2 = replicas(done3), exchange(mine2)
    self_grads = (first, second, third, back(self_back, (3, 4), 1))
    keep1, *sends1 = last_grads_call(at, tok, self_grads, small, shards, per_tree)
    (sends1, others3), done2 = landed((sends1, others3), got2, sum_over)
    got1 = [swap(v, "rep", 4, k) for k, v in zip((1, 2, 3), sends1)]
    tok_grad, extra = last_call(
        at, timesteps, tok, tie(self_grads, done2), resid, small, small2, small3, packed1, per_tree)
    (tok_grad, extra, done2), mine1 = landed((tok_grad, extra, done2), got1, lambda got: add_low(keep1, *got))
    others2, got1 = replicas(done2), exchange(jnp.concatenate([mine1, extra], 1))
    ffn_grads = finish(at, done3, others3, ((r, 4), (4 * r, 1), (r, 1)))
    cross_grads = finish(at, done2, others2, ((r, 1), (r, 1), (r, 2)))
    ((ffn_in_grad, ffn_out_grad, cross_out_grad), (self_out_grad, cross_query_grad, cross_kv_grad)), done1 = landed(
        (ffn_grads, cross_grads), got1, sum_over)
    self_qkv_grad, gain_grad, bias_grad, in_bias_grad, out_bias_grad, table_grad = finish(
        at, done1, replicas(done1), ((r, 3),), r, steps)
    return (
        out.reshape(tokens.shape), tok_grad.reshape(tokens.shape), enc_grad.reshape(encoder.shape),
        table_grad, gain_grad, bias_grad, self_qkv_grad, self_out_grad, cross_query_grad, cross_kv_grad,
        cross_out_grad, ffn_in_grad, in_bias_grad.reshape(-1), ffn_out_grad, out_bias_grad.reshape(-1),
    )


def solution(mesh):
    trees = P(("rep", "shard"), None, None)
    rows, columns, flat = P("shard", None), P(None, "shard"), P("shard")
    in_specs = (trees, trees, P(("rep", "shard")), P(("rep", "shard"), None), trees, columns, columns, columns,
                rows, rows, rows, rows, rows, rows, flat, rows, flat)
    out_specs = (trees, trees, trees, columns, columns, columns, rows, rows, rows, rows, rows, rows, flat, rows, flat)
    return jax.shard_map(
        functools.partial(per_device, mesh.shape["shard"]), mesh=mesh, in_specs=in_specs, out_specs=out_specs,
        check_vma=False)
```

```python
import functools

import jax
import jax.numpy as jnp
from jax import lax
from jax.experimental import pallas as pl
from jax.experimental.pallas import tpu as pltpu
from jax.sharding import PartitionSpec as P

BF = jnp.bfloat16
F32 = jnp.float32


def nt(a, b):
    return lax.dot_general(a, b, (((1,), (1,)), ((), ())), preferred_element_type=F32)


def nn(a, b):
    return jnp.dot(a, b, preferred_element_type=F32)


def cost(flops, moved, exps=0):
    return pl.CostEstimate(flops=int(flops), bytes_accessed=int(moved), transcendentals=int(exps))


def kernel_params(axes):
    return pltpu.CompilerParams(vmem_limit_bytes=58 << 20, dimension_semantics=("arbitrary",) * axes)


def split3(x):
    hi = x.astype(BF)
    rest = x - hi.astype(F32)
    mid = rest.astype(BF)
    return hi, mid, (rest - mid.astype(F32)).astype(BF)


def place3(sub, parts, base):
    hi, mid, lo = parts
    return jnp.where(sub == 13, hi, jnp.where(sub == 14, mid, jnp.where(sub == 15, lo, base)))


def forward_tiles(masked, qlen, klen, tile):
    if not masked:
        return [(i, i + tile, klen) for i in range(0, qlen, tile)]
    trunk, segment = qlen - 12 * (qlen // 32), 2 * (qlen // 32)
    cuts = [0, qlen // 2, qlen]
    ends = [min(qlen, -(-max(trunk, b + segment - 1) // 128) * 128) for b in cuts[1:]]
    return list(zip(cuts[:-1], cuts[1:], ends))


def attend_forward_kernel(masked, tile, *refs):
    if masked:
        q_ref, k_ref, v_ref, qm_ref, ko_ref = refs[:5]
    else:
        q_ref, k_ref, v_ref = refs[:3]
    o_ref, ext_ref = refs[-2:]
    lane = lax.broadcasted_iota(jnp.int32, (1, 128), 1)
    first, sub = lane < 64, lane & 63
    zero, one = jnp.zeros((1, 128), BF), jnp.ones((1, 128), BF)
    k, v = k_ref[...], v_ref[...]
    other = ko_ref[...] if masked else zero
    keys = (jnp.where(first, k, other), jnp.where(first, other, k))
    vals = (jnp.where(first, v, one), jnp.where(first, one, v))
    def scores(low, high, count, h):
        q = q_ref[low:high, :] * jnp.asarray(0.125, BF)
        qm = qm_ref[low:high, :] if masked else zero
        return nt(jnp.where(first, q, qm) if h == 0 else jnp.where(first, qm, q), keys[h][:count])

    work = [(*tile, h) for tile in forward_tiles(masked, q_ref.shape[0], k_ref.shape[0], tile) for h in range(2)]
    ahead = scores(*work[0])
    for n, (low, high, count, h) in enumerate(work):
        s = ahead
        if n + 1 < len(work):
            ahead = scores(*work[n + 1])
        peak = jnp.max(s, axis=1, keepdims=True)
        out = nn(jnp.exp(s - peak).astype(BF), vals[h][:count])
        if h == 0:
            kept = out, peak
            continue
        rows = pl.ds(low, high - low)
        sums = jnp.where(first, out, kept[0])
        o_ref[rows, :] = (jnp.where(first, kept[0], out) / pltpu.roll(sums, 64, 1)).astype(BF)
        logsum = jnp.where(first, peak, kept[1]) + jnp.log(sums)
        ext_ref[rows, :] = place3(sub, split3(-logsum), qm_ref[rows, :] if masked else zero)


def attend_forward(q, k, v, cols, pairs, trees, qm=None, ko=None, tile=1024):
    qlen, klen = q.shape[0] // trees, k.shape[0] // trees
    tile = min(tile, qlen)
    low, count = pairs[0], pairs[1] - pairs[0]
    at = lambda n, c: pl.BlockSpec((n, 128), lambda t, h: (t, c + h))
    specs = [at(qlen, cols[0] + low), at(klen, cols[1] + low), at(klen, cols[2] + low)]
    args = [q, k, v]
    if qm is not None:
        specs += [pl.BlockSpec((qlen, 128), lambda t, h: (t, 0)), pl.BlockSpec((klen, 128), lambda t, h: (t, 0))]
        args += [qm, ko]
    shape = jax.ShapeDtypeStruct((trees * qlen, count * 128), BF)
    return pl.pallas_call(
        functools.partial(attend_forward_kernel, qm is not None, tile),
        grid=(trees, count), in_specs=specs, out_specs=[at(qlen, 0)] * 2, out_shape=[shape] * 2,
        compiler_params=kernel_params(2), name="attend_forward",
        cost_estimate=cost(trees * count * qlen * klen * 2000, trees * count * qlen * 1600, trees * count * 2 * qlen * klen),
    )(*args)


def backward_tiles(masked, qlen, klen, tq, tk):
    if not masked:
        return [(j, j + tk, [(i, i + tq) for i in range(0, qlen, tq)]) for j in range(0, klen, tk)]
    trunk, segment = qlen - 12 * (qlen // 32), 2 * (qlen // 32)
    steps = []
    for low, high in [(0, trunk), (trunk, qlen)]:
        start = 0 if low < trunk else (low - segment + 1) // 64 * 64
        spans = [start] + [c for c in range(tq, qlen, tq) if c > start + 128] + [qlen]
        steps.append((low, high, list(zip(spans[:-1], spans[1:]))))
    return steps


def attend_backward_kernel(masked, tq, tk, *refs):
    if masked:
        q_ref, k_ref, v_ref, do_ref, o_ref, ext_ref, ko_ref = refs[:7]
    else:
        q_ref, k_ref, v_ref, do_ref, o_ref, ext_ref = refs[:6]
    dq_ref, dk_ref, dv_ref, qa, qz, da, dz, kt, dqt = refs[-9:]
    lane = lax.broadcasted_iota(jnp.int32, (1, 128), 1)
    first, sub = lane < 64, lane & 63
    zero = jnp.zeros((1, 128), BF)
    ones = jnp.where((sub >= 13) & (sub < 16), jnp.ones((1, 128), BF), zero)
    q = q_ref[...] * jnp.asarray(0.125, BF)
    ext, do = ext_ref[...], do_ref[...]
    prod = do.astype(F32) * o_ref[...].astype(F32)
    for h in range(2):
        mine = first if h == 0 else ~first
        delta = jnp.sum(jnp.where(mine, prod, 0.0), axis=1, keepdims=True)
        parts = place3(sub, split3(jnp.broadcast_to(-delta, prod.shape)), zero)
        qa[h] = jnp.where(mine, q, ext)
        qz[h] = jnp.where(mine, q, zero)
        da[h] = jnp.where(mine, do, parts)
        dz[h] = jnp.where(mine, do, zero)
    kt[...] = k_ref[...].T
    dqt[...] = jnp.zeros_like(dqt)
    def products(k_low, k_high, q_low, q_high, h):
        mine = first if h == 0 else ~first
        k, v = k_ref[k_low:k_high, :], v_ref[k_low:k_high, :]
        other = ko_ref[k_low:k_high, :] if masked else ones
        return (nt(jnp.where(mine, k, other), qa[h, q_low:q_high, :]),
                nt(jnp.where(mine, v, ones), da[h, q_low:q_high, :]))

    work = [(k_low, k_high, q_low, q_high, h)
            for k_low, k_high, spans in backward_tiles(masked, q_ref.shape[0], k_ref.shape[0], tq, tk)
            for q_low, q_high in spans for h in range(2)]
    ahead = products(*work[0])
    for n, (k_low, k_high, q_low, q_high, h) in enumerate(work):
        scores, centred = ahead
        if n + 1 < len(work):
            ahead = products(*work[n + 1])
        if n == 0 or k_low != work[n - 1][0]:
            dk = jnp.zeros((k_high - k_low, 128), F32)
            dv = jnp.zeros((k_high - k_low, 128), F32)
        probs = jnp.exp(scores)
        ds = (probs * centred).astype(BF)
        dv = dv + nn(probs.astype(BF), dz[h, q_low:q_high, :])
        dk = dk + nn(ds, qz[h, q_low:q_high, :])
        dqt[64 * h:64 * h + 64, q_low:q_high] += nn(kt[64 * h:64 * h + 64, k_low:k_high], ds)
        if n + 1 == len(work) or k_low != work[n + 1][0]:
            dk_ref[k_low:k_high, :] = dk.astype(BF)
            dv_ref[k_low:k_high, :] = dv.astype(BF)

    dq_ref[...] = (dqt[...].T * 0.125).astype(BF)


def attend_backward(q, k, v, do, o, ext, cols, pairs, trees, ko=None, mixed_from=0, tq=256, tk=512):
    qlen, klen = q.shape[0] // trees, k.shape[0] // trees
    tq, tk = min(tq, qlen), min(tk, klen)
    low, count = pairs[0], pairs[1] - pairs[0]
    at = lambda n, c: pl.BlockSpec((n, 128), lambda t, h: (t, c + h))
    specs = [at(qlen, cols[0] + low), at(klen, cols[1] + low), at(klen, cols[2] + low), at(qlen, low)]
    specs += [at(qlen, low - mixed_from)] * 2
    args = [q, k, v, do, o, ext]
    if ko is not None:
        specs += [pl.BlockSpec((klen, 128), lambda t, h: (t, 0))]
        args += [ko]
    return pl.pallas_call(
        functools.partial(attend_backward_kernel, ko is not None, tq, tk),
        grid=(trees, count), in_specs=specs, out_specs=[at(qlen, 0), at(klen, 0), at(klen, 0)],
        out_shape=[jax.ShapeDtypeStruct((trees * n, count * 128), BF) for n in (qlen, klen, klen)],
        scratch_shapes=[pltpu.VMEM((2, qlen, 128), BF)] * 4 + [pltpu.VMEM((128, klen), BF), pltpu.VMEM((128, qlen), F32)],
        compiler_params=kernel_params(2), name="attend_backward",
        cost_estimate=cost(trees * count * qlen * klen * 4000, trees * count * qlen * 2500, trees * count * 2 * qlen * klen),
    )(*args)


def self_backward_kernel(trees, tq, tk, at, *refs):
    xt_ref, dw_ref, acc = refs[7], refs[11], refs[-1]
    dq_ref, dk_ref, dv_ref = refs[8:11]
    attend_backward_kernel(True, tq, tk, *refs[:7], dq_ref, dk_ref, dv_ref, *refs[12:-1])
    term = nn(xt_ref[...], jnp.concatenate([dq_ref[...], dk_ref[...], dv_ref[...]], 1))
    step = pl.program_id(0)

    @pl.when(step == 0)
    def _():
        acc[...] = term

    @pl.when(step > 0)
    def _():
        acc[...] += term

    @pl.when(step == trees - 1)
    def _():
        shards = dw_ref.shape[0]
        r = 512 // shards
        for c in range(3):
            dw_ref[:, c * r:(c + 1) * r, :] = acc[:, c * 128:(c + 1) * 128].astype(BF).reshape(shards, r, 128)


def self_backward(at, qkv, do, o, ext, own, x_t, flip, shards, trees, tq=256, tk=512):
    rows = qkv.shape[0] // trees
    pair = lambda at: (at[1] * 2 + at[0]) ^ flip
    block = lambda c: pl.BlockSpec((rows, 128), lambda t, at: (t, c + pair(at)))
    plain = pl.BlockSpec((rows, 128), lambda t, at: (t, 0))
    piece = jax.ShapeDtypeStruct((shards, 3 * (512 // shards), 128), BF)
    *grads, dw = pl.pallas_call(
        functools.partial(self_backward_kernel, trees, tq, tk),
        grid_spec=pltpu.PrefetchScalarGridSpec(
            num_scalar_prefetch=1, grid=(trees,),
            in_specs=[block(0), block(4), block(8), block(0), block(0), block(0), plain,
                      pl.BlockSpec((512, rows), lambda t, at: (0, t))],
            out_specs=[plain] * 3 + [pl.BlockSpec(piece.shape, lambda t, at: (0, 0, 0))],
            scratch_shapes=[pltpu.VMEM((2, rows, 128), BF)] * 4 + [
                pltpu.VMEM((128, rows), BF), pltpu.VMEM((128, rows), F32), pltpu.VMEM((512, 384), F32)]),
        out_shape=[jax.ShapeDtypeStruct((trees * rows, 128), BF)] * 3 + [piece],
        compiler_params=kernel_params(1), name="attend_backward",
        cost_estimate=cost(trees * rows * rows * 4000, trees * rows * 4500, trees * 2 * rows * rows),
    )(at, qkv, qkv, qkv, do, o, ext, own, x_t)
    return tuple(grads), dw


TR = 512
RESID = F32


def norm_rows(h, gain, bias):
    centred = h - jnp.mean(h, -1, keepdims=True)
    inv = lax.rsqrt(jnp.mean(centred * centred, -1, keepdims=True) + 1e-05)
    normed = centred * inv
    return normed * gain + bias, normed, inv


def norm_pull(dy, normed, inv, gain):
    scaled = dy * gain
    along = jnp.mean(scaled * normed, -1, keepdims=True)
    dx = inv * (scaled - jnp.mean(scaled, -1, keepdims=True) - normed * along)
    return dx, jnp.sum(dy * normed, 0, keepdims=True), jnp.sum(dy, 0, keepdims=True)


def row_spec(width, rows=TR):
    return pl.BlockSpec((rows, width), lambda i, at: (i, 0))


def full_spec(shape):
    return pl.BlockSpec(shape, lambda i, at: (0,) * len(shape))


def part_spec(packed, part, rows):
    lead = packed.shape[:-2]
    return pl.BlockSpec((*lead, rows, 128), lambda i, at: (0,) * len(lead) + (part, 0))


def flip_bits(value, count):
    return sum(((value >> b) & 1) << (count - 1 - b) for b in range(count))


def place_weight(at, relative, ref, dst, slots=False):
    shards, rows = ref.shape[1], ref.shape[-2]
    bits = shards.bit_length() - 1
    for q in range(4):
        for j in range(shards):
            if slots:
                piece = ref[q & 1, flip_bits(j, bits) ^ at[2], q >> 1]
            elif relative and len(ref.shape) == 5:
                piece = ref[(q & 1) ^ at[0], flip_bits(j, bits) ^ at[2], (q >> 1) ^ at[1]]
            elif relative:
                piece = ref[q ^ (at[1] * 2 + at[0]), flip_bits(j, bits) ^ at[2]]
            else:
                piece = ref[q, j]
            dst[j * rows:(j + 1) * rows, q * 128:(q + 1) * 128] = piece


def pack_grad(at, acc, keep, send, offset):
    shards = keep.shape[1]
    rows = acc.shape[0] // shards
    for q in range(4):
        piece = acc[:, q * 128:(q + 1) * 128].astype(BF).reshape(shards, rows, 128)
        for core in range(2):
            @pl.when(at[0] == core)
            def _(q=q, core=core, piece=piece):
                (keep if (q & 1) == core else send)[(q >> 1) ^ at[1], :, offset:offset + rows, :] = piece


def start_rows(tok_ref, small_ref, per_tree):
    tree = pl.program_id(0) // per_tree
    return tok_ref[...].astype(F32) + small_ref[pl.ds(11 + tree, 1), :]


def side_by_side(refs):
    return jnp.concatenate([ref[...] for ref in refs], 1) if len(refs) > 1 else refs[0][...]


def clear(*refs):
    for ref in refs:
        ref[...] = jnp.zeros_like(ref)


def gelu_both(x):
    k = 0.7978845608028654
    x2 = x * x
    t = jnp.tanh(k * x * (1.0 + 0.044715 * x2))
    half = 0.5 * (1.0 + t)
    return x * half, half + 0.5 * x * (1.0 - t * t) * (k + (3 * 0.044715 * k) * x2)


def row_call(kernel, name, at, args, specs, outs, out_specs, scratch, steps, flops):
    moved = sum(a.size * a.dtype.itemsize for a in (*args, *outs))
    return pl.pallas_call(
        kernel,
        grid_spec=pltpu.PrefetchScalarGridSpec(
            num_scalar_prefetch=1, grid=(steps,), in_specs=specs, out_specs=out_specs, scratch_shapes=scratch),
        out_shape=outs, compiler_params=kernel_params(1), name=name, cost_estimate=cost(flops, moved),
    )(at, *args)


def sds(shape, dtype):
    return jax.ShapeDtypeStruct(shape, dtype)


def token_rows(starts, first_position, rows):
    position = lax.broadcasted_iota(jnp.int32, (rows, 128), 0) + first_position
    sub = lax.broadcasted_iota(jnp.int32, (rows, 128), 1) & 63
    seg = jnp.zeros((rows, 128), jnp.int32)
    for j in range(1, 13):
        seg = seg + (position >= starts(j)).astype(jnp.int32)
    parent = jnp.where(seg >= 5, 1 + ((seg - 5) >> 1), 0)
    seen = (sub == seg) | (sub == 0) | (sub == parent) | (sub >= 13)
    own = (sub == seg) | ((sub >= 13) & (sub < 16))
    return jnp.where(seen, 0.0, -1e30).astype(BF), jnp.where(own, 1.0, 0.0).astype(BF)


SMALL = 32
TABLE = 11


def pack_kernel(at, qkv, so, cq, ckv, co, fi, fo, gain, bias, in_bias, out_bias, table, p1, p2, p3, scratch):
    for out, flip, weights in ((p1.at[0], 0, (qkv,)), (p1.at[1], 2, (qkv,)), (p2, 0, (so, cq, ckv)), (p3, 0, (fi, fo, co))):
        lanes = pl.multiple_of(((at[1] * 2 + at[0]) ^ flip) * 128, 128)
        row = 0
        for ref in weights:
            for c in range(ref.shape[1] // 512):
                out[row:row + ref.shape[0], :] = ref[:, pl.ds(c * 512 + lanes, 128)]
                row += ref.shape[0]
    wide, steps, split = gain.shape[1], table.shape[0], SMALL - TABLE
    clear(scratch)
    for row, ref in ((0, gain), (3, bias)):
        scratch[row:row + ref.shape[0], :wide] = ref[...].astype(F32)
    flat = in_bias[...].astype(F32).reshape(1, 4 * wide)
    for a in range(4):
        scratch[6 + a:7 + a, :wide] = flat[:, a * wide:(a + 1) * wide]
    scratch[10:11, :wide] = out_bias[...].astype(F32).reshape(1, wide)
    scratch[TABLE:, :wide] = table[:split, :].astype(F32)
    scratch[:steps - split, 64:64 + wide] = table[split:, :].astype(F32)
    for half in range(2):
        p1[half, p1.shape[1] - SMALL:, :] = scratch[...].astype(BF)


def small_row(r):
    return -(-3 * r // SMALL) * SMALL


def pack_call(at, *args):
    r = args[0].shape[0]
    outs = (sds((2, small_row(r) + SMALL, 128), BF), sds((4 * r, 128), BF), sds((9 * r, 128), BF))
    return row_call(pack_kernel, "pack_quarters", at, args, [full_spec(a.shape) for a in args], outs,
                    [full_spec(o.shape) for o in outs], [pltpu.VMEM((SMALL, 128), F32)], 1, 0)


def join_lanes(pieces, wide):
    lane = lax.broadcasted_iota(jnp.int32, (1, 128), 1)
    out = pieces[0]
    for k, piece in enumerate(pieces[1:], 1):
        out = jnp.where(lane >= wide * k, pltpu.roll(piece, wide * k, 1), out)
    return out


def unpack_small(at, step_ref, ref, shards, trees, small, rows):
    wide, bits = 512 // shards, shards.bit_length() - 1
    each = 128 // wide
    pieces = [ref[0, flip_bits(j, bits) ^ at[2], 0].astype(F32) for j in range(shards)]
    turned = [pltpu.roll(p, 64, 1) for p in pieces]
    clear(small)
    for g in range(4):
        lanes = slice(g * 128, g * 128 + 128)
        rows[:SMALL, lanes] = join_lanes(pieces[g * each:(g + 1) * each], wide)
        rows[SMALL:, lanes] = join_lanes(turned[g * each:(g + 1) * each], wide)
    for n in range(16):
        parts = [divmod(n * each + k, 4) for k in range(each)]
        small[6 + n // 4:7 + n // 4, n % 4 * 128:n % 4 * 128 + 128] = join_lanes(
            [pieces[j][6 + a:7 + a, :] for j, a in parts], wide)
    small[0:6, :] = rows[0:6, :]
    small[10:11, :] = rows[10:11, :]
    for t in range(trees):
        small[TABLE + t:TABLE + t + 1, :] = rows[pl.ds(TABLE + step_ref[t], 1), :]


def first_kernel(shards, trees, per_tree, at, seg_ref, step_ref, tok_ref, held_ref, wq, wk, wv,
                 qkv_ref, barred_ref, own_ref, small_ref, xt_ref, w, small, rows):
    step = pl.program_id(0)

    @pl.when(step == 0)
    def _():
        for c, ref in enumerate((wq, wk, wv)):
            place_weight(at, True, ref, w.at[c])
        unpack_small(at, step_ref, held_ref, shards, trees, small, rows)
        small_ref[...] = small[...]

    tree = step // per_tree
    barred_ref[...], own_ref[...] = token_rows(lambda j: seg_ref[tree, j], (step % per_tree) * TR, TR)
    x, _, _ = norm_rows(start_rows(tok_ref, small, per_tree), small[0:1, :], small[3:4, :])
    x = x.astype(BF)
    xt_ref[...] = x.T
    for c in range(3):
        qkv_ref[:, c * 512:(c + 1) * 512] = nn(x, w[c]).astype(BF)


def first_call(at, seg_starts, timesteps, tokens, packed, per_tree):
    rows, shards, trees = tokens.shape[0], packed.shape[1], seg_starts.shape[0]
    r = 512 // shards
    held = pl.BlockSpec((1, shards, 1, SMALL, 128), lambda i, at: (0, 0, 0, small_row(r) // SMALL, 0))
    scalars = pl.BlockSpec(memory_space=pltpu.SMEM)
    lines = 16 * -(-(TABLE + trees) // 16)
    return row_call(
        functools.partial(first_kernel, shards, trees, per_tree), "project_qkv", at,
        (seg_starts, timesteps, tokens, packed, packed, packed, packed),
        [scalars, scalars, row_spec(512), held] + [part_spec(packed, c, r) for c in range(3)],
        (sds((rows, 1536), BF), sds((rows, 128), BF), sds((rows, 128), BF), sds((lines, 512), F32), sds((512, rows), BF)),
        [row_spec(1536), row_spec(128), row_spec(128), full_spec((lines, 512)), pl.BlockSpec((512, TR), lambda i, at: (0, i))],
        [pltpu.VMEM((3, 512, 512), BF), pltpu.VMEM((lines, 512), F32), pltpu.VMEM((2 * SMALL, 512), F32)],
        rows // TR, rows * 512 * 1536 * 2)


def second_kernel(per_tree, count, at, tok_ref, small_ref, enc_ref, wo, wq, wk, wv, *refs):
    mixed_refs, (after_ref, cq_ref, ckv_ref, w) = refs[:count], refs[count:]

    @pl.when(pl.program_id(0) == 0)
    def _():
        for c, ref in enumerate((wo, wq, wk, wv)):
            place_weight(at, True, ref, w.at[c])

    h = start_rows(tok_ref, small_ref, per_tree) + nn(side_by_side(mixed_refs), w[0])
    after_ref[...] = h.astype(RESID)
    x, _, _ = norm_rows(h, small_ref[1:2, :], small_ref[4:5, :])
    cq_ref[...] = nn(x.astype(BF), w[1]).astype(BF)
    e = enc_ref[...]
    ckv_ref[:, :512] = nn(e, w[2]).astype(BF)
    ckv_ref[:, 512:] = nn(e, w[3]).astype(BF)


def second_call(at, tokens, small, mixed, enc, packed, per_tree):
    rows, r = tokens.shape[0], 512 // packed.shape[1]
    steps = rows // TR
    er = enc.shape[0] // steps
    return row_call(
        functools.partial(second_kernel, per_tree, len(mixed)), "cross_inputs", at,
        (tokens, small, enc, packed, packed, packed, packed, *mixed),
        [row_spec(512), full_spec(small.shape), row_spec(512, er)] + [part_spec(packed, c, r) for c in range(4)]
        + [row_spec(m.shape[1]) for m in mixed],
        (sds((rows, 512), RESID), sds((rows, 512), BF), sds((enc.shape[0], 1024), BF)),
        [row_spec(512), row_spec(512), row_spec(1024, er)], [pltpu.VMEM((4, 512, 512), BF)], steps, rows * 512 * 1536 * 2)


def ffn_kernel(at, after_ref, mixed_ref, g_ref, small_ref, wi0, wi1, wi2, wi3, wf, wc,
               out_ref, resid_ref, cmg_ref, keep, send, gs_ref, w, wo, aco, afi, afo):
    step = pl.program_id(0)
    r = wc.shape[-2]

    @pl.when(step == 0)
    def _():
        clear(aco, afi, afo, gs_ref)
        for c, ref in enumerate((wi0, wi1, wi2, wi3, wc)):
            place_weight(at, False, ref, w.at[c])
        place_weight(at, False, wf, wo)

    mixed, g = mixed_ref[...], g_ref[...]
    h = after_ref[...].astype(F32) + nn(mixed, w[4])
    y, normed, inv = norm_rows(h, small_ref[2:3, :], small_ref[5:6, :])
    third = y.astype(BF)
    third_t, g_t = third.T, g.T
    out = h + small_ref[10:11, :]
    back = jnp.zeros(h.shape, F32)
    for c in range(4):
        wi, wf_c = w[c], wo[c * 512:(c + 1) * 512, :]
        value, slope = gelu_both(nn(third, wi) + small_ref[6 + c:7 + c, :])
        hidden = value.astype(BF)
        out = out + nn(hidden, wf_c)
        pre_grad = (nt(g, wf_c) * slope).astype(BF)
        gs_ref[2 + c:3 + c, :] += jnp.sum(pre_grad.astype(F32), 0, keepdims=True)
        back = back + nt(pre_grad, wi)
        afi[c] += nn(third_t, pre_grad)
        afo[c] += nn(g_t, hidden)
    out_ref[...] = out.astype(BF)
    g_high = g.astype(F32)
    gs_ref[6:7, :] += jnp.sum(g_high, 0, keepdims=True)
    dx, dg, db = norm_pull(back, normed, inv, small_ref[2:3, :])
    gs_ref[0:1, :] += dg
    gs_ref[1:2, :] += db
    resid = g_high + dx
    resid_ref[...] = resid.astype(RESID)
    low = resid.astype(BF)
    cmg_ref[...] = nt(low, w[4]).astype(BF)
    aco[...] += nn(mixed.T, low)

    @pl.when(step == pl.num_programs(0) - 1)
    def _():
        for c in range(4):
            pack_grad(at, afi[c], keep, send, c * r)
        for c in range(4):
            whole = afo[c].T
            shards = keep.shape[1]
            quarter = shards // 4
            for q in range(4):
                piece = whole[:, q * 128:(q + 1) * 128].astype(BF).reshape(quarter, 4 * r, 128)
                for core in range(2):
                    @pl.when(at[0] == core)
                    def _(q=q, core=core, piece=piece, c=c):
                        (keep if (q & 1) == core else send)[(q >> 1) ^ at[1], c * quarter:(c + 1) * quarter, 4 * r:8 * r, :] = piece
        pack_grad(at, aco[...], keep, send, 8 * r)


def ffn_call(at, after, mixed, g, small, packed):
    rows, shards = after.shape[0], packed.shape[1]
    r = 512 // shards
    half = sds((2, shards, 9 * r, 128), BF)
    return row_call(
        ffn_kernel, "ffn_both_ways", at,
        (after, mixed, g, small) + (packed,) * 6,
        [row_spec(512)] * 3 + [full_spec(small.shape)] + [part_spec(packed, c, r) for c in range(4)]
        + [part_spec(packed, 1, 4 * r), part_spec(packed, 8, r)],
        (sds((rows, 512), BF), sds((rows, 512), RESID), sds((rows, 512), BF), half, half, sds((8, 512), F32)),
        [row_spec(512)] * 3 + [full_spec(half.shape)] * 2 + [full_spec((8, 512))],
        [pltpu.VMEM((5, 512, 512), BF), pltpu.VMEM((2048, 512), BF), pltpu.VMEM((512, 512), F32),
         pltpu.VMEM((4, 512, 512), F32), pltpu.VMEM((4, 512, 512), F32)],
        rows // TR, rows * 512 * 2048 * 12)


def middle_kernel(mixes, chunks, at, after_ref, resid_ref, enc_ref, small_ref, wo, wq, wk, wv, *refs):
    mixed_refs, refs = refs[:mixes], refs[mixes:]
    cqg_refs, ckg_refs, cvg_refs = refs[:chunks], refs[chunks:2 * chunks], refs[2 * chunks:3 * chunks]
    resid2_ref, smg_ref, encg_ref, keep, send, gs_ref, w, acc = refs[3 * chunks:]
    step = pl.program_id(0)
    r = wo.shape[-2]

    @pl.when(step == 0)
    def _():
        clear(acc, gs_ref)
        for c, ref in enumerate((wo, wq, wk, wv)):
            place_weight(at, True, ref, w.at[c])

    y, normed, inv = norm_rows(after_ref[...].astype(F32), small_ref[1:2, :], small_ref[4:5, :])
    cqg = side_by_side(cqg_refs)
    acc[1] += nn(y.astype(BF).T, cqg)
    dx, dg, db = norm_pull(nt(cqg, w[1]), normed, inv, small_ref[1:2, :])
    gs_ref[0:1, :] += dg
    gs_ref[1:2, :] += db
    resid = resid_ref[...].astype(F32) + dx
    resid2_ref[...] = resid.astype(RESID)
    low = resid.astype(BF)
    acc[0] += nn(side_by_side(mixed_refs).T, low)
    smg_ref[...] = nt(low, w[0]).astype(BF)
    enc_t, ckg, cvg = enc_ref[...].T, side_by_side(ckg_refs), side_by_side(cvg_refs)
    acc[2] += nn(enc_t, ckg)
    acc[3] += nn(enc_t, cvg)
    encg_ref[...] = (nt(ckg, w[2]) + nt(cvg, w[3])).astype(BF)

    @pl.when(step == pl.num_programs(0) - 1)
    def _():
        for c in range(4):
            pack_grad(at, acc[c], keep, send, c * r)


def middle_call(at, cross_grads, after, resid, mixed, enc, small, packed):
    rows, shards = after.shape[0], packed.shape[1]
    r, steps = 512 // shards, rows // TR
    er = enc.shape[0] // steps
    half = sds((2, shards, 4 * r, 128), BF)
    cqg, ckg, cvg = zip(*cross_grads)
    return row_call(
        functools.partial(middle_kernel, len(mixed), len(cqg)), "between_attentions", at,
        (after, resid, enc, small) + (packed,) * 4 + tuple(mixed) + cqg + ckg + cvg,
        [row_spec(512)] * 2 + [row_spec(512, er), full_spec(small.shape)] + [part_spec(packed, c, r) for c in range(4)]
        + [row_spec(m.shape[1]) for m in (*mixed, *cqg)] + [row_spec(m.shape[1], er) for m in (*ckg, *cvg)],
        (sds((rows, 512), RESID), sds((rows, 512), BF), sds(enc.shape, BF), half, half, sds((8, 512), F32)),
        [row_spec(512), row_spec(512), row_spec(512, er)] + [full_spec(half.shape)] * 2 + [full_spec((8, 512))],
        [pltpu.VMEM((4, 512, 512), BF), pltpu.VMEM((4, 512, 512), F32)], steps, rows * 512 * 512 * 12)


def pack_small_grads(at, step_ref, sums, gs2, gs3, trees, rows, piece, extra):
    shards = extra.shape[0]
    wide = 512 // shards
    lane = lax.broadcasted_iota(jnp.int32, (1, 128), 1)
    clear(rows)
    for row, ref, src in ((0, sums, 0), (1, gs2, 0), (2, gs3, 0), (3, sums, 1), (4, gs2, 1), (5, gs3, 1), (10, gs3, 6)):
        rows[row:row + 1, :] = ref[src:src + 1, :]
    for t in range(trees):
        rows[pl.ds(TABLE + step_ref[t], 1), :] += sums[2 + t:3 + t, :]
    turn = lambda value, by: pltpu.roll(value, by % 128, 1) if by % 128 else value
    for j in range(shards):
        at_lane = j * wide
        lanes, off = slice(at_lane // 128 * 128, at_lane // 128 * 128 + 128), at_lane % 128
        low, high = turn(rows[:SMALL, lanes], -off), turn(rows[SMALL:, lanes], 64 - off)
        piece[...] = jnp.where(lane < wide, low, jnp.where((lane >= 64) & (lane < 64 + wide), high, 0.0))
        for a in range(4):
            row, col = divmod((j * 4 + a) * wide, 512)
            value = turn(gs3[2 + row:3 + row, col // 128 * 128:col // 128 * 128 + 128], -(col % 128))
            piece[6 + a:7 + a, :] = jnp.where(lane < wide, value, piece[6 + a:7 + a, :])
        extra[j] = piece[...].astype(BF)


def last_kernel(per_tree, trees, chunks, at, step_ref, tok_ref, resid_ref, small_ref, gs2, gs3, wq, wk, wv, *refs):
    grads = [refs[n * chunks:(n + 1) * chunks] for n in range(3)]
    tokg_ref, extra, w, sums, rows, piece = refs[3 * chunks:]
    step = pl.program_id(0)

    @pl.when(step == 0)
    def _():
        clear(sums)
        for c, ref in enumerate((wq, wk, wv)):
            place_weight(at, True, ref, w.at[c], True)

    _, normed, inv = norm_rows(start_rows(tok_ref, small_ref, per_tree), small_ref[0:1, :], small_ref[3:4, :])
    back = sum(nt(side_by_side(grads[c]), w[c]) for c in range(3))
    dx, dg, db = norm_pull(back, normed, inv, small_ref[0:1, :])
    sums[0:1, :] += dg
    sums[1:2, :] += db
    resid = resid_ref[...].astype(F32) + dx
    tokg_ref[...] = resid.astype(BF)
    sums[pl.ds(2 + step // per_tree, 1), :] += jnp.sum(resid, 0, keepdims=True)

    @pl.when(step == pl.num_programs(0) - 1)
    def _():
        pack_small_grads(at, step_ref, sums, gs2, gs3, trees, rows, piece, extra)


def last_call(at, timesteps, tokens, self_grads, resid, small, small2, small3, packed, per_tree):
    rows, shards, trees = tokens.shape[0], packed.shape[1], timesteps.shape[0]
    r = 512 // shards
    qg, kg, vg = zip(*self_grads)
    extra = sds((shards, SMALL, 128), BF)
    lines = 8 * -(-(2 + trees) // 8)
    return row_call(
        functools.partial(last_kernel, per_tree, trees, len(qg)), "first_norm_back", at,
        (timesteps, tokens, resid, small, small2, small3) + (packed,) * 3 + qg + kg + vg,
        [pl.BlockSpec(memory_space=pltpu.SMEM)] + [row_spec(512)] * 2 + [full_spec(a.shape) for a in (small, small2, small3)]
        + [part_spec(packed, c, r) for c in range(3)] + [row_spec(m.shape[1]) for m in (*qg, *kg, *vg)],
        (sds((rows, 512), BF), extra), [row_spec(512), full_spec(extra.shape)],
        [pltpu.VMEM((3, 512, 512), BF), pltpu.VMEM((lines, 512), F32), pltpu.VMEM((2 * SMALL, 512), F32), pltpu.VMEM((SMALL, 128), F32)],
        rows // TR, rows * 512 * 1536 * 2)


def finish_kernel(parts, steps, at, p0, p1, p2, p3, *outs):
    pieces = (p0, p1, p2, p3)
    if steps:
        row = p0.shape[0] - SMALL
        *outs, gain, bias, in_bias, out_bias, table, total = outs
        wide, split = gain.shape[1], SMALL - TABLE
        total[...] = sum(ref[row:, :].astype(F32) for ref in pieces)
        for at_row, out in ((0, gain), (3, bias), (10, out_bias)):
            out[...] = total[at_row:at_row + out.shape[0], :wide]
        each = min(128 // wide, 4)
        for n in range(4 // each):
            joined = join_lanes([total[6 + n * each + k:7 + n * each + k, :] for k in range(each)], wide)
            in_bias[:, n * each * wide:(n + 1) * each * wide] = joined[:, :each * wide]
        table[:split, :] = total[TABLE:, :wide]
        table[split:, :] = pltpu.roll(total[...], 64, 1)[:steps - split, :wide]
    for k, ref in enumerate(pieces):
        lanes = pl.multiple_of((k ^ (at[1] * 2 + at[0])) * 128, 128)
        row = 0
        for out, (rows, blocks) in zip(outs, parts):
            for c in range(blocks):
                out[:, pl.ds(c * 512 + lanes, 128)] = ref[row:row + rows, :].astype(F32)
                row += rows


def finish(at, piece, others, parts, wide=0, steps=0):
    shapes = [(rows, blocks * 512) for rows, blocks in parts]
    if steps:
        shapes += [(3, wide), (3, wide), (1, 4 * wide), (1, wide), (steps, wide)]
    outs = tuple(sds(s, F32) for s in shapes)
    return row_call(
        functools.partial(finish_kernel, parts, steps), "finish_grads", at, (piece, *others),
        [full_spec(piece.shape)] * 4, outs, [full_spec(s) for s in shapes],
        [pltpu.VMEM((SMALL, 128), F32)] if steps else [], 1, 0)


def swap(value, axis, count, bit):
    return lax.ppermute(value, axis, [(i, i ^ bit) for i in range(count)])


def tie(value, *first):
    return lax.optimization_barrier((value, *first))[0]


def double(held, axis, count, bit):
    return jnp.concatenate([held, swap(held, axis, count, bit)])


def spread(held, shards, bits):
    flips = [0]
    for bit in bits:
        flips = flips + [f ^ bit for f in flips]
    return jnp.concatenate([held if f == 0 else swap(held, "shard", shards, f) for f in flips])


def add_low(a, *others):
    return sum((v.astype(F32) for v in others), a.astype(F32)).astype(BF)


def landed(done, got, adds):
    done, got = lax.optimization_barrier((done, got))
    return lax.optimization_barrier((done, adds(got)))


def per_device(shards, tokens, encoder, timesteps, seg_starts, out_grad, time_table, norm_gain, norm_bias, self_qkv,
               self_out, cross_query, cross_kv, cross_out, ffn_in, ffn_in_bias, ffn_out, ffn_out_bias):
    trees, count, width = tokens.shape
    per_tree, r, steps = count // TR, width // shards, time_table.shape[0]
    rep, mine = lax.axis_index("rep"), lax.axis_index("shard")
    at = jnp.stack([rep & 1, rep >> 1, flip_bits(mine, shards.bit_length() - 1)]).astype(jnp.int32)
    tok, enc, g = tokens.reshape(-1, width), encoder.reshape(-1, width), out_grad.reshape(-1, width)
    piece1, piece2, piece3 = pack_call(
        at, self_qkv, self_out, cross_query, cross_kv, cross_out, ffn_in, ffn_out, norm_gain, norm_bias,
        ffn_in_bias, ffn_out_bias, time_table)

    high = [1 << b for b in range(shards.bit_length() - 2, 0, -1)]
    held = spread(piece1[None], shards, high)
    held, piece2 = lax.optimization_barrier((held, piece2))
    held, held2 = lax.optimization_barrier((double(held, "shard", shards, 1), spread(piece2[None], shards, high)))
    packed3 = lax.all_gather(tie(piece3, held), ("rep", "shard"), axis=0).reshape(4, shards, *piece3.shape)
    packed1 = double(held, "rep", 4, 1).reshape(2, shards, *piece1.shape)
    held2 = double(tie(held2, packed1), "shard", shards, 1)

    replicas = lambda v: [swap(v, "rep", 4, k) for k in (1, 2, 3)]
    (qkv, barred, own, small, x_t), held2 = lax.optimization_barrier(
        (first_call(at, seg_starts, timesteps, tok, packed1, per_tree), held2))
    packed2 = jnp.concatenate([held2, *replicas(held2)]).reshape(4, shards, *piece2.shape)
    self_mixed, self_ext = attend_forward(qkv, qkv, qkv, (0, 4, 8), (0, 4), trees, qm=barred, ko=own)
    after_self, cq, ckv = second_call(at, tok, small, (self_mixed,), enc, packed2, per_tree)
    cross_mixed, cross_ext = attend_forward(cq, ckv, ckv, (0, 0, 4), (0, 4), trees)
    out, resid, cross_back, keep3, send3, small3 = ffn_call(at, after_self, cross_mixed, g, small, packed3)

    exchange = lambda v: lax.all_to_all(v, "shard", split_axis=0, concat_axis=0, tiled=True)
    sum_over = lambda v: jnp.sum(v.astype(F32), 0).astype(BF)
    halves = lambda keep: lambda got: (add_low(keep[0], got[0]), add_low(keep[1], got[1]))
    got3 = swap(send3, "rep", 4, 1)
    cross = functools.partial(attend_backward, cq, ckv, ckv, cross_back, cross_mixed, cross_ext, (0, 0, 4))
    (cross_low, cross_back), (mine3, other3) = landed((cross((0, 2), trees), cross_back), got3, halves(keep3))
    got3 = swap(other3, "rep", 4, 2)
    cross_high = attend_backward(cq, ckv, ckv, cross_back, cross_mixed, cross_ext, (0, 0, 4), (2, 4), trees)
    resid, self_back, enc_grad, keep2, send2, small2 = middle_call(
        at, (cross_low, cross_high), after_self, resid, (self_mixed,), enc, small, packed2)
    (self_back, send2), mine3 = landed((self_back, send2), got3, lambda got: add_low(mine3, got))
    shared3 = lax.psum_scatter(mine3, "shard", scatter_dimension=0, tiled=True)[0]
    got2 = swap(send2, "rep", 4, 1)
    back = lambda grad, flip: self_backward(at, qkv, grad, self_mixed, self_ext, own, x_t, flip, shards, trees)
    (part3, self_back), (mine2, other2) = landed((back(self_back, 3), self_back), got2, halves(keep2))
    far3, got2 = swap(part3[1], "rep", 4, 3), swap(other2, "rep", 4, 2)
    part2 = back(tie(self_back, part3), 2)
    far2 = swap(part2[1], "rep", 4, 2)
    (part1, self_back), mine2 = landed((back(tie(self_back, part2), 1), self_back), got2, lambda got: add_low(mine2, got))
    far1, got2 = swap(part1[1], "rep", 4, 1), exchange(mine2)
    part0, mine1 = landed(back(self_back, 0), (far1, far2, far3), lambda got: got)
    mine1 = add_low(part0[1], *mine1)
    got1, others3 = exchange(mine1), replicas(tie(shared3, mine1))
    self_grads = tie((part0[0], part1[0], part2[0], part3[0]), mine1)
    tok_grad, extra = last_call(at, timesteps, tok, self_grads, resid, small, small2, small3, packed1, per_tree)
    (tok_grad, extra), (done1, done2) = landed((tok_grad, extra), (got1, got2), lambda got: (sum_over(got[0]), sum_over(got[1])))
    got_extra, others2 = exchange(extra), replicas(done2)
    ffn_grads = finish(at, shared3, others3, ((r, 4), (4 * r, 1), (r, 1)))
    cross_grads = finish(at, done2, others2, ((r, 1), (r, 1), (r, 2)))
    ((ffn_in_grad, ffn_out_grad, cross_out_grad), (self_out_grad, cross_query_grad, cross_kv_grad)), piece1 = landed(
        (ffn_grads, cross_grads), got_extra, lambda got: jnp.concatenate([done1, sum_over(got)]))
    self_qkv_grad, gain_grad, bias_grad, in_bias_grad, out_bias_grad, table_grad = finish(
        at, piece1, replicas(piece1), ((r, 3),), r, steps)
    return (
        out.reshape(tokens.shape), tok_grad.reshape(tokens.shape), enc_grad.reshape(encoder.shape),
        table_grad, gain_grad, bias_grad, self_qkv_grad, self_out_grad, cross_query_grad, cross_kv_grad,
        cross_out_grad, ffn_in_grad, in_bias_grad.reshape(-1), ffn_out_grad, out_bias_grad.reshape(-1),
    )


def solution(mesh):
    trees = P(("rep", "shard"), None, None)
    rows, columns, flat = P("shard", None), P(None, "shard"), P("shard")
    in_specs = (trees, trees, P(("rep", "shard")), P(("rep", "shard"), None), trees, columns, columns, columns,
                rows, rows, rows, rows, rows, rows, flat, rows, flat)
    out_specs = (trees, trees, trees, columns, columns, columns, rows, rows, rows, rows, rows, rows, flat, rows, flat)
    return jax.shard_map(
        functools.partial(per_device, mesh.shape["shard"]), mesh=mesh, in_specs=in_specs, out_specs=out_specs,
        check_vma=False)
```

```python
import functools

import jax
import jax.numpy as jnp
from jax import lax
from jax.experimental import pallas as pl
from jax.experimental.pallas import tpu as pltpu
from jax.sharding import PartitionSpec as P

BF = jnp.bfloat16
F32 = jnp.float32


def nt(a, b):
    return lax.dot_general(a, b, (((1,), (1,)), ((), ())), preferred_element_type=F32)


def nn(a, b):
    return jnp.dot(a, b, preferred_element_type=F32)


def cost(flops, moved, exps=0):
    return pl.CostEstimate(flops=int(flops), bytes_accessed=int(moved), transcendentals=int(exps))


def kernel_params(axes):
    return pltpu.CompilerParams(vmem_limit_bytes=58 << 20, dimension_semantics=("arbitrary",) * axes)


def split3(x):
    hi = x.astype(BF)
    rest = x - hi.astype(F32)
    mid = rest.astype(BF)
    return hi, mid, (rest - mid.astype(F32)).astype(BF)


def place3(sub, parts, base):
    hi, mid, lo = parts
    return jnp.where(sub == 13, hi, jnp.where(sub == 14, mid, jnp.where(sub == 15, lo, base)))


def forward_tiles(masked, qlen, klen, tile):
    if not masked:
        return [(i, i + tile, klen) for i in range(0, qlen, tile)]
    trunk, segment = qlen - 12 * (qlen // 32), 2 * (qlen // 32)
    cuts = [0, qlen // 2, qlen]
    ends = [min(qlen, -(-max(trunk, b + segment - 1) // 128) * 128) for b in cuts[1:]]
    return list(zip(cuts[:-1], cuts[1:], ends))


def attend_forward_kernel(masked, tile, *refs):
    if masked:
        q_ref, k_ref, v_ref, qm_ref, ko_ref = refs[:5]
    else:
        q_ref, k_ref, v_ref = refs[:3]
    o_ref, ext_ref = refs[-2:]
    lane = lax.broadcasted_iota(jnp.int32, (1, 128), 1)
    first, sub = lane < 64, lane & 63
    zero, one = jnp.zeros((1, 128), BF), jnp.ones((1, 128), BF)
    k, v = k_ref[...], v_ref[...]
    other = ko_ref[...] if masked else zero
    keys = (jnp.where(first, k, other), jnp.where(first, other, k))
    vals = (jnp.where(first, v, one), jnp.where(first, one, v))
    def scores(low, high, count, h):
        q = q_ref[low:high, :] * jnp.asarray(0.125, BF)
        qm = qm_ref[low:high, :] if masked else zero
        return nt(jnp.where(first, q, qm) if h == 0 else jnp.where(first, qm, q), keys[h][:count])

    work = [(*tile, h) for tile in forward_tiles(masked, q_ref.shape[0], k_ref.shape[0], tile) for h in range(2)]
    ahead = scores(*work[0])
    for n, (low, high, count, h) in enumerate(work):
        s = ahead
        if n + 1 < len(work):
            ahead = scores(*work[n + 1])
        peak = jnp.max(s, axis=1, keepdims=True)
        out = nn(jnp.exp(s - peak).astype(BF), vals[h][:count])
        if h == 0:
            kept = out, peak
            continue
        rows = pl.ds(low, high - low)
        sums = jnp.where(first, out, kept[0])
        o_ref[rows, :] = (jnp.where(first, kept[0], out) / pltpu.roll(sums, 64, 1)).astype(BF)
        logsum = jnp.where(first, peak, kept[1]) + jnp.log(sums)
        ext_ref[rows, :] = place3(sub, split3(-logsum), qm_ref[rows, :] if masked else zero)


def attend_forward(q, k, v, cols, pairs, trees, qm=None, ko=None, tile=1024):
    qlen, klen = q.shape[0] // trees, k.shape[0] // trees
    tile = min(tile, qlen)
    low, count = pairs[0], pairs[1] - pairs[0]
    at = lambda n, c: pl.BlockSpec((n, 128), lambda t, h: (t, c + h))
    specs = [at(qlen, cols[0] + low), at(klen, cols[1] + low), at(klen, cols[2] + low)]
    args = [q, k, v]
    if qm is not None:
        specs += [pl.BlockSpec((qlen, 128), lambda t, h: (t, 0)), pl.BlockSpec((klen, 128), lambda t, h: (t, 0))]
        args += [qm, ko]
    shape = jax.ShapeDtypeStruct((trees * qlen, count * 128), BF)
    return pl.pallas_call(
        functools.partial(attend_forward_kernel, qm is not None, tile),
        grid=(trees, count), in_specs=specs, out_specs=[at(qlen, 0)] * 2, out_shape=[shape] * 2,
        compiler_params=kernel_params(2), name="attend_forward",
        cost_estimate=cost(trees * count * qlen * klen * 2000, trees * count * qlen * 1600, trees * count * 2 * qlen * klen),
    )(*args)


def backward_tiles(masked, qlen, klen, tq, tk):
    if not masked:
        return [(j, j + tk, [(i, i + tq) for i in range(0, qlen, tq)]) for j in range(0, klen, tk)]
    trunk, segment = qlen - 12 * (qlen // 32), 2 * (qlen // 32)
    steps = []
    for low, high in [(0, trunk), (trunk, qlen)]:
        start = 0 if low < trunk else (low - segment + 1) // 64 * 64
        spans = [start] + [c for c in range(tq, qlen, tq) if c > start + 128] + [qlen]
        steps.append((low, high, list(zip(spans[:-1], spans[1:]))))
    return steps


def attend_backward_kernel(masked, tq, tk, *refs):
    if masked:
        q_ref, k_ref, v_ref, do_ref, o_ref, ext_ref, ko_ref = refs[:7]
    else:
        q_ref, k_ref, v_ref, do_ref, o_ref, ext_ref = refs[:6]
    dq_ref, dk_ref, dv_ref, qa, qz, da, dz, kt, dqt = refs[-9:]
    lane = lax.broadcasted_iota(jnp.int32, (1, 128), 1)
    first, sub = lane < 64, lane & 63
    zero = jnp.zeros((1, 128), BF)
    ones = jnp.where((sub >= 13) & (sub < 16), jnp.ones((1, 128), BF), zero)
    q = q_ref[...] * jnp.asarray(0.125, BF)
    ext, do = ext_ref[...], do_ref[...]
    prod = do.astype(F32) * o_ref[...].astype(F32)
    for h in range(2):
        mine = first if h == 0 else ~first
        delta = jnp.sum(jnp.where(mine, prod, 0.0), axis=1, keepdims=True)
        parts = place3(sub, split3(jnp.broadcast_to(-delta, prod.shape)), zero)
        qa[h] = jnp.where(mine, q, ext)
        qz[h] = jnp.where(mine, q, zero)
        da[h] = jnp.where(mine, do, parts)
        dz[h] = jnp.where(mine, do, zero)
    kt[...] = k_ref[...].T
    dqt[...] = jnp.zeros_like(dqt)
    def products(k_low, k_high, q_low, q_high, h):
        mine = first if h == 0 else ~first
        k, v = k_ref[k_low:k_high, :], v_ref[k_low:k_high, :]
        other = ko_ref[k_low:k_high, :] if masked else ones
        return (nt(jnp.where(mine, k, other), qa[h, q_low:q_high, :]),
                nt(jnp.where(mine, v, ones), da[h, q_low:q_high, :]))

    work = [(k_low, k_high, q_low, q_high, h)
            for k_low, k_high, spans in backward_tiles(masked, q_ref.shape[0], k_ref.shape[0], tq, tk)
            for q_low, q_high in spans for h in range(2)]
    ahead = products(*work[0])
    for n, (k_low, k_high, q_low, q_high, h) in enumerate(work):
        scores, centred = ahead
        if n + 1 < len(work):
            ahead = products(*work[n + 1])
        if n == 0 or k_low != work[n - 1][0]:
            dk = jnp.zeros((k_high - k_low, 128), F32)
            dv = jnp.zeros((k_high - k_low, 128), F32)
        probs = jnp.exp(scores)
        ds = (probs * centred).astype(BF)
        dv = dv + nn(probs.astype(BF), dz[h, q_low:q_high, :])
        dk = dk + nn(ds, qz[h, q_low:q_high, :])
        dqt[64 * h:64 * h + 64, q_low:q_high] += nn(kt[64 * h:64 * h + 64, k_low:k_high], ds)
        if n + 1 == len(work) or k_low != work[n + 1][0]:
            dk_ref[k_low:k_high, :] = dk.astype(BF)
            dv_ref[k_low:k_high, :] = dv.astype(BF)

    dq_ref[...] = (dqt[...].T * 0.125).astype(BF)


def attend_backward(q, k, v, do, o, ext, cols, pairs, trees, ko=None, mixed_from=0, tq=256, tk=512):
    qlen, klen = q.shape[0] // trees, k.shape[0] // trees
    tq, tk = min(tq, qlen), min(tk, klen)
    low, count = pairs[0], pairs[1] - pairs[0]
    at = lambda n, c: pl.BlockSpec((n, 128), lambda t, h: (t, c + h))
    specs = [at(qlen, cols[0] + low), at(klen, cols[1] + low), at(klen, cols[2] + low), at(qlen, low)]
    specs += [at(qlen, low - mixed_from)] * 2
    args = [q, k, v, do, o, ext]
    if ko is not None:
        specs += [pl.BlockSpec((klen, 128), lambda t, h: (t, 0))]
        args += [ko]
    return pl.pallas_call(
        functools.partial(attend_backward_kernel, ko is not None, tq, tk),
        grid=(trees, count), in_specs=specs, out_specs=[at(qlen, 0), at(klen, 0), at(klen, 0)],
        out_shape=[jax.ShapeDtypeStruct((trees * n, count * 128), BF) for n in (qlen, klen, klen)],
        scratch_shapes=[pltpu.VMEM((2, qlen, 128), BF)] * 4 + [pltpu.VMEM((128, klen), BF), pltpu.VMEM((128, qlen), F32)],
        compiler_params=kernel_params(2), name="attend_backward",
        cost_estimate=cost(trees * count * qlen * klen * 4000, trees * count * qlen * 2500, trees * count * 2 * qlen * klen),
    )(*args)


def self_backward_kernel(trees, tq, tk, at, *refs):
    xt_ref, dw_ref, acc = refs[7], refs[11], refs[-1]
    dq_ref, dk_ref, dv_ref = refs[8:11]
    attend_backward_kernel(True, tq, tk, *refs[:7], dq_ref, dk_ref, dv_ref, *refs[12:-1])
    term = nn(xt_ref[...], jnp.concatenate([dq_ref[...], dk_ref[...], dv_ref[...]], 1))
    step = pl.program_id(1)

    @pl.when(step == 0)
    def _():
        acc[...] = term

    @pl.when(step > 0)
    def _():
        acc[...] += term

    @pl.when(step == trees - 1)
    def _():
        shards = dw_ref.shape[0]
        r = 512 // shards
        for c in range(3):
            dw_ref[:, c * r:(c + 1) * r, :] = acc[:, c * 128:(c + 1) * 128].astype(BF).reshape(shards, r, 128)


def self_backward(at, qkv, do, o, ext, own, x_t, flip, count, shards, trees, tq=256, tk=512):
    rows = qkv.shape[0] // trees
    block = lambda c: pl.BlockSpec((rows, 128), lambda h, t, at: (t, c + ((at[1] * 2 + at[0]) ^ (flip - h))))
    plain = pl.BlockSpec((rows, 128), lambda h, t, at: (t, h))
    piece = (shards, 3 * (512 // shards), 128)
    *grads, dw = pl.pallas_call(
        functools.partial(self_backward_kernel, trees, tq, tk),
        grid_spec=pltpu.PrefetchScalarGridSpec(
            num_scalar_prefetch=1, grid=(count, trees),
            in_specs=[block(0), block(4), block(8), block(0), block(0), block(0),
                      pl.BlockSpec((rows, 128), lambda h, t, at: (t, 0)), pl.BlockSpec((512, rows), lambda h, t, at: (0, t))],
            out_specs=[plain] * 3 + [pl.BlockSpec((None, *piece), lambda h, t, at: (h, 0, 0, 0))],
            scratch_shapes=[pltpu.VMEM((2, rows, 128), BF)] * 4 + [
                pltpu.VMEM((128, rows), BF), pltpu.VMEM((128, rows), F32), pltpu.VMEM((512, 384), F32)]),
        out_shape=[jax.ShapeDtypeStruct((trees * rows, count * 128), BF)] * 3 + [jax.ShapeDtypeStruct((count, *piece), BF)],
        compiler_params=kernel_params(2), name="attend_backward",
        cost_estimate=cost(count * trees * rows * rows * 4000, count * trees * rows * 4500, count * trees * 2 * rows * rows),
    )(at, qkv, qkv, qkv, do, o, ext, own, x_t)
    return tuple(grads), tuple(dw[h] for h in range(count))


TR = 512
RESID = F32


def norm_rows(h, gain, bias):
    centred = h - jnp.mean(h, -1, keepdims=True)
    inv = lax.rsqrt(jnp.mean(centred * centred, -1, keepdims=True) + 1e-05)
    normed = centred * inv
    return normed * gain + bias, normed, inv


def norm_pull(dy, normed, inv, gain):
    scaled = dy * gain
    along = jnp.mean(scaled * normed, -1, keepdims=True)
    dx = inv * (scaled - jnp.mean(scaled, -1, keepdims=True) - normed * along)
    return dx, jnp.sum(dy * normed, 0, keepdims=True), jnp.sum(dy, 0, keepdims=True)


def row_spec(width, rows=TR):
    return pl.BlockSpec((rows, width), lambda i, at: (i, 0))


def full_spec(shape):
    return pl.BlockSpec(shape, lambda i, at: (0,) * len(shape))


def part_spec(packed, part, rows):
    lead = packed.shape[:-2]
    return pl.BlockSpec((*lead, rows, 128), lambda i, at: (0,) * len(lead) + (part, 0))


def flip_bits(value, count):
    return sum(((value >> b) & 1) << (count - 1 - b) for b in range(count))


def place_weight(at, relative, ref, dst, slots=None):
    shards, rows = ref.shape[1], ref.shape[-2]
    bits = shards.bit_length() - 1
    for q in range(4):
        for j in range(shards):
            if slots:
                piece = ref[slots[q] & 1, flip_bits(j, bits) ^ at[2], slots[q] >> 1]
            elif relative and len(ref.shape) == 5:
                piece = ref[(q & 1) ^ at[0], flip_bits(j, bits) ^ at[2], (q >> 1) ^ at[1]]
            elif relative:
                piece = ref[q ^ (at[1] * 2 + at[0]), flip_bits(j, bits) ^ at[2]]
            else:
                piece = ref[q, j]
            dst[j * rows:(j + 1) * rows, q * 128:(q + 1) * 128] = piece


def pack_grad(at, acc, keep, send, offset):
    shards = keep.shape[1]
    rows = acc.shape[0] // shards
    for q in range(4):
        piece = acc[:, q * 128:(q + 1) * 128].astype(BF).reshape(shards, rows, 128)
        for core in range(2):
            @pl.when(at[0] == core)
            def _(q=q, core=core, piece=piece):
                (keep if (q & 1) == core else send)[(q >> 1) ^ at[1], :, offset:offset + rows, :] = piece


def start_rows(tok_ref, small_ref, per_tree):
    tree = pl.program_id(0) // per_tree
    return tok_ref[...].astype(F32) + small_ref[pl.ds(11 + tree, 1), :]


def side_by_side(refs):
    return jnp.concatenate([ref[...] for ref in refs], 1) if len(refs) > 1 else refs[0][...]


def clear(*refs):
    for ref in refs:
        ref[...] = jnp.zeros_like(ref)


def gelu_both(x):
    k = 0.7978845608028654
    x2 = x * x
    t = jnp.tanh(k * x * (1.0 + 0.044715 * x2))
    half = 0.5 * (1.0 + t)
    return x * half, half + 0.5 * x * (1.0 - t * t) * (k + (3 * 0.044715 * k) * x2)


def row_call(kernel, name, at, args, specs, outs, out_specs, scratch, steps, flops):
    moved = sum(a.size * a.dtype.itemsize for a in (*args, *outs))
    return pl.pallas_call(
        kernel,
        grid_spec=pltpu.PrefetchScalarGridSpec(
            num_scalar_prefetch=1, grid=(steps,), in_specs=specs, out_specs=out_specs, scratch_shapes=scratch),
        out_shape=outs, compiler_params=kernel_params(1), name=name, cost_estimate=cost(flops, moved),
    )(at, *args)


def sds(shape, dtype):
    return jax.ShapeDtypeStruct(shape, dtype)


def token_rows(starts, first_position, rows):
    position = lax.broadcasted_iota(jnp.int32, (rows, 128), 0) + first_position
    sub = lax.broadcasted_iota(jnp.int32, (rows, 128), 1) & 63
    seg = jnp.zeros((rows, 128), jnp.int32)
    for j in range(1, 13):
        seg = seg + (position >= starts(j)).astype(jnp.int32)
    parent = jnp.where(seg >= 5, 1 + ((seg - 5) >> 1), 0)
    seen = (sub == seg) | (sub == 0) | (sub == parent) | (sub >= 13)
    own = (sub == seg) | ((sub >= 13) & (sub < 16))
    return jnp.where(seen, 0.0, -1e30).astype(BF), jnp.where(own, 1.0, 0.0).astype(BF)


SMALL = 32
TABLE = 11


def pack_kernel(at, qkv, so, cq, ckv, co, fi, fo, gain, bias, in_bias, out_bias, table, p1, p2, p3, scratch):
    for out, flip, weights in ((p1.at[0], 0, (qkv,)), (p1.at[1], 2, (qkv,)), (p2, 0, (so, cq, ckv)), (p3, 0, (fi, fo, co))):
        lanes = pl.multiple_of(((at[1] * 2 + at[0]) ^ flip) * 128, 128)
        row = 0
        for ref in weights:
            for c in range(ref.shape[1] // 512):
                out[row:row + ref.shape[0], :] = ref[:, pl.ds(c * 512 + lanes, 128)]
                row += ref.shape[0]
    wide, steps, split = gain.shape[1], table.shape[0], SMALL - TABLE
    clear(scratch)
    for row, ref in ((0, gain), (3, bias)):
        scratch[row:row + ref.shape[0], :wide] = ref[...].astype(F32)
    flat = in_bias[...].astype(F32).reshape(1, 4 * wide)
    for a in range(4):
        scratch[6 + a:7 + a, :wide] = flat[:, a * wide:(a + 1) * wide]
    scratch[10:11, :wide] = out_bias[...].astype(F32).reshape(1, wide)
    scratch[TABLE:, :wide] = table[:split, :].astype(F32)
    scratch[:steps - split, 64:64 + wide] = table[split:, :].astype(F32)
    for half in range(2):
        p1[half, p1.shape[1] - SMALL:, :] = scratch[...].astype(BF)


def small_row(r):
    return -(-3 * r // SMALL) * SMALL


def pack_call(at, *args):
    r = args[0].shape[0]
    outs = (sds((2, small_row(r) + SMALL, 128), BF), sds((4 * r, 128), BF), sds((9 * r, 128), BF))
    return row_call(pack_kernel, "pack_quarters", at, args, [full_spec(a.shape) for a in args], outs,
                    [full_spec(o.shape) for o in outs], [pltpu.VMEM((SMALL, 128), F32)], 1, 0)


def join_lanes(pieces, wide):
    lane = lax.broadcasted_iota(jnp.int32, (1, 128), 1)
    out = pieces[0]
    for k, piece in enumerate(pieces[1:], 1):
        out = jnp.where(lane >= wide * k, pltpu.roll(piece, wide * k, 1), out)
    return out


def unpack_small(at, step_ref, ref, shards, trees, small, rows):
    wide, bits = 512 // shards, shards.bit_length() - 1
    each = 128 // wide
    pieces = [ref[0, flip_bits(j, bits) ^ at[2], 0].astype(F32) for j in range(shards)]
    turned = [pltpu.roll(p, 64, 1) for p in pieces]
    clear(small)
    for g in range(4):
        lanes = slice(g * 128, g * 128 + 128)
        rows[:SMALL, lanes] = join_lanes(pieces[g * each:(g + 1) * each], wide)
        rows[SMALL:, lanes] = join_lanes(turned[g * each:(g + 1) * each], wide)
    for n in range(16):
        parts = [divmod(n * each + k, 4) for k in range(each)]
        small[6 + n // 4:7 + n // 4, n % 4 * 128:n % 4 * 128 + 128] = join_lanes(
            [pieces[j][6 + a:7 + a, :] for j, a in parts], wide)
    small[0:6, :] = rows[0:6, :]
    small[10:11, :] = rows[10:11, :]
    for t in range(trees):
        small[TABLE + t:TABLE + t + 1, :] = rows[pl.ds(TABLE + step_ref[t], 1), :]


def first_kernel(shards, trees, per_tree, at, seg_ref, step_ref, tok_ref, held_ref, wq, wk, wv,
                 qkv_ref, barred_ref, own_ref, small_ref, xt_ref, w, small, rows):
    step = pl.program_id(0)

    @pl.when(step == 0)
    def _():
        for c, ref in enumerate((wq, wk, wv)):
            place_weight(at, True, ref, w.at[c])
        unpack_small(at, step_ref, held_ref, shards, trees, small, rows)
        small_ref[...] = small[...]

    tree = step // per_tree
    barred_ref[...], own_ref[...] = token_rows(lambda j: seg_ref[tree, j], (step % per_tree) * TR, TR)
    x, _, _ = norm_rows(start_rows(tok_ref, small, per_tree), small[0:1, :], small[3:4, :])
    x = x.astype(BF)
    xt_ref[...] = x.T
    for c in range(3):
        qkv_ref[:, c * 512:(c + 1) * 512] = nn(x, w[c]).astype(BF)


def first_call(at, seg_starts, timesteps, tokens, packed, per_tree):
    rows, shards, trees = tokens.shape[0], packed.shape[1], seg_starts.shape[0]
    r = 512 // shards
    held = pl.BlockSpec((1, shards, 1, SMALL, 128), lambda i, at: (0, 0, 0, small_row(r) // SMALL, 0))
    scalars = pl.BlockSpec(memory_space=pltpu.SMEM)
    lines = 16 * -(-(TABLE + trees) // 16)
    return row_call(
        functools.partial(first_kernel, shards, trees, per_tree), "project_qkv", at,
        (seg_starts, timesteps, tokens, packed, packed, packed, packed),
        [scalars, scalars, row_spec(512), held] + [part_spec(packed, c, r) for c in range(3)],
        (sds((rows, 1536), BF), sds((rows, 128), BF), sds((rows, 128), BF), sds((lines, 512), F32), sds((512, rows), BF)),
        [row_spec(1536), row_spec(128), row_spec(128), full_spec((lines, 512)), pl.BlockSpec((512, TR), lambda i, at: (0, i))],
        [pltpu.VMEM((3, 512, 512), BF), pltpu.VMEM((lines, 512), F32), pltpu.VMEM((2 * SMALL, 512), F32)],
        rows // TR, rows * 512 * 1536 * 2)


def second_kernel(per_tree, count, at, tok_ref, small_ref, enc_ref, wo, wq, wk, wv, *refs):
    mixed_refs, (after_ref, cq_ref, ckv_ref, w) = refs[:count], refs[count:]

    @pl.when(pl.program_id(0) == 0)
    def _():
        for c, ref in enumerate((wo, wq, wk, wv)):
            place_weight(at, True, ref, w.at[c])

    h = start_rows(tok_ref, small_ref, per_tree) + nn(side_by_side(mixed_refs), w[0])
    after_ref[...] = h.astype(RESID)
    x, _, _ = norm_rows(h, small_ref[1:2, :], small_ref[4:5, :])
    cq_ref[...] = nn(x.astype(BF), w[1]).astype(BF)
    e = enc_ref[...]
    ckv_ref[:, :512] = nn(e, w[2]).astype(BF)
    ckv_ref[:, 512:] = nn(e, w[3]).astype(BF)


def second_call(at, tokens, small, mixed, enc, packed, per_tree):
    rows, r = tokens.shape[0], 512 // packed.shape[1]
    steps = rows // TR
    er = enc.shape[0] // steps
    return row_call(
        functools.partial(second_kernel, per_tree, len(mixed)), "cross_inputs", at,
        (tokens, small, enc, packed, packed, packed, packed, *mixed),
        [row_spec(512), full_spec(small.shape), row_spec(512, er)] + [part_spec(packed, c, r) for c in range(4)]
        + [row_spec(m.shape[1]) for m in mixed],
        (sds((rows, 512), RESID), sds((rows, 512), BF), sds((enc.shape[0], 1024), BF)),
        [row_spec(512), row_spec(512), row_spec(1024, er)], [pltpu.VMEM((4, 512, 512), BF)], steps, rows * 512 * 1536 * 2)


def ffn_kernel(at, after_ref, mixed_ref, g_ref, small_ref, wi0, wi1, wi2, wi3, wf, wc,
               out_ref, resid_ref, cmg_ref, keep, send, gs_ref, w, wo, aco, afi, afo):
    step = pl.program_id(0)
    r = wc.shape[-2]

    @pl.when(step == 0)
    def _():
        clear(aco, afi, afo, gs_ref)
        for c, ref in enumerate((wi0, wi1, wi2, wi3, wc)):
            place_weight(at, False, ref, w.at[c])
        place_weight(at, False, wf, wo)

    mixed, g = mixed_ref[...], g_ref[...]
    h = after_ref[...].astype(F32) + nn(mixed, w[4])
    y, normed, inv = norm_rows(h, small_ref[2:3, :], small_ref[5:6, :])
    third = y.astype(BF)
    third_t, g_t = third.T, g.T
    out = h + small_ref[10:11, :]
    back = jnp.zeros(h.shape, F32)
    for c in range(4):
        wi, wf_c = w[c], wo[c * 512:(c + 1) * 512, :]
        value, slope = gelu_both(nn(third, wi) + small_ref[6 + c:7 + c, :])
        hidden = value.astype(BF)
        out = out + nn(hidden, wf_c)
        pre_grad = (nt(g, wf_c) * slope).astype(BF)
        gs_ref[2 + c:3 + c, :] += jnp.sum(pre_grad.astype(F32), 0, keepdims=True)
        back = back + nt(pre_grad, wi)
        afi[c] += nn(third_t, pre_grad)
        afo[c] += nn(g_t, hidden)
    out_ref[...] = out.astype(BF)
    g_high = g.astype(F32)
    gs_ref[6:7, :] += jnp.sum(g_high, 0, keepdims=True)
    dx, dg, db = norm_pull(back, normed, inv, small_ref[2:3, :])
    gs_ref[0:1, :] += dg
    gs_ref[1:2, :] += db
    resid = g_high + dx
    resid_ref[...] = resid.astype(RESID)
    low = resid.astype(BF)
    cmg_ref[...] = nt(low, w[4]).astype(BF)
    aco[...] += nn(mixed.T, low)

    @pl.when(step == pl.num_programs(0) - 1)
    def _():
        for c in range(4):
            pack_grad(at, afi[c], keep, send, c * r)
        for c in range(4):
            whole = afo[c].T
            shards = keep.shape[1]
            quarter = shards // 4
            for q in range(4):
                piece = whole[:, q * 128:(q + 1) * 128].astype(BF).reshape(quarter, 4 * r, 128)
                for core in range(2):
                    @pl.when(at[0] == core)
                    def _(q=q, core=core, piece=piece, c=c):
                        (keep if (q & 1) == core else send)[(q >> 1) ^ at[1], c * quarter:(c + 1) * quarter, 4 * r:8 * r, :] = piece
        pack_grad(at, aco[...], keep, send, 8 * r)


def ffn_call(at, after, mixed, g, small, packed):
    rows, shards = after.shape[0], packed.shape[1]
    r = 512 // shards
    half = sds((2, shards, 9 * r, 128), BF)
    return row_call(
        ffn_kernel, "ffn_both_ways", at,
        (after, mixed, g, small) + (packed,) * 6,
        [row_spec(512)] * 3 + [full_spec(small.shape)] + [part_spec(packed, c, r) for c in range(4)]
        + [part_spec(packed, 1, 4 * r), part_spec(packed, 8, r)],
        (sds((rows, 512), BF), sds((rows, 512), RESID), sds((rows, 512), BF), half, half, sds((8, 512), F32)),
        [row_spec(512)] * 3 + [full_spec(half.shape)] * 2 + [full_spec((8, 512))],
        [pltpu.VMEM((5, 512, 512), BF), pltpu.VMEM((2048, 512), BF), pltpu.VMEM((512, 512), F32),
         pltpu.VMEM((4, 512, 512), F32), pltpu.VMEM((4, 512, 512), F32)],
        rows // TR, rows * 512 * 2048 * 12)


def middle_kernel(mixes, chunks, at, after_ref, resid_ref, enc_ref, small_ref, wo, wq, wk, wv, *refs):
    mixed_refs, refs = refs[:mixes], refs[mixes:]
    cqg_refs, ckg_refs, cvg_refs = refs[:chunks], refs[chunks:2 * chunks], refs[2 * chunks:3 * chunks]
    resid2_ref, smg_ref, encg_ref, keep, send, gs_ref, w, acc = refs[3 * chunks:]
    step = pl.program_id(0)
    r = wo.shape[-2]

    @pl.when(step == 0)
    def _():
        clear(acc, gs_ref)
        for c, ref in enumerate((wo, wq, wk, wv)):
            place_weight(at, True, ref, w.at[c])

    y, normed, inv = norm_rows(after_ref[...].astype(F32), small_ref[1:2, :], small_ref[4:5, :])
    cqg = side_by_side(cqg_refs)
    acc[1] += nn(y.astype(BF).T, cqg)
    dx, dg, db = norm_pull(nt(cqg, w[1]), normed, inv, small_ref[1:2, :])
    gs_ref[0:1, :] += dg
    gs_ref[1:2, :] += db
    resid = resid_ref[...].astype(F32) + dx
    resid2_ref[...] = resid.astype(RESID)
    low = resid.astype(BF)
    acc[0] += nn(side_by_side(mixed_refs).T, low)
    smg_ref[...] = nt(low, w[0]).astype(BF)
    enc_t, ckg, cvg = enc_ref[...].T, side_by_side(ckg_refs), side_by_side(cvg_refs)
    acc[2] += nn(enc_t, ckg)
    acc[3] += nn(enc_t, cvg)
    encg_ref[...] = (nt(ckg, w[2]) + nt(cvg, w[3])).astype(BF)

    @pl.when(step == pl.num_programs(0) - 1)
    def _():
        for c in range(4):
            pack_grad(at, acc[c], keep, send, c * r)


def middle_call(at, cross_grads, after, resid, mixed, enc, small, packed):
    rows, shards = after.shape[0], packed.shape[1]
    r, steps = 512 // shards, rows // TR
    er = enc.shape[0] // steps
    half = sds((2, shards, 4 * r, 128), BF)
    cqg, ckg, cvg = zip(*cross_grads)
    return row_call(
        functools.partial(middle_kernel, len(mixed), len(cqg)), "between_attentions", at,
        (after, resid, enc, small) + (packed,) * 4 + tuple(mixed) + cqg + ckg + cvg,
        [row_spec(512)] * 2 + [row_spec(512, er), full_spec(small.shape)] + [part_spec(packed, c, r) for c in range(4)]
        + [row_spec(m.shape[1]) for m in (*mixed, *cqg)] + [row_spec(m.shape[1], er) for m in (*ckg, *cvg)],
        (sds((rows, 512), RESID), sds((rows, 512), BF), sds(enc.shape, BF), half, half, sds((8, 512), F32)),
        [row_spec(512), row_spec(512), row_spec(512, er)] + [full_spec(half.shape)] * 2 + [full_spec((8, 512))],
        [pltpu.VMEM((4, 512, 512), BF), pltpu.VMEM((4, 512, 512), F32)], steps, rows * 512 * 512 * 12)


def pack_small_grads(at, step_ref, sums, gs2, gs3, trees, rows, piece, extra):
    shards = extra.shape[0]
    wide = 512 // shards
    lane = lax.broadcasted_iota(jnp.int32, (1, 128), 1)
    clear(rows)
    for row, ref, src in ((0, sums, 0), (1, gs2, 0), (2, gs3, 0), (3, sums, 1), (4, gs2, 1), (5, gs3, 1), (10, gs3, 6)):
        rows[row:row + 1, :] = ref[src:src + 1, :]
    for t in range(trees):
        rows[pl.ds(TABLE + step_ref[t], 1), :] += sums[2 + t:3 + t, :]
    turn = lambda value, by: pltpu.roll(value, by % 128, 1) if by % 128 else value
    for j in range(shards):
        at_lane = j * wide
        lanes, off = slice(at_lane // 128 * 128, at_lane // 128 * 128 + 128), at_lane % 128
        low, high = turn(rows[:SMALL, lanes], -off), turn(rows[SMALL:, lanes], 64 - off)
        piece[...] = jnp.where(lane < wide, low, jnp.where((lane >= 64) & (lane < 64 + wide), high, 0.0))
        for a in range(4):
            row, col = divmod((j * 4 + a) * wide, 512)
            value = turn(gs3[2 + row:3 + row, col // 128 * 128:col // 128 * 128 + 128], -(col % 128))
            piece[6 + a:7 + a, :] = jnp.where(lane < wide, value, piece[6 + a:7 + a, :])
        extra[j] = piece[...].astype(BF)


def last_kernel(per_tree, trees, chunks, at, step_ref, tok_ref, resid_ref, small_ref, gs2, gs3, wq, wk, wv, *refs):
    grads = [refs[n * chunks:(n + 1) * chunks] for n in range(3)]
    tokg_ref, extra, w, sums, rows, piece = refs[3 * chunks:]
    step = pl.program_id(0)

    @pl.when(step == 0)
    def _():
        clear(sums)
        for c, ref in enumerate((wq, wk, wv)):
            place_weight(at, True, ref, w.at[c], (0, 2, 1, 3))

    _, normed, inv = norm_rows(start_rows(tok_ref, small_ref, per_tree), small_ref[0:1, :], small_ref[3:4, :])
    back = sum(nt(side_by_side(grads[c]), w[c]) for c in range(3))
    dx, dg, db = norm_pull(back, normed, inv, small_ref[0:1, :])
    sums[0:1, :] += dg
    sums[1:2, :] += db
    resid = resid_ref[...].astype(F32) + dx
    tokg_ref[...] = resid.astype(BF)
    sums[pl.ds(2 + step // per_tree, 1), :] += jnp.sum(resid, 0, keepdims=True)

    @pl.when(step == pl.num_programs(0) - 1)
    def _():
        pack_small_grads(at, step_ref, sums, gs2, gs3, trees, rows, piece, extra)


def last_call(at, timesteps, tokens, self_grads, resid, small, small2, small3, packed, per_tree):
    rows, shards, trees = tokens.shape[0], packed.shape[1], timesteps.shape[0]
    r = 512 // shards
    qg, kg, vg = zip(*self_grads)
    extra = sds((shards, SMALL, 128), BF)
    lines = 8 * -(-(2 + trees) // 8)
    return row_call(
        functools.partial(last_kernel, per_tree, trees, len(qg)), "first_norm_back", at,
        (timesteps, tokens, resid, small, small2, small3) + (packed,) * 3 + qg + kg + vg,
        [pl.BlockSpec(memory_space=pltpu.SMEM)] + [row_spec(512)] * 2 + [full_spec(a.shape) for a in (small, small2, small3)]
        + [part_spec(packed, c, r) for c in range(3)] + [row_spec(m.shape[1]) for m in (*qg, *kg, *vg)],
        (sds((rows, 512), BF), extra), [row_spec(512), full_spec(extra.shape)],
        [pltpu.VMEM((3, 512, 512), BF), pltpu.VMEM((lines, 512), F32), pltpu.VMEM((2 * SMALL, 512), F32), pltpu.VMEM((SMALL, 128), F32)],
        rows // TR, rows * 512 * 1536 * 2)


def finish_kernel(parts, steps, at, p0, p1, p2, p3, *outs):
    pieces = (p0, p1, p2, p3)
    if steps:
        row = p0.shape[0] - SMALL
        *outs, gain, bias, in_bias, out_bias, table, total = outs
        wide, split = gain.shape[1], SMALL - TABLE
        total[...] = sum(ref[row:, :].astype(F32) for ref in pieces)
        for at_row, out in ((0, gain), (3, bias), (10, out_bias)):
            out[...] = total[at_row:at_row + out.shape[0], :wide]
        each = min(128 // wide, 4)
        for n in range(4 // each):
            joined = join_lanes([total[6 + n * each + k:7 + n * each + k, :] for k in range(each)], wide)
            in_bias[:, n * each * wide:(n + 1) * each * wide] = joined[:, :each * wide]
        table[:split, :] = total[TABLE:, :wide]
        table[split:, :] = pltpu.roll(total[...], 64, 1)[:steps - split, :wide]
    for k, ref in enumerate(pieces):
        lanes = pl.multiple_of((k ^ (at[1] * 2 + at[0])) * 128, 128)
        row = 0
        for out, (rows, blocks) in zip(outs, parts):
            for c in range(blocks):
                out[:, pl.ds(c * 512 + lanes, 128)] = ref[row:row + rows, :].astype(F32)
                row += rows


def finish(at, piece, others, parts, wide=0, steps=0):
    shapes = [(rows, blocks * 512) for rows, blocks in parts]
    if steps:
        shapes += [(3, wide), (3, wide), (1, 4 * wide), (1, wide), (steps, wide)]
    outs = tuple(sds(s, F32) for s in shapes)
    return row_call(
        functools.partial(finish_kernel, parts, steps), "finish_grads", at, (piece, *others),
        [full_spec(piece.shape)] * 4, outs, [full_spec(s) for s in shapes],
        [pltpu.VMEM((SMALL, 128), F32)] if steps else [], 1, 0)


def swap(value, axis, count, bit):
    return lax.ppermute(value, axis, [(i, i ^ bit) for i in range(count)])


def tie(value, *first):
    return lax.optimization_barrier((value, *first))[0]


def double(held, axis, count, bit):
    return jnp.concatenate([held, swap(held, axis, count, bit)])


def spread(held, shards, bits):
    flips = [0]
    for bit in bits:
        flips = flips + [f ^ bit for f in flips]
    return jnp.concatenate([held if f == 0 else swap(held, "shard", shards, f) for f in flips])


def add_low(a, *others):
    return sum((v.astype(F32) for v in others), a.astype(F32)).astype(BF)


def landed(done, got, adds):
    done, got = lax.optimization_barrier((done, got))
    return lax.optimization_barrier((done, adds(got)))


def per_device(shards, tokens, encoder, timesteps, seg_starts, out_grad, time_table, norm_gain, norm_bias, self_qkv,
               self_out, cross_query, cross_kv, cross_out, ffn_in, ffn_in_bias, ffn_out, ffn_out_bias):
    trees, count, width = tokens.shape
    per_tree, r, steps = count // TR, width // shards, time_table.shape[0]
    rep, mine = lax.axis_index("rep"), lax.axis_index("shard")
    at = jnp.stack([rep & 1, rep >> 1, flip_bits(mine, shards.bit_length() - 1)]).astype(jnp.int32)
    tok, enc, g = tokens.reshape(-1, width), encoder.reshape(-1, width), out_grad.reshape(-1, width)
    piece1, piece2, piece3 = pack_call(
        at, self_qkv, self_out, cross_query, cross_kv, cross_out, ffn_in, ffn_out, norm_gain, norm_bias,
        ffn_in_bias, ffn_out_bias, time_table)

    high = [1 << b for b in range(shards.bit_length() - 2, 0, -1)]
    held = spread(piece1[None], shards, high)
    held, piece2 = lax.optimization_barrier((held, piece2))
    held, held2 = lax.optimization_barrier((double(held, "shard", shards, 1), spread(piece2[None], shards, high)))
    packed3 = lax.all_gather(tie(piece3, held), ("rep", "shard"), axis=0).reshape(4, shards, *piece3.shape)
    packed1 = double(held, "rep", 4, 1).reshape(2, shards, *piece1.shape)
    held2 = double(tie(held2, packed1), "shard", shards, 1)

    replicas = lambda v: [swap(v, "rep", 4, k) for k in (1, 2, 3)]
    (qkv, barred, own, small, x_t), held2 = lax.optimization_barrier(
        (first_call(at, seg_starts, timesteps, tok, packed1, per_tree), held2))
    packed2 = jnp.concatenate([held2, *replicas(held2)]).reshape(4, shards, *piece2.shape)
    self_mixed, self_ext = attend_forward(qkv, qkv, qkv, (0, 4, 8), (0, 4), trees, qm=barred, ko=own)
    after_self, cq, ckv = second_call(at, tok, small, (self_mixed,), enc, packed2, per_tree)
    cross_mixed, cross_ext = attend_forward(cq, ckv, ckv, (0, 0, 4), (0, 4), trees)
    out, resid, cross_back, keep3, send3, small3 = ffn_call(at, after_self, cross_mixed, g, small, packed3)

    exchange = lambda v: lax.all_to_all(v, "shard", split_axis=0, concat_axis=0, tiled=True)
    sum_over = lambda v: jnp.sum(v.astype(F32), 0).astype(BF)
    halves = lambda keep: lambda got: (add_low(keep[0], got[0]), add_low(keep[1], got[1]))
    got3 = swap(send3, "rep", 4, 1)
    cross = functools.partial(attend_backward, cq, ckv, ckv, cross_back, cross_mixed, cross_ext, (0, 0, 4))
    (cross_low, cross_back), (mine3, other3) = landed((cross((0, 2), trees), cross_back), got3, halves(keep3))
    got3 = swap(other3, "rep", 4, 2)
    cross_high = attend_backward(cq, ckv, ckv, cross_back, cross_mixed, cross_ext, (0, 0, 4), (2, 4), trees)
    resid, self_back, enc_grad, keep2, send2, small2 = middle_call(
        at, (cross_low, cross_high), after_self, resid, (self_mixed,), enc, small, packed2)
    (self_back, send2), mine3 = landed((self_back, send2), got3, lambda got: add_low(mine3, got))
    shared3 = lax.psum_scatter(mine3, "shard", scatter_dimension=0, tiled=True)[0]
    got2 = swap(send2, "rep", 4, 1)
    back = lambda grad, flip, count: self_backward(
        at, qkv, grad, self_mixed, self_ext, own, x_t, flip, count, shards, trees)
    (part3, self_back), (mine2, other2) = landed((back(self_back, 3, 1), self_back), got2, halves(keep2))
    far3, got2 = swap(part3[1][0], "rep", 4, 3), swap(other2, "rep", 4, 2)
    (part2, self_back), mine2 = landed((back(tie(self_back, part3), 2, 2), self_back), got2, lambda got: add_low(mine2, got))
    far2, far1, got2 = swap(part2[1][0], "rep", 4, 2), swap(part2[1][1], "rep", 4, 1), exchange(mine2)
    part0, mine1 = landed(back(self_back, 0, 1), (far1, far2, far3), lambda got: got)
    mine1 = add_low(part0[1][0], *mine1)
    got1, others3 = exchange(mine1), replicas(tie(shared3, mine1))
    self_grads = tie((part0[0], part2[0], part3[0]), mine1)
    tok_grad, extra = last_call(at, timesteps, tok, self_grads, resid, small, small2, small3, packed1, per_tree)
    (tok_grad, extra), (done1, done2) = landed((tok_grad, extra), (got1, got2), lambda got: (sum_over(got[0]), sum_over(got[1])))
    got_extra, others2 = exchange(extra), replicas(done2)
    ffn_grads, piece1 = landed(
        finish(at, shared3, others3, ((r, 4), (4 * r, 1), (r, 1))), got_extra,
        lambda got: jnp.concatenate([done1, sum_over(got)]))
    others1 = replicas(piece1)
    cross_grads = finish(at, done2, tie(others2, piece1), ((r, 1), (r, 1), (r, 2)))
    cross_grads, others1 = lax.optimization_barrier((cross_grads, others1))
    ffn_in_grad, ffn_out_grad, cross_out_grad = ffn_grads
    self_out_grad, cross_query_grad, cross_kv_grad = cross_grads
    self_qkv_grad, gain_grad, bias_grad, in_bias_grad, out_bias_grad, table_grad = finish(
        at, piece1, others1, ((r, 3),), r, steps)
    return (
        out.reshape(tokens.shape), tok_grad.reshape(tokens.shape), enc_grad.reshape(encoder.shape),
        table_grad, gain_grad, bias_grad, self_qkv_grad, self_out_grad, cross_query_grad, cross_kv_grad,
        cross_out_grad, ffn_in_grad, in_bias_grad.reshape(-1), ffn_out_grad, out_bias_grad.reshape(-1),
    )


def solution(mesh):
    trees = P(("rep", "shard"), None, None)
    rows, columns, flat = P("shard", None), P(None, "shard"), P("shard")
    in_specs = (trees, trees, P(("rep", "shard")), P(("rep", "shard"), None), trees, columns, columns, columns,
                rows, rows, rows, rows, rows, rows, flat, rows, flat)
    out_specs = (trees, trees, trees, columns, columns, columns, rows, rows, rows, rows, rows, rows, flat, rows, flat)
    return jax.shard_map(
        functools.partial(per_device, mesh.shape["shard"]), mesh=mesh, in_specs=in_specs, out_specs=out_specs,
        check_vma=False)
```
